256 devices in a mesh: apa: 32 (over x_hi, z, core), chan: 8 (over x_lo, y).
Axes of the slice: x: 4 (x_hi: 2, x_lo: 2; x = x_hi * 2 + x_lo), y: 4, z: 8, core: 2. Of those that a mesh axis runs over, the one named last changes fastest.
Arguments:
- frames: bfloat16 [32, 2560, 256], P('apa', 'chan'), may hold values from -6 to 6
- link_to_wire: int32 [32, 2560], P('apa'), may hold values from 0 to 2559, each once within a row
- neighbours: int32 [32, 2], P('apa'), may hold values from -1 to 31, as said below
- kernel: float32 [2, 128, 2816], P(None, 'chan'), may hold values from -6 to 6
- wide_filter: float32 [128], replicated, may hold values from 0.3 to 1
- tight_filter: float32 [128], replicated, may hold values from 0.05 to 0.5
- roi_mask: int32 [32, 160, 4], P('apa', 'chan'), may hold values 0 or 1
Outputs:
- deconvolved: float32 [32, 2560, 256], P('apa', 'chan')
The draws below stay inside these ranges and needn't reach their ends.
Inputs may be any that keep to these rules, and one draw needn't show every extreme that they name: `link_to_wire`: each row names every channel once. `neighbours`: the 32 APAs form one chain along the detector: column 0 names the APA before, column 1 the APA after, -1 at the two ends of the chain; every named APA lies on the same index of apa as the naming APA or on an adjacent one.
All inputs are finite; a program needn't handle non-finite values. No bound on the sum of `roi_mask` on one device may be relied on, other than what follows from the above.
Results may differ from the reference program's by a relative error of at most 0.0023.
Values may be sent and summed in bfloat16 or wider, within the bound.
A program may use at most 128 MiB of HBM per device.

```python
import math
import jax
import jax.numpy as jnp
from jax import lax

PU = 800
PV = 800
PW = 960
TICKS = 256
HALO_CH = 128
BC = 16
BT = 64
APA_DEV = 1
APAS = 32
CHANNELS = 2560
FREQS = 128
KCH = 2816


def draw_neighbours(key, part):
    blocks = APAS // APA_DEV
    keys = jax.random.split(key, blocks)
    inner = jax.vmap(lambda single: jax.random.permutation(single, APA_DEV))(keys)
    offsets = jnp.arange(blocks, dtype=jnp.int32) * APA_DEV
    order = (inner.astype(jnp.int32) + offsets[:, None]).reshape(-1)
    before = jnp.concatenate([jnp.full((1,), -1, jnp.int32), order[:-1]])
    after = jnp.concatenate([order[1:], jnp.full((1,), -1, jnp.int32)])
    lower = jnp.zeros((APAS,), jnp.int32).at[order].set(before)
    upper = jnp.zeros((APAS,), jnp.int32).at[order].set(after)
    return jnp.stack([lower, upper], axis=1)


def with_ends(result, rng, least, largest):
    longest = result.shape.index(max(result.shape))
    spots = []
    for shift in (0, 1):
        where = [jax.random.randint(jax.random.fold_in(rng, axis), (), 0, length) for axis, length in enumerate(result.shape)]
        where[longest] = (where[longest] + shift) % result.shape[longest]
        spots.append(tuple(where))
    return result.at[spots[0]].set(least).at[spots[1]].set(largest)


def levels(own_key, extent, cuts, least, high):
    def one(position, blocks):
        steps = jax.random.uniform(jax.random.fold_in(jax.random.fold_in(own_key, 6), position), (blocks,), jnp.float32, least / len(cuts), high / len(cuts))
        return jnp.repeat(jnp.exp(steps), extent[position] // blocks).reshape((-1,) + (1,) * (len(extent) - position - 1))

    factor_of = one(*cuts[0])
    for cut in cuts[1:]:
        factor_of = factor_of * one(*cut)
    return factor_of


def scatter_about(own_key, dims, scale, bound, shards=(), kind=jnp.bfloat16):
    entries = jax.random.normal(own_key, dims, jnp.float32) * scale
    if len(shards) > 0:
        entries = levels(own_key, dims, shards, -0.22, 0.18) * entries
    return jnp.clip(entries, min=-bound, max=bound).astype(kind)


def setup_inputs(seed: int = 0) -> dict:
    seeds = jax.random.split(jax.random.key(seed), 8)
    frames = scatter_about(seeds[0], (APAS, CHANNELS, TICKS), 1.0, 6.0, ((0, 32), (1, 8)))
    link_to_wire = jax.vmap(lambda own: jax.random.permutation(own, CHANNELS))(jax.random.split(seeds[1], APAS)).reshape((APAS, CHANNELS)).astype(jnp.int32)
    neighbours = draw_neighbours(jax.random.fold_in(seeds[7], 71), 0)
    kernel = scatter_about(seeds[3], (2, FREQS, KCH), 1.0, 6.0, ((1, 8),), jnp.float32)
    wide_filter = jnp.clip(jnp.exp(jax.random.uniform(seeds[4], (FREQS,), jnp.float32, math.log(0.3), math.log(1.0))), 0.3, 1.0)
    tight_filter = jnp.clip(jnp.exp(jax.random.uniform(seeds[5], (FREQS,), jnp.float32, math.log(0.05), math.log(0.5))), 0.05, 0.5)
    roi_mask = with_ends((jax.random.randint(seeds[6], (APAS, CHANNELS // BC, TICKS // BT), 0, 3) < 1).astype(jnp.int32), jax.random.fold_in(seeds[6], 1), 0, 1)
    return {"frames": frames, "link_to_wire": link_to_wire, "neighbours": neighbours, "kernel": kernel, "wide_filter": wide_filter, "tight_filter": tight_filter, "roi_mask": roi_mask}


two_pi = 2.0 * math.pi
highest = lax.Precision.HIGHEST


def tick_angles(ticks):
    moment = lax.iota(jnp.int32, ticks)
    harmonic = lax.iota(jnp.int32, ticks // 2)
    return ((moment[:, None] * harmonic[None, :]) % ticks).astype(jnp.float32) * (two_pi / ticks)


def forward_table(ticks):
    angles = tick_angles(ticks)
    return jnp.concatenate([jnp.cos(angles), -jnp.sin(angles)], axis=1).astype(jnp.bfloat16)


def inverse_basis(ticks, filter_gain):
    angles = tick_angles(ticks).T
    harmonic = lax.iota(jnp.int32, ticks // 2)
    weights = jnp.where(harmonic == 0, 1.0, 2.0).astype(jnp.float32) / ticks * filter_gain
    return jnp.stack([jnp.cos(angles) * weights[:, None], -jnp.sin(angles) * weights[:, None]])


def deconvolve(plane_field, response_part, keep_lo, keep_hi):
    product = jnp.fft.fft(plane_field, axis=-1) * response_part[None]
    return jnp.fft.ifft(product, axis=-1)[:, :, keep_lo:keep_hi]


def reference(frames, link_to_wire, neighbours, kernel, wide_filter, tight_filter, roi_mask):
    apa_index = jnp.arange(APAS, dtype=jnp.int32)[:, None]
    wired = jnp.zeros_like(frames).at[apa_index, link_to_wire].set(frames)
    spectra = jnp.dot(wired.reshape(-1, TICKS), forward_table(TICKS), preferred_element_type=jnp.float32)
    spectra = spectra.reshape(APAS, CHANNELS, 2, FREQS)
    field = jnp.transpose(spectra[:, :, 0] + 1j * spectra[:, :, 1], (0, 2, 1))
    plane_start = PU + PV
    lower_id = neighbours[:, 0]
    upper_id = neighbours[:, 1]
    lower_band = field[:, :, CHANNELS - HALO_CH:]
    upper_band = field[:, :, plane_start:plane_start + HALO_CH]
    lower_rim = lower_band[jnp.maximum(lower_id, 0)] * (lower_id >= 0)[:, None, None]
    upper_rim = upper_band[jnp.maximum(upper_id, 0)] * (upper_id >= 0)[:, None, None]
    extended = jnp.concatenate([lower_rim, field[:, :, plane_start:], upper_rim], axis=2)
    response = kernel[0] + 1j * kernel[1]
    parts = jnp.concatenate([
        deconvolve(field[:, :, :PU], response[:, :PU], 0, PU),
        deconvolve(field[:, :, PU:plane_start], response[:, PU:plane_start], 0, PV),
        deconvolve(extended, response[:, plane_start:], HALO_CH, HALO_CH + PW)], axis=2)
    stacked = jnp.stack([jnp.real(parts).astype(jnp.float32), jnp.imag(parts).astype(jnp.float32)], axis=1)

    def signal(filter_gain):
        return jnp.einsum("azkc,zkt->act", stacked, inverse_basis(TICKS, filter_gain), precision=highest)

    expanded = jnp.repeat(jnp.repeat(roi_mask, BC, axis=1), BT, axis=2)
    return jnp.where(expanded == 1, signal(wide_filter), signal(tight_filter))
```

```python
import math

import jax
import jax.numpy as jnp
import numpy as np
from jax import lax
from jax.experimental import pallas as pl
from jax.experimental.pallas import tpu as pltpu
from jax.sharding import PartitionSpec as P

PU = 800
PV = 800
PW = 960
HALO = 128
BC = 16
BT = 64
CHANNELS = 2560
TICKS = 256
FREQS = 128

CHAN = 8
SHARE = CHANNELS // CHAN
PAD = 384
KB = FREQS // CHAN
ROWS = 2 * KB
RADIX = 8
NU = PU // RADIX
PE = PW + 2 * HALO
NW = PE // RADIX
LINKS = CHAN * PAD
OUTS = SHARE // RADIX

MESH = pl.DeviceIdType.MESH
NT = (((1,), (1,)), ((), ()))
f32 = jnp.float32
bf16 = jnp.bfloat16


def halves(table):
    high = table.astype(bf16)
    low = (table - high.astype(np.float64)).astype(bf16)
    return high, low


def tick_rows():
    row = np.arange(2 * FREQS)
    k = row // ROWS * KB + row % KB
    return k, row % ROWS // KB


def forward_ticks():
    k, z = tick_rows()
    angle = 2.0 * math.pi / TICKS * (k[:, None] * np.arange(TICKS)[None, :] % TICKS)
    return np.where(z[:, None] == 0, np.cos(angle), -np.sin(angle)).astype(bf16)


def inverse_ticks():
    k, z = tick_rows()
    angle = 2.0 * math.pi / TICKS * (k[:, None] * np.arange(TICKS)[None, :] % TICKS)
    weight = np.where(k == 0, 1.0, 2.0)[:, None] / TICKS
    return np.stack(halves(np.where(z[:, None] == 0, np.cos(angle), -np.sin(angle)) * weight))


def spread_filters():
    k, _ = tick_rows()
    return (np.arange(FREQS)[:, None] == k[None, :]).astype(np.float32)


def dense(length, width, scale=1.0):
    index = np.arange(length)
    angle = 2.0 * math.pi / length * (index[:, None] * index[None, :] % length)
    table = np.zeros((width, 2 * width))
    table[:length, :length] = np.cos(angle) * scale
    table[:length, width : width + length] = np.sin(angle) * scale
    return table


def forward_dense(length, width):
    high, low = halves(dense(length, width))
    return np.concatenate([high, high, low], axis=0)


def inverse_dense(length, width, period, first, count, lead, rows):
    table = np.zeros((rows, 2 * width))
    table[lead : lead + count] = dense(length, width, 1.0 / period)[first : first + count]
    return np.stack(halves(table))


def twiddles(length, width, period):
    angle = 2.0 * math.pi / period * (np.arange(RADIX)[:, None] * np.arange(length)[None, :])
    table = np.zeros((2, RADIX, 1, width), np.float32)
    table[0, :, 0, :length] = np.cos(angle)
    table[1, :, 0, :length] = np.sin(angle)
    return table


def rim_places():
    lane = np.arange(2 * HALO)
    place = np.where(lane < HALO, lane // RADIX, (HALO + PW) // RADIX + (lane - HALO) // RADIX)
    return (np.arange(256)[:, None] == place[None, :]).astype(np.float32).astype(bf16)


def mask_rows():
    return (np.arange(OUTS)[:, None] // (BC // RADIX) == np.arange(SHARE // BC)[None, :]).astype(np.float32)


def mask_columns():
    return (np.arange(TICKS // BT)[:, None] == np.arange(TICKS)[None, :] // BT).astype(np.float32)


def split(value):
    high = value.astype(bf16)
    return high, (value - high.astype(f32)).astype(bf16)


def mul(left, right):
    return jnp.dot(left, right, preferred_element_type=f32)


def mul_nt(left, right):
    return lax.dot_general(left, right, NT, preferred_element_type=f32)


def four(values, sign):
    (ar, ai), (br, bi), (cr, ci), (dr, di) = values
    s0r, s0i, s1r, s1i = ar + cr, ai + ci, ar - cr, ai - ci
    s2r, s2i, s3r, s3i = br + dr, bi + di, br - dr, bi - di
    if sign > 0:
        tr, ti = -s3i, s3r
    else:
        tr, ti = s3i, -s3r
    return [(s0r + s2r, s0i + s2i), (s1r + tr, s1i + ti), (s0r - s2r, s0i - s2i), (s1r - tr, s1i - ti)]


def eight(values, sign):
    even = four(values[0::2], sign)
    odd = four(values[1::2], sign)
    root = math.sqrt(0.5)
    r, i = odd[1]
    odd[1] = ((r - sign * i) * root, (i + sign * r) * root)
    r, i = odd[2]
    odd[2] = (-i, r) if sign > 0 else (i, -r)
    r, i = odd[3]
    odd[3] = ((-r - sign * i) * root, (sign * r - i) * root)
    first = [(a + c, b + d) for (a, b), (c, d) in zip(even, odd)]
    second = [(a - c, b - d) for (a, b), (c, d) in zip(even, odd)]
    return first + second


def channel_product(product, kern, twiddle, width):
    values = []
    for c in range(RADIX):
        re = product[c * ROWS : c * ROWS + KB]
        im = product[c * ROWS + KB : (c + 1) * ROWS]
        yr = re[:, :width] + im[:, width:]
        yi = im[:, :width] - re[:, width:]
        if c > 0:
            tc, ts = twiddle[0, c], twiddle[1, c]
            yr, yi = yr * tc + yi * ts, yi * tc - yr * ts
        values.append((yr, yi))
    values = eight(values, -1)
    values = [
        (r * kern[m, 0] - i * kern[m, 1], r * kern[m, 1] + i * kern[m, 0]) for m, (r, i) in enumerate(values)
    ]
    values = eight(values, 1)
    rows = []
    for c, (r, i) in enumerate(values):
        if c > 0:
            tc, ts = twiddle[0, c], twiddle[1, c]
            r, i = r * tc - i * ts, i * tc + r * ts
        rows.append(jnp.concatenate([r, -i], axis=1))
        rows.append(jnp.concatenate([i, r], axis=1))
    return jnp.concatenate(rows, axis=0)


def inverse_product(table, value):
    high, low = split(value)
    return mul_nt(table[0], high) + mul_nt(table[1], high) + mul_nt(table[0], low)


def kernel_window(kern, part, start, length, width):
    base = start // 128 * 128
    span = -(-(start - base + length) // 128) * 128
    span = max(span, width)
    piece = kern[part, :, base : base + span]
    if start > base:
        piece = pltpu.roll(piece, span - (start - base), axis=1)
    return piece[:, :width]


INPUTS = 17


def body_kernel(apas, near, *refs):
    hbm = refs[:INPUTS]
    out = refs[INPUTS]
    local = refs[INPUTS + 1 : 2 * INPUTS + 1]
    (tx1, rx1, tx2, rx2, txh, rxh, onehot, edge, masks, big, small, kern_u, kern_v, kern_w, result) = refs[
        2 * INPUTS + 1 : 2 * INPUTS + 16
    ]
    in_sem, send1, recv1, send2, recv2, sendh, recvh, out_sem = refs[2 * INPUTS + 16 :]
    (frames, ticks, links, kern, wide, tight, roi, fwd_u, fwd_w, inv_u, inv_v, inv_w, tw_u, tw_w, rim, back, expand) = local

    me = lax.axis_index("chan")
    apa = lax.axis_index("apa")
    after = lax.rem(apa + 1, apas)
    before = lax.rem(apa + apas - 1, apas)

    loads = [pltpu.make_async_copy(hbm[i], local[i], in_sem.at[i]) for i in range(INPUTS)]
    for load in loads:
        load.start()

    barrier = pltpu.get_barrier_semaphore()
    for step in range(1, CHAN):
        pl.semaphore_signal(barrier, inc=1, device_id={"chan": lax.rem(me + step, CHAN)}, device_id_type=MESH)
    pl.semaphore_signal(barrier, inc=1, device_id={"apa": after}, device_id_type=MESH)
    pl.semaphore_signal(barrier, inc=1, device_id={"apa": before}, device_id_type=MESH)

    loads[0].wait()
    loads[1].wait()
    padded = jnp.concatenate([frames[0], jnp.zeros((PAD - SHARE, TICKS), bf16)], axis=0)
    tx1[...] = mul_nt(ticks[...], padded).reshape(CHAN, ROWS, PAD)

    pl.semaphore_wait(barrier, CHAN + 1)

    def first_copy(step):
        dest = lax.rem(me + step, CHAN)
        return pltpu.make_async_remote_copy(
            src_ref=tx1.at[dest],
            dst_ref=rx1.at[me],
            send_sem=send1.at[dest],
            recv_sem=recv1.at[me],
            device_id={"chan": dest},
            device_id_type=MESH,
        )

    for step in range(1, CHAN):
        first_copy(step).start()
    rx1[me] = tx1[me]

    loads[2].wait()
    for s in range(CHAN):
        wire = links[:, s * SHARE : (s + 1) * SHARE]
        wire = jnp.concatenate([wire, jnp.full((1, PAD - SHARE), -8, jnp.int32)], axis=1)
        group = lax.shift_right_arithmetic(wire, 3)
        rest = lax.bitwise_and(wire, 7)
        place = group + jnp.where(wire >= PU + PV, 72, jnp.where(wire >= PU, 28, 0))
        row = lax.broadcasted_iota(jnp.int32, (512, PAD), 0)
        onehot[:, s * PAD : (s + 1) * PAD] = jnp.where(row == place, 1.0, 0.0).astype(bf16)
        row = lax.broadcasted_iota(jnp.int32, (256, PAD), 0)
        spot = row + jnp.where(row >= HALO, CHANNELS - 2 * HALO, PU + PV)
        edge[:, s * PAD : (s + 1) * PAD] = jnp.where(spot == wire, 1.0, 0.0).astype(bf16)
        for h in range(RADIX):
            here = jnp.where((rest == h) & (wire >= 0), 1.0, 0.0)
            masks[s, h] = jnp.broadcast_to(here, (16, PAD)).astype(bf16)

    loads[3].wait()
    for m in range(RADIX):
        for part in range(2):
            kern_u[m, part] = kernel_window(kern, part, NU * m, NU, 128)
            kern_v[m, part] = kernel_window(kern, part, PU + NU * m, NU, 128)
            kern_w[m, part] = kernel_window(kern, part, PU + PV + NW * m, NW, 256)

    for load in loads[4:]:
        load.wait()
    gains = jnp.concatenate([wide[...], tight[...], jnp.zeros((6, FREQS), f32)], axis=0)
    gains = jnp.dot(gains, expand[0:FREQS], precision=lax.Precision.HIGHEST, preferred_element_type=f32)
    inside = roi[0].astype(f32)
    row_index = lax.broadcasted_iota(jnp.int32, (OUTS, SHARE // BC), 0) // (BC // RADIX)
    col_index = lax.broadcasted_iota(jnp.int32, (OUTS, SHARE // BC), 1)
    pick = jnp.where(row_index == col_index, 1.0, 0.0)
    inside = mul(pick, inside)
    row_index = lax.broadcasted_iota(jnp.int32, (TICKS // BT, TICKS), 0)
    col_index = lax.broadcasted_iota(jnp.int32, (TICKS // BT, TICKS), 1) // BT
    inside = mul(inside, jnp.where(row_index == col_index, 1.0, 0.0))

    for step in range(1, CHAN):
        source = lax.rem(me + step, CHAN)
        pltpu.make_async_remote_copy(
            src_ref=tx1.at[source],
            dst_ref=rx1.at[source],
            send_sem=send1.at[source],
            recv_sem=recv1.at[source],
            device_id={"chan": source},
            device_id_type=MESH,
        ).wait_recv()
    for s in range(CHAN):
        lanes = slice(s * PAD, (s + 1) * PAD)
        high, low = split(rx1[s])
        small[0:ROWS, lanes] = high
        small[ROWS : 2 * ROWS, lanes] = low
        for h in range(RADIX):
            mask = jnp.concatenate([masks[s, h], masks[s, h]], axis=0)
            big[h * ROWS : (h + 1) * ROWS, lanes] = high * mask
            big[256 + h * ROWS : 256 + (h + 1) * ROWS, lanes] = low * mask

    bands = mul_nt(small[...], edge[...])
    first_band = bands[:, :HALO]
    last_band = bands[:, HALO:]
    lower = near[0, 0]
    upper = near[0, 1]
    none = jnp.zeros_like(first_band)
    to_after = jnp.where(upper == after, last_band, jnp.where(lower == after, first_band, none))
    to_before = jnp.where(lower == before, first_band, jnp.where(upper == before, last_band, none))
    txh[0] = to_after.astype(bf16)
    txh[1] = to_before.astype(bf16)

    def edge_copy(way):
        return pltpu.make_async_remote_copy(
            src_ref=txh.at[way],
            dst_ref=rxh.at[way],
            send_sem=sendh.at[way],
            recv_sem=recvh.at[way],
            device_id={"apa": after if way == 0 else before},
            device_id_type=MESH,
        )

    edge_copy(0).start()
    edge_copy(1).start()

    placed = mul_nt(big[...], onehot[...])

    def second_copy(dest):
        return pltpu.make_async_remote_copy(
            src_ref=tx2.at[dest],
            dst_ref=rx2.at[me],
            send_sem=send2.at[dest],
            recv_sem=recv2.at[me],
            device_id={"chan": dest},
            device_id_type=MESH,
        )

    def send_on(dests):
        for dest in dests:

            @pl.when(me != dest)
            def _():
                second_copy(dest).start()

            @pl.when(me == dest)
            def _():
                rx2[dest] = tx2[dest]

    def plane(lanes, fwd, kern_part, twiddle, table, width):
        high = placed[0:256, lanes].astype(bf16)
        low = placed[256:512, lanes].astype(bf16)
        product = mul(jnp.concatenate([high, low, high], axis=1), fwd[...])
        return inverse_product(table, channel_product(product, kern_part, twiddle, width))

    part_u = plane(slice(0, 128), fwd_u, kern_u, tw_u, inv_u, 128)
    part_v = plane(slice(128, 256), fwd_u, kern_v, tw_u, inv_v, 128)
    tx2[0] = part_u[0:40]
    tx2[1] = part_u[40:80]
    tx2[2, 0:16] = part_u[80:96]
    tx2[2, 16:24] = part_u[96:104] + part_v[0:8]
    tx2[2, 24:40] = part_v[8:24]
    tx2[3] = part_v[24:64]
    tx2[4] = part_v[64:104]
    send_on(range(0, 5))

    edge_copy(0).wait_recv()
    edge_copy(1).wait_recv()
    from_before = rxh[0].astype(f32)
    from_after = rxh[1].astype(f32)
    blank = jnp.zeros_like(from_before)
    rim_low = jnp.where(lower == before, from_before, jnp.where(lower == after, from_after, blank))
    rim_up = jnp.where(upper == after, from_after, jnp.where(upper == before, from_before, blank))
    rims = jnp.concatenate([rim_low, rim_up], axis=1)
    lane = lax.bitwise_and(lax.broadcasted_iota(jnp.int32, (ROWS, 2 * HALO), 1), RADIX - 1)
    spread = [
        jnp.where(lane == h, rims[part * ROWS : (part + 1) * ROWS], 0.0) for part in range(2) for h in range(RADIX)
    ]
    rim_part = mul_nt(jnp.concatenate(spread, axis=0).astype(bf16), rim[...])
    full = placed[:, 256:512] + rim_part
    high = full[0:256].astype(bf16)
    low = full[256:512].astype(bf16)
    product = mul(jnp.concatenate([high, low, high], axis=1), fwd_w[...])
    part_w = inverse_product(inv_w, channel_product(product, kern_w, tw_w, 256))
    tx2[5] = part_w[0:40]
    tx2[6] = part_w[40:80]
    tx2[7] = part_w[80:120]
    send_on(range(5, 8))

    for step in range(1, CHAN):
        source = lax.rem(me + step, CHAN)
        pltpu.make_async_remote_copy(
            src_ref=tx2.at[source],
            dst_ref=rx2.at[source],
            send_sem=send2.at[source],
            recv_sem=recv2.at[source],
            device_id={"chan": source},
            device_id_type=MESH,
        ).wait_recv()

    block = lax.broadcasted_iota(jnp.int32, (OUTS, 128), 1) // ROWS
    columns = []
    for side in range(2):
        for c in range(RADIX):
            acc = None
            for q in range(4):
                piece = rx2[4 * side + q, :, c // 4 * 128 : (c // 4 + 1) * 128]
                turn = (q - c % 4) % 4 * ROWS
                if turn:
                    piece = pltpu.roll(piece, turn, axis=1)
                acc = piece if acc is None else jnp.where(block == q, piece, acc)
            columns.append(acc)
    gathered = jnp.concatenate(
        [jnp.concatenate(columns[:RADIX], axis=0), jnp.concatenate(columns[RADIX:], axis=0)], axis=1
    )

    def signal(gain):
        high, low = split(gathered * gain)
        return mul(high, back[0]) + mul(low, back[0]) + mul(high, back[1])

    wide_signal = signal(gains[0:1])
    tight_signal = signal(gains[1:2])
    for c in range(RADIX):
        rows = slice(c * OUTS, (c + 1) * OUTS)
        chosen = jnp.where(inside > 0.5, wide_signal[rows], tight_signal[rows])
        for side in range(2):
            result[side, pl.ds(c, OUTS, stride=RADIX), :] = chosen[:, side * 128 : (side + 1) * 128]
    stores = [
        pltpu.make_async_copy(result.at[side], out.at[0, :, pl.ds(side * 128, 128)], out_sem.at[side])
        for side in range(2)
    ]
    for store in stores:
        store.start()
    for store in stores:
        store.wait()

    for step in range(1, CHAN):
        first_copy(step).wait_send()
        second_copy(lax.rem(me + step, CHAN)).wait_send()
    edge_copy(0).wait_send()
    edge_copy(1).wait_send()


def body(frames, links, near, kern, wide, tight, roi):
    apas = lax.axis_size("apa")
    arrays = [
        frames,
        jnp.asarray(forward_ticks()),
        links,
        kern,
        wide.reshape(1, FREQS),
        tight.reshape(1, FREQS),
        roi,
        jnp.asarray(forward_dense(NU, 128)),
        jnp.asarray(forward_dense(NW, 256)),
        jnp.asarray(inverse_dense(NU, 128, PU, 0, NU, 0, 104)),
        jnp.asarray(inverse_dense(NU, 128, PV, 0, NU, 4, 104)),
        jnp.asarray(inverse_dense(NW, 256, PE, HALO // RADIX, PW // RADIX, 0, 120)),
        jnp.asarray(twiddles(NU, 128, PU)),
        jnp.asarray(twiddles(NW, 256, PE)),
        jnp.asarray(rim_places()),
        jnp.asarray(inverse_ticks()),
        jnp.asarray(spread_filters()),
    ]
    scratch = [pltpu.VMEM(a.shape, a.dtype) for a in arrays]
    scratch += [
        pltpu.VMEM((CHAN, ROWS, PAD), f32),
        pltpu.VMEM((CHAN, ROWS, PAD), f32),
        pltpu.VMEM((CHAN, OUTS, 256), f32),
        pltpu.VMEM((CHAN, OUTS, 256), f32),
        pltpu.VMEM((2, 2 * ROWS, HALO), bf16),
        pltpu.VMEM((2, 2 * ROWS, HALO), bf16),
        pltpu.VMEM((512, LINKS), bf16),
        pltpu.VMEM((256, LINKS), bf16),
        pltpu.VMEM((CHAN, RADIX, 16, PAD), bf16),
        pltpu.VMEM((512, LINKS), bf16),
        pltpu.VMEM((2 * ROWS, LINKS), bf16),
        pltpu.VMEM((RADIX, 2, KB, 128), f32),
        pltpu.VMEM((RADIX, 2, KB, 128), f32),
        pltpu.VMEM((RADIX, 2, KB, 256), f32),
        pltpu.VMEM((2, SHARE, 128), f32),
        pltpu.SemaphoreType.DMA((INPUTS,)),
        pltpu.SemaphoreType.DMA((CHAN,)),
        pltpu.SemaphoreType.DMA((CHAN,)),
        pltpu.SemaphoreType.DMA((CHAN,)),
        pltpu.SemaphoreType.DMA((CHAN,)),
        pltpu.SemaphoreType.DMA((2,)),
        pltpu.SemaphoreType.DMA((2,)),
        pltpu.SemaphoreType.DMA((2,)),
    ]

    def kernel(near_ref, *refs):
        body_kernel(apas, near_ref, *refs)

    return pl.pallas_call(
        kernel,
        out_shape=jax.ShapeDtypeStruct(frames.shape, f32),
        in_specs=[pl.BlockSpec(memory_space=pltpu.SMEM)] + [pl.BlockSpec(memory_space=pl.ANY)] * len(arrays),
        out_specs=pl.BlockSpec(memory_space=pl.ANY),
        scratch_shapes=scratch,
        compiler_params=pltpu.CompilerParams(
            collective_id=0, has_side_effects=True, vmem_limit_bytes=48 * 1024 * 1024
        ),
    )(near, *arrays)


def solution(mesh):
    placed = (
        P("apa", "chan", None),
        P("apa", None),
        P("apa", None),
        P(None, "chan", None),
        P(),
        P(),
        P("apa", "chan", None),
    )
    return jax.shard_map(body, mesh=mesh, in_specs=placed, out_specs=P("apa", "chan", None), check_vma=False)
```

```python
import math

import jax
import jax.numpy as jnp
import numpy as np
from jax import lax
from jax.experimental import pallas as pl
from jax.experimental.pallas import tpu as pltpu
from jax.sharding import PartitionSpec as P

PU = 800
PV = 800
PW = 960
HALO = 128
BC = 16
BT = 64
CHANNELS = 2560
TICKS = 256
FREQS = 128

CHAN = 8
SHARE = CHANNELS // CHAN
PAD = 384
KB = FREQS // CHAN
ROWS = 2 * KB
RADIX = 8
NU = PU // RADIX
PE = PW + 2 * HALO
NW = PE // RADIX
LINKS = CHAN * PAD
OUTS = SHARE // RADIX

MESH = pl.DeviceIdType.MESH
NT = (((1,), (1,)), ((), ()))
f32 = jnp.float32
bf16 = jnp.bfloat16


def halves(table):
    high = table.astype(bf16)
    low = (table - high.astype(np.float64)).astype(bf16)
    return high, low


def tick_rows():
    row = np.arange(2 * FREQS)
    k = row // ROWS * KB + row % KB
    return k, row % ROWS // KB


def forward_ticks():
    k, z = tick_rows()
    angle = 2.0 * math.pi / TICKS * (k[:, None] * np.arange(TICKS)[None, :] % TICKS)
    return np.where(z[:, None] == 0, np.cos(angle), -np.sin(angle)).astype(bf16)


def inverse_ticks():
    k, z = tick_rows()
    angle = 2.0 * math.pi / TICKS * (k[:, None] * np.arange(TICKS)[None, :] % TICKS)
    weight = np.where(k == 0, 1.0, 2.0)[:, None] / TICKS
    return np.stack(halves(np.where(z[:, None] == 0, np.cos(angle), -np.sin(angle)) * weight))


def spread_filters():
    k, _ = tick_rows()
    return (np.arange(FREQS)[:, None] == k[None, :]).astype(np.float32)


def dense(length, width, scale=1.0):
    index = np.arange(length)
    angle = 2.0 * math.pi / length * (index[:, None] * index[None, :] % length)
    table = np.zeros((width, 2 * width))
    table[:length, :length] = np.cos(angle) * scale
    table[:length, width : width + length] = np.sin(angle) * scale
    return table


def forward_dense(length, width):
    high, low = halves(dense(length, width))
    return np.concatenate([high, high, low], axis=0)


def inverse_dense(length, width, period, first, count, lead, rows):
    table = np.zeros((rows, 2 * width))
    table[lead : lead + count] = dense(length, width, 1.0 / period)[first : first + count]
    return np.stack(halves(table))


def twiddles(length, width, period):
    angle = 2.0 * math.pi / period * (np.arange(RADIX)[:, None] * np.arange(length)[None, :])
    table = np.zeros((2, RADIX, 1, width), np.float32)
    table[0, :, 0, :length] = np.cos(angle)
    table[1, :, 0, :length] = np.sin(angle)
    return table


def rim_places():
    lane = np.arange(2 * HALO)
    place = np.where(lane < HALO, lane // RADIX, (HALO + PW) // RADIX + (lane - HALO) // RADIX)
    return (np.arange(256)[:, None] == place[None, :]).astype(np.float32).astype(bf16)


def mask_rows():
    return (np.arange(OUTS)[:, None] // (BC // RADIX) == np.arange(SHARE // BC)[None, :]).astype(np.float32)


def mask_columns():
    return (np.arange(TICKS // BT)[:, None] == np.arange(TICKS)[None, :] // BT).astype(np.float32)


def split(value):
    high = value.astype(bf16)
    return high, (value - high.astype(f32)).astype(bf16)


def mul(left, right):
    return jnp.dot(left, right, preferred_element_type=f32)


def mul_nt(left, right):
    return lax.dot_general(left, right, NT, preferred_element_type=f32)


def four(values, sign):
    (ar, ai), (br, bi), (cr, ci), (dr, di) = values
    s0r, s0i, s1r, s1i = ar + cr, ai + ci, ar - cr, ai - ci
    s2r, s2i, s3r, s3i = br + dr, bi + di, br - dr, bi - di
    if sign > 0:
        tr, ti = -s3i, s3r
    else:
        tr, ti = s3i, -s3r
    return [(s0r + s2r, s0i + s2i), (s1r + tr, s1i + ti), (s0r - s2r, s0i - s2i), (s1r - tr, s1i - ti)]


def eight(values, sign):
    even = four(values[0::2], sign)
    odd = four(values[1::2], sign)
    root = math.sqrt(0.5)
    r, i = odd[1]
    odd[1] = ((r - sign * i) * root, (i + sign * r) * root)
    r, i = odd[2]
    odd[2] = (-i, r) if sign > 0 else (i, -r)
    r, i = odd[3]
    odd[3] = ((-r - sign * i) * root, (sign * r - i) * root)
    first = [(a + c, b + d) for (a, b), (c, d) in zip(even, odd)]
    second = [(a - c, b - d) for (a, b), (c, d) in zip(even, odd)]
    return first + second


def channel_product(product, kern, twiddle, width):
    values = []
    for c in range(RADIX):
        re = product[c * ROWS : c * ROWS + KB]
        im = product[c * ROWS + KB : (c + 1) * ROWS]
        yr = re[:, :width] + im[:, width:]
        yi = im[:, :width] - re[:, width:]
        if c > 0:
            tc, ts = twiddle[0, c], twiddle[1, c]
            yr, yi = yr * tc + yi * ts, yi * tc - yr * ts
        values.append((yr, yi))
    values = eight(values, -1)
    values = [
        (r * kern[m, 0] - i * kern[m, 1], r * kern[m, 1] + i * kern[m, 0]) for m, (r, i) in enumerate(values)
    ]
    values = eight(values, 1)
    rows = []
    for c, (r, i) in enumerate(values):
        if c > 0:
            tc, ts = twiddle[0, c], twiddle[1, c]
            r, i = r * tc - i * ts, i * tc + r * ts
        rows.append(jnp.concatenate([r, -i], axis=1))
        rows.append(jnp.concatenate([i, r], axis=1))
    return jnp.concatenate(rows, axis=0)


def inverse_product(table, value):
    high, low = split(value)
    return mul_nt(table[0], high) + mul_nt(table[1], high) + mul_nt(table[0], low)


def kernel_window(kern, part, start, length, width):
    base = start // 128 * 128
    span = -(-(start - base + length) // 128) * 128
    span = max(span, width)
    piece = kern[part, :, base : base + span]
    if start > base:
        piece = pltpu.roll(piece, span - (start - base), axis=1)
    return piece[:, :width]


INPUTS = 17


def body_kernel(apas, near, *refs):
    hbm = refs[:INPUTS]
    out = refs[INPUTS]
    local = refs[INPUTS + 1 : 2 * INPUTS + 1]
    (tx1, rx1, tx2, rx2, txh, rxh, onehot, edge, masks, big, small, kern_u, kern_v, kern_w, result) = refs[
        2 * INPUTS + 1 : 2 * INPUTS + 16
    ]
    in_sem, send1, recv1, send2, recv2, sendh, recvh, out_sem = refs[2 * INPUTS + 16 :]
    (frames, ticks, links, kern, wide, tight, roi, fwd_u, fwd_w, inv_u, inv_v, inv_w, tw_u, tw_w, rim, back, expand) = local

    me = lax.axis_index("chan")
    apa = lax.axis_index("apa")
    after = lax.rem(apa + 1, apas)
    before = lax.rem(apa + apas - 1, apas)

    loads = [pltpu.make_async_copy(hbm[i], local[i], in_sem.at[i]) for i in range(INPUTS)]
    for load in loads:
        load.start()

    barrier = pltpu.get_barrier_semaphore()
    for step in range(1, CHAN):
        pl.semaphore_signal(barrier, inc=1, device_id={"chan": lax.rem(me + step, CHAN)}, device_id_type=MESH)
    pl.semaphore_signal(barrier, inc=1, device_id={"apa": after}, device_id_type=MESH)
    pl.semaphore_signal(barrier, inc=1, device_id={"apa": before}, device_id_type=MESH)

    loads[0].wait()
    loads[1].wait()
    padded = jnp.concatenate([frames[0], jnp.zeros((PAD - SHARE, TICKS), bf16)], axis=0)
    tx1[...] = mul_nt(ticks[...], padded).reshape(CHAN, ROWS, PAD)

    pl.semaphore_wait(barrier, CHAN + 1)

    def first_copy(step):
        dest = lax.rem(me + step, CHAN)
        return pltpu.make_async_remote_copy(
            src_ref=tx1.at[dest],
            dst_ref=rx1.at[me],
            send_sem=send1.at[dest],
            recv_sem=recv1.at[me],
            device_id={"chan": dest},
            device_id_type=MESH,
        )

    for step in range(1, CHAN):
        first_copy(step).start()
    rx1[me] = tx1[me]

    loads[2].wait()
    for s in range(CHAN):
        wire = links[:, s * SHARE : (s + 1) * SHARE]
        wire = jnp.concatenate([wire, jnp.full((1, PAD - SHARE), -8, jnp.int32)], axis=1)
        group = lax.shift_right_arithmetic(wire, 3)
        rest = lax.bitwise_and(wire, 7)
        place = group + jnp.where(wire >= PU + PV, 72, jnp.where(wire >= PU, 28, 0))
        row = lax.broadcasted_iota(jnp.int32, (512, PAD), 0)
        onehot[:, s * PAD : (s + 1) * PAD] = jnp.where(row == place, 1.0, 0.0).astype(bf16)
        row = lax.broadcasted_iota(jnp.int32, (256, PAD), 0)
        spot = row + jnp.where(row >= HALO, CHANNELS - 2 * HALO, PU + PV)
        edge[:, s * PAD : (s + 1) * PAD] = jnp.where(spot == wire, 1.0, 0.0).astype(bf16)
        for h in range(RADIX):
            here = jnp.where((rest == h) & (wire >= 0), 1.0, 0.0)
            masks[s, h] = jnp.broadcast_to(here, (16, PAD)).astype(bf16)

    loads[3].wait()
    for m in range(RADIX):
        for part in range(2):
            kern_u[m, part] = kernel_window(kern, part, NU * m, NU, 128)
            kern_v[m, part] = kernel_window(kern, part, PU + NU * m, NU, 128)
            kern_w[m, part] = kernel_window(kern, part, PU + PV + NW * m, NW, 256)

    for load in loads[4:]:
        load.wait()
    gains = jnp.concatenate([wide[...], tight[...], jnp.zeros((6, FREQS), f32)], axis=0)
    gains = jnp.dot(gains, expand[0:FREQS], precision=lax.Precision.HIGHEST, preferred_element_type=f32)
    inside = roi[0].astype(f32)
    row_index = lax.broadcasted_iota(jnp.int32, (OUTS, SHARE // BC), 0) // (BC // RADIX)
    col_index = lax.broadcasted_iota(jnp.int32, (OUTS, SHARE // BC), 1)
    pick = jnp.where(row_index == col_index, 1.0, 0.0)
    inside = mul_nt(pick, inside)
    row_index = lax.broadcasted_iota(jnp.int32, (TICKS // BT, TICKS), 0)
    col_index = lax.broadcasted_iota(jnp.int32, (TICKS // BT, TICKS), 1) // BT
    inside = mul(inside, jnp.where(row_index == col_index, 1.0, 0.0))

    for step in range(1, CHAN):
        source = lax.rem(me + step, CHAN)
        pltpu.make_async_remote_copy(
            src_ref=tx1.at[source],
            dst_ref=rx1.at[source],
            send_sem=send1.at[source],
            recv_sem=recv1.at[source],
            device_id={"chan": source},
            device_id_type=MESH,
        ).wait_recv()
    for s in range(CHAN):
        lanes = slice(s * PAD, (s + 1) * PAD)
        high, low = split(rx1[s])
        small[0:ROWS, lanes] = high
        small[ROWS : 2 * ROWS, lanes] = low
        for h in range(RADIX):
            mask = jnp.concatenate([masks[s, h], masks[s, h]], axis=0)
            big[h * ROWS : (h + 1) * ROWS, lanes] = high * mask
            big[256 + h * ROWS : 256 + (h + 1) * ROWS, lanes] = low * mask

    bands = mul_nt(small[...], edge[...])
    first_band = bands[:, :HALO]
    last_band = bands[:, HALO:]
    lower = near[0, 0]
    upper = near[0, 1]
    none = jnp.zeros_like(first_band)
    to_after = jnp.where(upper == after, last_band, jnp.where(lower == after, first_band, none))
    to_before = jnp.where(lower == before, first_band, jnp.where(upper == before, last_band, none))
    txh[0] = to_after.astype(bf16)
    txh[1] = to_before.astype(bf16)

    def edge_copy(way):
        return pltpu.make_async_remote_copy(
            src_ref=txh.at[way],
            dst_ref=rxh.at[way],
            send_sem=sendh.at[way],
            recv_sem=recvh.at[way],
            device_id={"apa": after if way == 0 else before},
            device_id_type=MESH,
        )

    edge_copy(0).start()
    edge_copy(1).start()

    placed = mul_nt(big[...], onehot[...])

    def second_copy(dest):
        return pltpu.make_async_remote_copy(
            src_ref=tx2.at[dest],
            dst_ref=rx2.at[me],
            send_sem=send2.at[dest],
            recv_sem=recv2.at[me],
            device_id={"chan": dest},
            device_id_type=MESH,
        )

    def send_on(dests):
        for dest in dests:

            @pl.when(me != dest)
            def _():
                second_copy(dest).start()

            @pl.when(me == dest)
            def _():
                rx2[dest] = tx2[dest]

    def plane(lanes, fwd, kern_part, twiddle, table, width):
        high = placed[0:256, lanes].astype(bf16)
        low = placed[256:512, lanes].astype(bf16)
        product = mul(jnp.concatenate([high, low, high], axis=1), fwd[...])
        return inverse_product(table, channel_product(product, kern_part, twiddle, width))

    part_u = plane(slice(0, 128), fwd_u, kern_u, tw_u, inv_u, 128)
    part_v = plane(slice(128, 256), fwd_u, kern_v, tw_u, inv_v, 128)
    tx2[0] = part_u[0:40]
    tx2[1] = part_u[40:80]
    tx2[2, 0:16] = part_u[80:96]
    tx2[2, 16:24] = part_u[96:104] + part_v[0:8]
    tx2[2, 24:40] = part_v[8:24]
    tx2[3] = part_v[24:64]
    tx2[4] = part_v[64:104]
    send_on(range(0, 5))

    edge_copy(0).wait_recv()
    edge_copy(1).wait_recv()
    from_before = rxh[0].astype(f32)
    from_after = rxh[1].astype(f32)
    blank = jnp.zeros_like(from_before)
    rim_low = jnp.where(lower == before, from_before, jnp.where(lower == after, from_after, blank))
    rim_up = jnp.where(upper == after, from_after, jnp.where(upper == before, from_before, blank))
    rims = jnp.concatenate([rim_low, rim_up], axis=1)
    lane = lax.bitwise_and(lax.broadcasted_iota(jnp.int32, (ROWS, 2 * HALO), 1), RADIX - 1)
    spread = [
        jnp.where(lane == h, rims[part * ROWS : (part + 1) * ROWS], 0.0) for part in range(2) for h in range(RADIX)
    ]
    rim_part = mul_nt(jnp.concatenate(spread, axis=0).astype(bf16), rim[...])
    full = placed[:, 256:512] + rim_part
    high = full[0:256].astype(bf16)
    low = full[256:512].astype(bf16)
    product = mul(jnp.concatenate([high, low, high], axis=1), fwd_w[...])
    part_w = inverse_product(inv_w, channel_product(product, kern_w, tw_w, 256))
    tx2[5] = part_w[0:40]
    tx2[6] = part_w[40:80]
    tx2[7] = part_w[80:120]
    send_on(range(5, 8))

    for step in range(1, CHAN):
        source = lax.rem(me + step, CHAN)
        pltpu.make_async_remote_copy(
            src_ref=tx2.at[source],
            dst_ref=rx2.at[source],
            send_sem=send2.at[source],
            recv_sem=recv2.at[source],
            device_id={"chan": source},
            device_id_type=MESH,
        ).wait_recv()

    block = lax.broadcasted_iota(jnp.int32, (OUTS, 128), 1) // ROWS
    columns = []
    for side in range(2):
        for c in range(RADIX):
            acc = None
            for q in range(4):
                piece = rx2[4 * side + q, :, c // 4 * 128 : (c // 4 + 1) * 128]
                turn = (q - c % 4) % 4 * ROWS
                if turn:
                    piece = pltpu.roll(piece, turn, axis=1)
                acc = piece if acc is None else jnp.where(block == q, piece, acc)
            columns.append(acc)
    gathered = jnp.concatenate(
        [jnp.concatenate(columns[:RADIX], axis=0), jnp.concatenate(columns[RADIX:], axis=0)], axis=1
    )

    def signal(gain):
        high, low = split(gathered * gain)
        return mul(high, back[0]) + mul(low, back[0]) + mul(high, back[1])

    wide_signal = signal(gains[0:1])
    tight_signal = signal(gains[1:2])
    for c in range(RADIX):
        rows = slice(c * OUTS, (c + 1) * OUTS)
        chosen = jnp.where(inside > 0.5, wide_signal[rows], tight_signal[rows])
        for side in range(2):
            result[side, pl.ds(c, OUTS, stride=RADIX), :] = chosen[:, side * 128 : (side + 1) * 128]
    stores = [
        pltpu.make_async_copy(result.at[side], out.at[0, :, pl.ds(side * 128, 128)], out_sem.at[side])
        for side in range(2)
    ]
    for store in stores:
        store.start()
    for store in stores:
        store.wait()

    for step in range(1, CHAN):
        first_copy(step).wait_send()
        second_copy(lax.rem(me + step, CHAN)).wait_send()
    edge_copy(0).wait_send()
    edge_copy(1).wait_send()


def body(frames, links, near, kern, wide, tight, roi):
    apas = lax.axis_size("apa")
    arrays = [
        frames,
        jnp.asarray(forward_ticks()),
        links,
        kern,
        wide.reshape(1, FREQS),
        tight.reshape(1, FREQS),
        jnp.swapaxes(roi, 1, 2),
        jnp.asarray(forward_dense(NU, 128)),
        jnp.asarray(forward_dense(NW, 256)),
        jnp.asarray(inverse_dense(NU, 128, PU, 0, NU, 0, 104)),
        jnp.asarray(inverse_dense(NU, 128, PV, 0, NU, 4, 104)),
        jnp.asarray(inverse_dense(NW, 256, PE, HALO // RADIX, PW // RADIX, 0, 120)),
        jnp.asarray(twiddles(NU, 128, PU)),
        jnp.asarray(twiddles(NW, 256, PE)),
        jnp.asarray(rim_places()),
        jnp.asarray(inverse_ticks()),
        jnp.asarray(spread_filters()),
    ]
    scratch = [pltpu.VMEM(a.shape, a.dtype) for a in arrays]
    scratch += [
        pltpu.VMEM((CHAN, ROWS, PAD), f32),
        pltpu.VMEM((CHAN, ROWS, PAD), f32),
        pltpu.VMEM((CHAN, OUTS, 256), f32),
        pltpu.VMEM((CHAN, OUTS, 256), f32),
        pltpu.VMEM((2, 2 * ROWS, HALO), bf16),
        pltpu.VMEM((2, 2 * ROWS, HALO), bf16),
        pltpu.VMEM((512, LINKS), bf16),
        pltpu.VMEM((256, LINKS), bf16),
        pltpu.VMEM((CHAN, RADIX, 16, PAD), bf16),
        pltpu.VMEM((512, LINKS), bf16),
        pltpu.VMEM((2 * ROWS, LINKS), bf16),
        pltpu.VMEM((RADIX, 2, KB, 128), f32),
        pltpu.VMEM((RADIX, 2, KB, 128), f32),
        pltpu.VMEM((RADIX, 2, KB, 256), f32),
        pltpu.VMEM((2, SHARE, 128), f32),
        pltpu.SemaphoreType.DMA((INPUTS,)),
        pltpu.SemaphoreType.DMA((CHAN,)),
        pltpu.SemaphoreType.DMA((CHAN,)),
        pltpu.SemaphoreType.DMA((CHAN,)),
        pltpu.SemaphoreType.DMA((CHAN,)),
        pltpu.SemaphoreType.DMA((2,)),
        pltpu.SemaphoreType.DMA((2,)),
        pltpu.SemaphoreType.DMA((2,)),
    ]

    def kernel(near_ref, *refs):
        body_kernel(apas, near_ref, *refs)

    return pl.pallas_call(
        kernel,
        out_shape=jax.ShapeDtypeStruct(frames.shape, f32),
        in_specs=[pl.BlockSpec(memory_space=pltpu.SMEM)] + [pl.BlockSpec(memory_space=pltpu.HBM)] * len(arrays),
        out_specs=pl.BlockSpec(memory_space=pltpu.HBM),
        scratch_shapes=scratch,
        compiler_params=pltpu.CompilerParams(
            collective_id=0, has_side_effects=True, vmem_limit_bytes=60 * 1024 * 1024
        ),
    )(near, *arrays)


def solution(mesh):
    placed = (
        P("apa", "chan", None),
        P("apa", None),
        P("apa", None),
        P(None, "chan", None),
        P(),
        P(),
        P("apa", "chan", None),
    )
    return jax.shard_map(body, mesh=mesh, in_specs=placed, out_specs=P("apa", "chan", None), check_vma=False)
```

```python
import math

import jax
import jax.numpy as jnp
import numpy as np
from jax import lax
from jax.experimental import pallas as pl
from jax.experimental.pallas import tpu as pltpu
from jax.sharding import PartitionSpec as P

PU = 800
PV = 800
PW = 960
HALO = 128
BC = 16
BT = 64
CHANNELS = 2560
TICKS = 256
FREQS = 128

CHAN = 8
SHARE = CHANNELS // CHAN
PAD = 384
KB = FREQS // CHAN
ROWS = 2 * KB
RADIX = 8
NU = PU // RADIX
PE = PW + 2 * HALO
NW = PE // RADIX
LINKS = CHAN * PAD
OUTS = SHARE // RADIX

MESH = pl.DeviceIdType.MESH
NT = (((1,), (1,)), ((), ()))
f32 = jnp.float32
bf16 = jnp.bfloat16


def halves(table):
    high = table.astype(bf16)
    low = (table - high.astype(np.float64)).astype(bf16)
    return high, low


def tick_rows():
    row = np.arange(2 * FREQS)
    k = row // ROWS * KB + row % KB
    return k, row % ROWS // KB


def forward_ticks():
    k, z = tick_rows()
    angle = 2.0 * math.pi / TICKS * (k[:, None] * np.arange(TICKS)[None, :] % TICKS)
    return np.where(z[:, None] == 0, np.cos(angle), -np.sin(angle)).astype(bf16)


def inverse_ticks():
    k, z = tick_rows()
    angle = 2.0 * math.pi / TICKS * (k[:, None] * np.arange(TICKS)[None, :] % TICKS)
    weight = np.where(k == 0, 1.0, 2.0)[:, None] / TICKS
    return np.stack(halves(np.where(z[:, None] == 0, np.cos(angle), -np.sin(angle)) * weight))


def spread_filters():
    k, _ = tick_rows()
    return (np.arange(FREQS)[:, None] == k[None, :]).astype(np.float32)


def dense(length, width, scale=1.0):
    index = np.arange(length)
    angle = 2.0 * math.pi / length * (index[:, None] * index[None, :] % length)
    table = np.zeros((width, 2 * width))
    table[:length, :length] = np.cos(angle) * scale
    table[:length, width : width + length] = np.sin(angle) * scale
    return table


def forward_dense(length, width):
    high, low = halves(dense(length, width))
    return np.concatenate([high, high, low], axis=0)


def inverse_dense(length, width, period, first, count, lead, rows):
    table = np.zeros((rows, 2 * width))
    table[lead : lead + count] = dense(length, width, 1.0 / period)[first : first + count]
    return np.stack(halves(table))


def twiddles(length, width, period):
    angle = 2.0 * math.pi / period * (np.arange(RADIX)[:, None] * np.arange(length)[None, :])
    table = np.zeros((2, RADIX, 1, width), np.float32)
    table[0, :, 0, :length] = np.cos(angle)
    table[1, :, 0, :length] = np.sin(angle)
    return table


def rim_places():
    lane = np.arange(2 * HALO)
    place = np.where(lane < HALO, lane // RADIX, (HALO + PW) // RADIX + (lane - HALO) // RADIX)
    return (np.arange(256)[:, None] == place[None, :]).astype(np.float32).astype(bf16)


def levels_of(largest):
    return jnp.ceil(jnp.log2(jnp.maximum(largest, 1e-30)) * STEPS)


def to_short(value):
    return value.astype(jnp.int32).astype(jnp.int16)


def from_short(value):
    return value.astype(jnp.int32).astype(f32)


def split(value):
    high = value.astype(bf16)
    return high, (value - high.astype(f32)).astype(bf16)


def mul(left, right):
    return jnp.dot(left, right, preferred_element_type=f32)


def mul_nt(left, right):
    return lax.dot_general(left, right, NT, preferred_element_type=f32)


def four(values, sign):
    (ar, ai), (br, bi), (cr, ci), (dr, di) = values
    s0r, s0i, s1r, s1i = ar + cr, ai + ci, ar - cr, ai - ci
    s2r, s2i, s3r, s3i = br + dr, bi + di, br - dr, bi - di
    if sign > 0:
        tr, ti = -s3i, s3r
    else:
        tr, ti = s3i, -s3r
    return [(s0r + s2r, s0i + s2i), (s1r + tr, s1i + ti), (s0r - s2r, s0i - s2i), (s1r - tr, s1i - ti)]


def eight(values, sign):
    even = four(values[0::2], sign)
    odd = four(values[1::2], sign)
    root = math.sqrt(0.5)
    r, i = odd[1]
    odd[1] = ((r - sign * i) * root, (i + sign * r) * root)
    r, i = odd[2]
    odd[2] = (-i, r) if sign > 0 else (i, -r)
    r, i = odd[3]
    odd[3] = ((-r - sign * i) * root, (sign * r - i) * root)
    first = [(a + c, b + d) for (a, b), (c, d) in zip(even, odd)]
    second = [(a - c, b - d) for (a, b), (c, d) in zip(even, odd)]
    return first + second


def channel_product(product, kern, twiddle, width):
    values = []
    for c in range(RADIX):
        re = product[c * ROWS : c * ROWS + KB]
        im = product[c * ROWS + KB : (c + 1) * ROWS]
        yr = re[:, :width] + im[:, width:]
        yi = im[:, :width] - re[:, width:]
        if c > 0:
            tc, ts = twiddle[0, c], twiddle[1, c]
            yr, yi = yr * tc + yi * ts, yi * tc - yr * ts
        values.append((yr, yi))
    values = eight(values, -1)
    values = [
        (r * kern[m, 0] - i * kern[m, 1], r * kern[m, 1] + i * kern[m, 0]) for m, (r, i) in enumerate(values)
    ]
    values = eight(values, 1)
    rows = []
    for c, (r, i) in enumerate(values):
        if c > 0:
            tc, ts = twiddle[0, c], twiddle[1, c]
            r, i = r * tc - i * ts, i * tc + r * ts
        rows.append(jnp.concatenate([r, -i], axis=1))
        rows.append(jnp.concatenate([i, r], axis=1))
    return jnp.concatenate(rows, axis=0)


def inverse_product(table, value):
    high, low = split(value)
    return mul_nt(table[0], high) + mul_nt(table[1], high) + mul_nt(table[0], low)


def message(part):
    level = levels_of(jnp.max(jnp.abs(part), axis=0, keepdims=True))
    scaled = jnp.round(part * (LEVELS * jnp.exp2(-level / STEPS)))
    return to_short(jnp.concatenate([scaled, jnp.broadcast_to(level, (8, 256))], axis=0))


def kernel_window(kern, part, start, length, width):
    base = start // 128 * 128
    span = -(-(start - base + length) // 128) * 128
    span = max(span, width)
    piece = kern[part, :, base : base + span]
    if start > base:
        piece = pltpu.roll(piece, span - (start - base), axis=1)
    return piece[:, :width]


INPUTS = 18
LEVELS = 32000.0
STEPS = 8.0


def body_kernel(apas, *refs):
    hbm = refs[:INPUTS]
    out = refs[INPUTS]
    local = refs[INPUTS + 1 : 2 * INPUTS + 1]
    (tx1, rx1, tx2, rx2, txh, rxh, onehot, edge, masks, big, small, kern_u, kern_v, kern_w, result) = refs[
        2 * INPUTS + 1 : 2 * INPUTS + 16
    ]
    in_sem, send1, recv1, send2, recv2, sendh, recvh, out_sem = refs[2 * INPUTS + 16 :]
    (frames, ticks, links, kern, wide, tight, roi, fwd_u, fwd_w, inv_u, inv_v, inv_w, tw_u, tw_w, rim, back, expand, near) = local

    me = lax.axis_index("chan")
    apa = lax.axis_index("apa")
    after = lax.rem(apa + 1, apas)
    before = lax.rem(apa + apas - 1, apas)

    barrier = pltpu.get_barrier_semaphore()
    for step in range(1, CHAN):
        pl.semaphore_signal(barrier, inc=1, device_id={"chan": lax.rem(me + step, CHAN)}, device_id_type=MESH)
    @pl.when(apa < apas - 1)
    def _():
        pl.semaphore_signal(barrier, inc=1, device_id={"apa": after}, device_id_type=MESH)
    @pl.when(apa > 0)
    def _():
        pl.semaphore_signal(barrier, inc=1, device_id={"apa": before}, device_id_type=MESH)

    loads = [pltpu.make_async_copy(hbm[i], local[i], in_sem.at[i]) for i in range(INPUTS)]
    for load in loads:
        load.start()

    loads[0].wait()
    loads[1].wait()
    padded = jnp.concatenate([frames[0], jnp.zeros((PAD - SHARE, TICKS), bf16)], axis=0)
    spectra = mul_nt(ticks[...], padded)
    level = levels_of(jnp.max(jnp.abs(spectra), axis=1, keepdims=True))
    scaled = jnp.round(spectra * (LEVELS * jnp.exp2(-level / STEPS)))
    lane = lax.broadcasted_iota(jnp.int32, scaled.shape, 1)
    tx1[...] = to_short(jnp.where(lane < SHARE, scaled, level)).reshape(CHAN, ROWS, PAD)

    first = apa == 0
    final = apa == apas - 1
    pl.semaphore_wait(barrier, CHAN + 1 - first.astype(jnp.int32) - final.astype(jnp.int32))

    def first_copy(step):
        dest = lax.rem(me + step, CHAN)
        return pltpu.make_async_remote_copy(
            src_ref=tx1.at[dest],
            dst_ref=rx1.at[me],
            send_sem=send1.at[dest],
            recv_sem=recv1.at[me],
            device_id={"chan": dest},
            device_id_type=MESH,
        )

    for step in range(1, CHAN):
        first_copy(step).start()
    rx1[me] = tx1[me]

    loads[2].wait()
    for s in range(CHAN):
        wire = links[:, s * SHARE : (s + 1) * SHARE]
        wire = jnp.concatenate([wire, jnp.full((1, PAD - SHARE), -8, jnp.int32)], axis=1)
        group = lax.shift_right_arithmetic(wire, 3)
        rest = lax.bitwise_and(wire, 7)
        place = group + jnp.where(wire >= PU + PV, 72, jnp.where(wire >= PU, 28, 0))
        row = lax.broadcasted_iota(jnp.int32, (512, PAD), 0)
        onehot[:, s * PAD : (s + 1) * PAD] = jnp.where(row == place, 1.0, 0.0).astype(bf16)
        row = lax.broadcasted_iota(jnp.int32, (256, PAD), 0)
        spot = row + jnp.where(row >= HALO, CHANNELS - 2 * HALO, PU + PV)
        edge[:, s * PAD : (s + 1) * PAD] = jnp.where(spot == wire, 1.0, 0.0).astype(bf16)
        for h in range(RADIX):
            here = jnp.where((rest == h) & (wire >= 0), 1.0, 0.0)
            masks[s, h] = jnp.broadcast_to(here, (16, PAD)).astype(bf16)

    loads[3].wait()
    for m in range(RADIX):
        for part in range(2):
            kern_u[m, part] = kernel_window(kern, part, NU * m, NU, 128)
            kern_v[m, part] = kernel_window(kern, part, PU + NU * m, NU, 128)
            kern_w[m, part] = kernel_window(kern, part, PU + PV + NW * m, NW, 256)

    for load in loads[4:]:
        load.wait()
    gains = jnp.concatenate([wide[...], tight[...], jnp.zeros((6, FREQS), f32)], axis=0)
    gains = jnp.dot(gains, expand[0:FREQS], precision=lax.Precision.HIGHEST, preferred_element_type=f32)
    inside = roi[0].astype(f32)
    row_index = lax.broadcasted_iota(jnp.int32, (OUTS, SHARE // BC), 0) // (BC // RADIX)
    col_index = lax.broadcasted_iota(jnp.int32, (OUTS, SHARE // BC), 1)
    pick = jnp.where(row_index == col_index, 1.0, 0.0)
    inside = mul_nt(pick, inside)
    row_index = lax.broadcasted_iota(jnp.int32, (TICKS // BT, TICKS), 0)
    col_index = lax.broadcasted_iota(jnp.int32, (TICKS // BT, TICKS), 1) // BT
    inside = mul(inside, jnp.where(row_index == col_index, 1.0, 0.0))

    for step in range(1, CHAN):
        source = lax.rem(me + step, CHAN)
        pltpu.make_async_remote_copy(
            src_ref=tx1.at[source],
            dst_ref=rx1.at[source],
            send_sem=send1.at[source],
            recv_sem=recv1.at[source],
            device_id={"chan": source},
            device_id_type=MESH,
        ).wait_recv()
    for s in range(CHAN):
        lanes = slice(s * PAD, (s + 1) * PAD)
        value = from_short(rx1[s])
        high, low = split(value * (jnp.exp2(value[:, SHARE : SHARE + 1] / STEPS) / LEVELS))
        small[0:ROWS, lanes] = high
        small[ROWS : 2 * ROWS, lanes] = low

    bands = mul_nt(small[...], edge[...])
    first_band = bands[:, :HALO]
    last_band = bands[:, HALO:]
    lower = jnp.broadcast_to(near[:, 0:1], first_band.shape)
    upper = jnp.broadcast_to(near[:, 1:2], first_band.shape)
    none = jnp.zeros_like(first_band)
    to_after = jnp.where(upper == after, last_band, jnp.where(lower == after, first_band, none))
    to_before = jnp.where(lower == before, first_band, jnp.where(upper == before, last_band, none))
    txh[0] = to_after.astype(bf16)
    txh[1] = to_before.astype(bf16)

    @pl.when(apa == 0)
    def _():
        rxh[0] = jnp.zeros((2 * ROWS, HALO), bf16)

    @pl.when(apa == apas - 1)
    def _():
        rxh[1] = jnp.zeros((2 * ROWS, HALO), bf16)

    def edge_copy(way):
        return pltpu.make_async_remote_copy(
            src_ref=txh.at[way],
            dst_ref=rxh.at[way],
            send_sem=sendh.at[way],
            recv_sem=recvh.at[way],
            device_id={"apa": after if way == 0 else before},
            device_id_type=MESH,
        )

    @pl.when(apa < apas - 1)
    def _():
        edge_copy(0).start()

    @pl.when(apa > 0)
    def _():
        edge_copy(1).start()

    for s in range(CHAN):
        lanes = slice(s * PAD, (s + 1) * PAD)
        for h in range(RADIX):
            mask = jnp.concatenate([masks[s, h], masks[s, h]], axis=0)
            big[h * ROWS : (h + 1) * ROWS, lanes] = small[0:ROWS, lanes] * mask
            big[256 + h * ROWS : 256 + (h + 1) * ROWS, lanes] = small[ROWS : 2 * ROWS, lanes] * mask
    placed = mul_nt(big[...], onehot[...])

    def second_copy(dest):
        return pltpu.make_async_remote_copy(
            src_ref=tx2.at[dest],
            dst_ref=rx2.at[me],
            send_sem=send2.at[dest],
            recv_sem=recv2.at[me],
            device_id={"chan": dest},
            device_id_type=MESH,
        )

    def send_on(dests):
        for dest in dests:

            @pl.when(me != dest)
            def _():
                second_copy(dest).start()

            @pl.when(me == dest)
            def _():
                rx2[dest] = tx2[dest]

    def plane(lanes, fwd, kern_part, twiddle, table, width):
        high = placed[0:256, lanes].astype(bf16)
        low = placed[256:512, lanes].astype(bf16)
        product = mul(jnp.concatenate([high, low, high], axis=1), fwd[...])
        return inverse_product(table, channel_product(product, kern_part, twiddle, width))

    part_u = plane(slice(0, 128), fwd_u, kern_u, tw_u, inv_u, 128)
    part_v = plane(slice(128, 256), fwd_u, kern_v, tw_u, inv_v, 128)
    middle = jnp.concatenate([part_u[80:96], part_u[96:104] + part_v[0:8], part_v[8:24]], axis=0)
    for dest, part in enumerate([part_u[0:40], part_u[40:80], middle, part_v[24:64], part_v[64:104]]):
        tx2[dest] = message(part)
    send_on(range(0, 5))

    @pl.when(apa > 0)
    def _():
        edge_copy(0).wait_recv()

    @pl.when(apa < apas - 1)
    def _():
        edge_copy(1).wait_recv()
    from_before = rxh[0].astype(f32)
    from_after = rxh[1].astype(f32)
    blank = jnp.zeros_like(from_before)
    rim_low = jnp.where(lower == before, from_before, jnp.where(lower == after, from_after, blank))
    rim_up = jnp.where(upper == after, from_after, jnp.where(upper == before, from_before, blank))
    rims = jnp.concatenate([rim_low, rim_up], axis=1)
    lane = lax.bitwise_and(lax.broadcasted_iota(jnp.int32, (ROWS, 2 * HALO), 1), RADIX - 1)
    spread = [
        jnp.where(lane == h, rims[part * ROWS : (part + 1) * ROWS], 0.0) for part in range(2) for h in range(RADIX)
    ]
    rim_part = mul_nt(jnp.concatenate(spread, axis=0).astype(bf16), rim[...])
    full = placed[:, 256:512] + rim_part
    high = full[0:256].astype(bf16)
    low = full[256:512].astype(bf16)
    product = mul(jnp.concatenate([high, low, high], axis=1), fwd_w[...])
    part_w = inverse_product(inv_w, channel_product(product, kern_w, tw_w, 256))
    for dest in range(3):
        tx2[5 + dest] = message(part_w[dest * OUTS : (dest + 1) * OUTS])
    send_on(range(5, 8))

    for step in range(1, CHAN):
        source = lax.rem(me + step, CHAN)
        pltpu.make_async_remote_copy(
            src_ref=tx2.at[source],
            dst_ref=rx2.at[source],
            send_sem=send2.at[source],
            recv_sem=recv2.at[source],
            device_id={"chan": source},
            device_id_type=MESH,
        ).wait_recv()

    block = lax.broadcasted_iota(jnp.int32, (OUTS, 128), 1) // ROWS
    columns = []
    pieces = []
    for s in range(CHAN):
        value = from_short(rx2[s])
        pieces.append(value[:OUTS] * (jnp.exp2(value[OUTS : OUTS + 1] / STEPS) / LEVELS))
    for side in range(2):
        for c in range(RADIX):
            acc = None
            for q in range(4):
                piece = pieces[4 * side + q][:, c // 4 * 128 : (c // 4 + 1) * 128]
                turn = (q - c % 4) % 4 * ROWS
                if turn:
                    piece = pltpu.roll(piece, turn, axis=1)
                acc = piece if acc is None else jnp.where(block == q, piece, acc)
            columns.append(acc)
    gathered = jnp.concatenate(
        [jnp.concatenate(columns[:RADIX], axis=0), jnp.concatenate(columns[RADIX:], axis=0)], axis=1
    )

    def signal(gain):
        high, low = split(gathered * gain)
        return mul(high, back[0]) + mul(low, back[0]) + mul(high, back[1])

    wide_signal = signal(gains[0:1])
    tight_signal = signal(gains[1:2])
    for c in range(RADIX):
        rows = slice(c * OUTS, (c + 1) * OUTS)
        chosen = jnp.where(inside > 0.5, wide_signal[rows], tight_signal[rows])
        for side in range(2):
            result[side, pl.ds(c, OUTS, stride=RADIX), :] = chosen[:, side * 128 : (side + 1) * 128]
    stores = [
        pltpu.make_async_copy(result.at[side], out.at[0, :, pl.ds(side * 128, 128)], out_sem.at[side])
        for side in range(2)
    ]
    for store in stores:
        store.start()
    for store in stores:
        store.wait()

    for step in range(1, CHAN):
        first_copy(step).wait_send()
        second_copy(lax.rem(me + step, CHAN)).wait_send()
    @pl.when(apa < apas - 1)
    def _():
        edge_copy(0).wait_send()

    @pl.when(apa > 0)
    def _():
        edge_copy(1).wait_send()


def body(frames, links, near, kern, wide, tight, roi):
    apas = lax.axis_size("apa")
    arrays = [
        frames,
        jnp.asarray(forward_ticks()),
        links,
        kern,
        wide.reshape(1, FREQS),
        tight.reshape(1, FREQS),
        jnp.swapaxes(roi, 1, 2),
        jnp.asarray(forward_dense(NU, 128)),
        jnp.asarray(forward_dense(NW, 256)),
        jnp.asarray(inverse_dense(NU, 128, PU, 0, NU, 0, 104)),
        jnp.asarray(inverse_dense(NU, 128, PV, 0, NU, 4, 104)),
        jnp.asarray(inverse_dense(NW, 256, PE, HALO // RADIX, PW // RADIX, 0, 120)),
        jnp.asarray(twiddles(NU, 128, PU)),
        jnp.asarray(twiddles(NW, 256, PE)),
        jnp.asarray(rim_places()),
        jnp.asarray(inverse_ticks()),
        jnp.asarray(spread_filters()),
        near,
    ]
    scratch = [pltpu.VMEM(a.shape, a.dtype) for a in arrays]
    scratch += [
        pltpu.VMEM((CHAN, ROWS, PAD), jnp.int16),
        pltpu.VMEM((CHAN, ROWS, PAD), jnp.int16),
        pltpu.VMEM((CHAN, OUTS + 8, 256), jnp.int16),
        pltpu.VMEM((CHAN, OUTS + 8, 256), jnp.int16),
        pltpu.VMEM((2, 2 * ROWS, HALO), bf16),
        pltpu.VMEM((2, 2 * ROWS, HALO), bf16),
        pltpu.VMEM((512, LINKS), bf16),
        pltpu.VMEM((256, LINKS), bf16),
        pltpu.VMEM((CHAN, RADIX, 16, PAD), bf16),
        pltpu.VMEM((512, LINKS), bf16),
        pltpu.VMEM((2 * ROWS, LINKS), bf16),
        pltpu.VMEM((RADIX, 2, KB, 128), f32),
        pltpu.VMEM((RADIX, 2, KB, 128), f32),
        pltpu.VMEM((RADIX, 2, KB, 256), f32),
        pltpu.VMEM((2, SHARE, 128), f32),
        pltpu.SemaphoreType.DMA((INPUTS,)),
        pltpu.SemaphoreType.DMA((CHAN,)),
        pltpu.SemaphoreType.DMA((CHAN,)),
        pltpu.SemaphoreType.DMA((CHAN,)),
        pltpu.SemaphoreType.DMA((CHAN,)),
        pltpu.SemaphoreType.DMA((2,)),
        pltpu.SemaphoreType.DMA((2,)),
        pltpu.SemaphoreType.DMA((2,)),
    ]

    def kernel(*refs):
        body_kernel(apas, *refs)

    halves_out = pl.pallas_call(
        kernel,
        out_shape=jax.ShapeDtypeStruct(frames.shape, f32),
        in_specs=[pl.BlockSpec(memory_space=pltpu.HBM)] * len(arrays),
        out_specs=pl.BlockSpec(memory_space=pl.ANY),
        scratch_shapes=scratch,
        compiler_params=pltpu.CompilerParams(
            collective_id=0, has_side_effects=True, vmem_limit_bytes=40 * 1024 * 1024
        ),
    )(*[pltpu.with_memory_space_constraint(a, pltpu.HBM) for a in arrays])
    return halves_out


def solution(mesh):
    placed = (
        P("apa", "chan", None),
        P("apa", None),
        P("apa", None),
        P(None, "chan", None),
        P(),
        P(),
        P("apa", "chan", None),
    )
    return jax.shard_map(body, mesh=mesh, in_specs=placed, out_specs=P("apa", "chan", None), check_vma=False)
```

```python
import math

import jax
import jax.numpy as jnp
import numpy as np
from jax import lax
from jax.experimental import pallas as pl
from jax.experimental.pallas import tpu as pltpu
from jax.sharding import PartitionSpec as P

PU = 800
PV = 800
PW = 960
HALO = 128
BC = 16
BT = 64
CHANNELS = 2560
TICKS = 256
FREQS = 128

CHAN = 8
SHARE = CHANNELS // CHAN
PAD = 384
KB = FREQS // CHAN
ROWS = 2 * KB
RADIX = 8
NU = PU // RADIX
PE = PW + 2 * HALO
NW = PE // RADIX
OUTS = SHARE // RADIX

MESH = pl.DeviceIdType.MESH
NT = (((1,), (1,)), ((), ()))
f32 = jnp.float32
bf16 = jnp.bfloat16


def halves(table):
    high = table.astype(bf16)
    low = (table - high.astype(np.float64)).astype(bf16)
    return high, low


def tick_rows():
    row = np.arange(2 * FREQS)
    k = row // ROWS * KB + row % KB
    return k, row % ROWS // KB


def forward_ticks():
    k, z = tick_rows()
    angle = 2.0 * math.pi / TICKS * (k[:, None] * np.arange(TICKS)[None, :] % TICKS)
    return np.where(z[:, None] == 0, np.cos(angle), -np.sin(angle)).astype(bf16)


def inverse_ticks():
    k, z = tick_rows()
    angle = 2.0 * math.pi / TICKS * (k[:, None] * np.arange(TICKS)[None, :] % TICKS)
    weight = np.where(k == 0, 1.0, 2.0)[:, None] / TICKS
    return np.stack(halves(np.where(z[:, None] == 0, np.cos(angle), -np.sin(angle)) * weight))


def spread_filters():
    k, _ = tick_rows()
    return (np.arange(FREQS)[:, None] == k[None, :]).astype(np.float32)


def dense(length, width, scale=1.0):
    index = np.arange(length)
    angle = 2.0 * math.pi / length * (index[:, None] * index[None, :] % length)
    table = np.zeros((width, 2 * width))
    table[:length, :length] = np.cos(angle) * scale
    table[:length, width : width + length] = np.sin(angle) * scale
    return table


def forward_dense(length, width):
    high, low = halves(dense(length, width))
    return np.concatenate([high, high, low], axis=0)


def inverse_dense(length, width, period, first, count, lead, rows):
    table = np.zeros((rows, 2 * width))
    table[lead : lead + count] = dense(length, width, 1.0 / period)[first : first + count]
    return np.stack(halves(table))


def twiddles(length, width, period):
    angle = 2.0 * math.pi / period * (np.arange(RADIX)[:, None] * np.arange(length)[None, :])
    table = np.zeros((2, RADIX, 1, width), np.float32)
    table[0, :, 0, :length] = np.cos(angle)
    table[1, :, 0, :length] = np.sin(angle)
    return table


def rim_places():
    lane = np.arange(2 * HALO)
    place = np.where(lane < HALO, lane // RADIX, (HALO + PW) // RADIX + (lane - HALO) // RADIX)
    return (np.arange(256)[:, None] == place[None, :]).astype(np.float32).astype(bf16)


def levels_of(largest):
    return jnp.ceil(jnp.log2(jnp.maximum(largest, 1e-30)) * STEPS)


def to_short(value):
    return value.astype(jnp.int32).astype(jnp.int16)


def from_short(value):
    return value.astype(jnp.int32).astype(f32)


def split(value):
    high = value.astype(bf16)
    return high, (value - high.astype(f32)).astype(bf16)


def mul(left, right):
    return jnp.dot(left, right, preferred_element_type=f32)


def mul_nt(left, right):
    return lax.dot_general(left, right, NT, preferred_element_type=f32)


def four(values, sign):
    (ar, ai), (br, bi), (cr, ci), (dr, di) = values
    s0r, s0i, s1r, s1i = ar + cr, ai + ci, ar - cr, ai - ci
    s2r, s2i, s3r, s3i = br + dr, bi + di, br - dr, bi - di
    if sign > 0:
        tr, ti = -s3i, s3r
    else:
        tr, ti = s3i, -s3r
    return [(s0r + s2r, s0i + s2i), (s1r + tr, s1i + ti), (s0r - s2r, s0i - s2i), (s1r - tr, s1i - ti)]


def eight(values, sign):
    even = four(values[0::2], sign)
    odd = four(values[1::2], sign)
    root = math.sqrt(0.5)
    r, i = odd[1]
    odd[1] = ((r - sign * i) * root, (i + sign * r) * root)
    r, i = odd[2]
    odd[2] = (-i, r) if sign > 0 else (i, -r)
    r, i = odd[3]
    odd[3] = ((-r - sign * i) * root, (sign * r - i) * root)
    first = [(a + c, b + d) for (a, b), (c, d) in zip(even, odd)]
    second = [(a - c, b - d) for (a, b), (c, d) in zip(even, odd)]
    return first + second


def channel_product(product, kern, twiddle, width):
    values = []
    for c in range(RADIX):
        re = product[c * ROWS : c * ROWS + KB]
        im = product[c * ROWS + KB : (c + 1) * ROWS]
        yr = re[:, :width] + im[:, width:]
        yi = im[:, :width] - re[:, width:]
        if c > 0:
            tc, ts = twiddle[0, c], twiddle[1, c]
            yr, yi = yr * tc + yi * ts, yi * tc - yr * ts
        values.append((yr, yi))
    values = eight(values, -1)
    values = [
        (r * kern[m, 0] - i * kern[m, 1], r * kern[m, 1] + i * kern[m, 0]) for m, (r, i) in enumerate(values)
    ]
    values = eight(values, 1)
    rows = []
    for c, (r, i) in enumerate(values):
        if c > 0:
            tc, ts = twiddle[0, c], twiddle[1, c]
            r, i = r * tc - i * ts, i * tc + r * ts
        rows.append(jnp.concatenate([r, -i], axis=1))
        rows.append(jnp.concatenate([i, r], axis=1))
    return jnp.concatenate(rows, axis=0)


def inverse_product(table, value):
    high, low = split(value)
    return mul_nt(table[0], high) + mul_nt(table[1], high) + mul_nt(table[0], low)


def message(part):
    level = levels_of(jnp.max(jnp.abs(part), axis=0, keepdims=True))
    scaled = jnp.round(part * (LEVELS * jnp.exp2(-level / STEPS)))
    return to_short(jnp.concatenate([scaled, jnp.broadcast_to(level, (8, part.shape[1]))], axis=0))


def kernel_window(kern, part, start, length, width):
    base = start // 128 * 128
    span = -(-(start - base + length) // 128) * 128
    span = max(span, width)
    piece = kern[part, :, base : base + span]
    if start > base:
        piece = pltpu.roll(piece, span - (start - base), axis=1)
    return piece[:, :width]


INPUTS = 18
LEVELS = 32000.0
STEPS = 8.0


def body_kernel(apas, *refs):
    hbm = refs[:INPUTS]
    out = refs[INPUTS]
    local = refs[INPUTS + 1 : 2 * INPUTS + 1]
    (tx1, rx1, tx2, rx2, txh, rxh, onehot, masks, big, kern_u, kern_v, kern_w, result) = refs[
        2 * INPUTS + 1 : 2 * INPUTS + 14
    ]
    in_sem, send1, recv1, send2, recv2, sendh, recvh, entered, out_sem = refs[2 * INPUTS + 14 :]
    (frames, ticks, links, kern, wide, tight, roi, fwd_u, fwd_w, inv_u, inv_v, inv_w, tw_u, tw_w, rim, back, expand, near) = local

    me = lax.axis_index("chan")
    apa = lax.axis_index("apa")
    after = apa + 1
    before = apa - 1
    has_after = apa < apas - 1
    has_before = apa > 0
    even = lax.rem(apa, 2) == 0
    wait_after = has_after & (even | (after == apas // 2))
    wait_before = has_before & even & (apa != apas // 2)
    greet_after = has_after & jnp.logical_not(wait_after)
    greet_before = has_before & jnp.logical_not(wait_before)

    barrier = pltpu.get_barrier_semaphore()
    for step in range(1, CHAN):
        pl.semaphore_signal(barrier, inc=1, device_id={"chan": lax.rem(me + step, CHAN)}, device_id_type=MESH)
    loads = [pltpu.make_async_copy(hbm[i], local[i], in_sem.at[i]) for i in range(INPUTS)]
    for load in loads:
        load.start()

    loads[0].wait()
    loads[1].wait()
    padded = jnp.concatenate([frames[0], jnp.zeros((PAD - SHARE, TICKS), bf16)], axis=0)
    spectra = mul_nt(ticks[...], padded)
    level = levels_of(jnp.max(jnp.abs(spectra), axis=1, keepdims=True))
    scaled = jnp.round(spectra * (LEVELS * jnp.exp2(-level / STEPS)))
    lane = lax.broadcasted_iota(jnp.int32, scaled.shape, 1)
    tx1[...] = to_short(jnp.where(lane < SHARE, scaled, level)).reshape(CHAN, ROWS, PAD)

    pl.semaphore_wait(barrier, CHAN - 1 + wait_after.astype(jnp.int32) + wait_before.astype(jnp.int32))

    @pl.when(greet_after)
    def _():
        pl.semaphore_signal(barrier, inc=1, device_id={"apa": after}, device_id_type=MESH)

    @pl.when(greet_before)
    def _():
        pl.semaphore_signal(barrier, inc=1, device_id={"apa": before}, device_id_type=MESH)

    def first_copy(step):
        dest = lax.rem(me + step, CHAN)
        return pltpu.make_async_remote_copy(
            src_ref=tx1.at[dest],
            dst_ref=rx1.at[me],
            send_sem=send1.at[dest],
            recv_sem=recv1.at[me],
            device_id={"chan": dest},
            device_id_type=MESH,
        )

    for step in range(1, CHAN):
        first_copy(step).start()
    rx1[me] = tx1[me]

    @pl.when(wait_after)
    def _():
        pl.semaphore_signal(entered.at[1], inc=1, device_id={"apa": after}, device_id_type=MESH)

    @pl.when(wait_before)
    def _():
        pl.semaphore_signal(entered.at[0], inc=1, device_id={"apa": before}, device_id_type=MESH)

    loads[2].wait()
    loads[17].wait()
    mine = jnp.zeros((1, SHARE), jnp.int32)
    for s in range(CHAN):
        mine = jnp.where(me == s, links[:, s * SHARE : (s + 1) * SHARE], mine)
    mine = jnp.concatenate([mine, jnp.full((1, PAD - SHARE), -8, jnp.int32)], axis=1)
    row = lax.broadcasted_iota(jnp.int32, (2 * HALO, PAD), 0)
    spot = row + jnp.where(row >= HALO, CHANNELS - 2 * HALO, PU + PV)
    local_edge = jnp.where(spot == mine, 1.0, 0.0).astype(bf16)
    high, low = split(spectra)
    bands = mul_nt(high, local_edge) + mul_nt(low, local_edge)
    first_band = bands[:, :HALO]
    last_band = bands[:, HALO:]
    lower = jnp.broadcast_to(near[:, 0:1], first_band.shape)
    upper = jnp.broadcast_to(near[:, 1:2], first_band.shape)
    none = jnp.zeros_like(first_band)
    to_after = jnp.where(upper == after, last_band, jnp.where(lower == after, first_band, none))
    to_before = jnp.where(lower == before, first_band, jnp.where(upper == before, last_band, none))
    for way, band in enumerate([to_after, to_before]):
        for dest in range(CHAN):
            txh[way, dest] = message(band[dest * ROWS : (dest + 1) * ROWS])

    def edge_copy(way, dest):
        return pltpu.make_async_remote_copy(
            src_ref=txh.at[way, dest],
            dst_ref=rxh.at[way, me],
            send_sem=sendh.at[way, dest],
            recv_sem=recvh.at[way, me],
            device_id={"apa": after if way == 0 else before, "chan": dest},
            device_id_type=MESH,
        )

    def send_edges(way):
        for step in range(CHAN):
            edge_copy(way, lax.rem(me + step, CHAN)).start()

    @pl.when(wait_after)
    def _():
        send_edges(0)

    @pl.when(wait_before)
    def _():
        send_edges(1)

    @pl.when(apa == 0)
    def _():
        rxh[0] = jnp.zeros((CHAN, ROWS + 8, HALO), jnp.int16)

    @pl.when(apa == apas - 1)
    def _():
        rxh[1] = jnp.zeros((CHAN, ROWS + 8, HALO), jnp.int16)

    for part in range(5):
        lanes = slice(part * 512, (part + 1) * 512)
        wire = links[:, lanes]
        group = lax.shift_right_arithmetic(wire, 3)
        rest = lax.bitwise_and(wire, 7)
        place = group + jnp.where(wire >= PU + PV, 72, jnp.where(wire >= PU, 28, 0))
        row = lax.broadcasted_iota(jnp.int32, (512, 512), 0)
        onehot[:, lanes] = jnp.where(row == place, 1.0, 0.0).astype(bf16)
        for h in range(RADIX):
            masks[h, :, lanes] = jnp.broadcast_to(jnp.where(rest == h, 1.0, 0.0), (16, 512)).astype(bf16)

    loads[3].wait()
    for m in range(RADIX):
        for part in range(2):
            kern_u[m, part] = kernel_window(kern, part, NU * m, NU, 128)
            kern_v[m, part] = kernel_window(kern, part, PU + NU * m, NU, 128)
            kern_w[m, part] = kernel_window(kern, part, PU + PV + NW * m, NW, 256)

    for load in loads[4:17]:
        load.wait()
    gains = jnp.concatenate([wide[...], tight[...], jnp.zeros((6, FREQS), f32)], axis=0)
    gains = jnp.dot(gains, expand[0:FREQS], precision=lax.Precision.HIGHEST, preferred_element_type=f32)
    inside = roi[0].astype(f32)
    row_index = lax.broadcasted_iota(jnp.int32, (OUTS, SHARE // BC), 0) // (BC // RADIX)
    col_index = lax.broadcasted_iota(jnp.int32, (OUTS, SHARE // BC), 1)
    pick = jnp.where(row_index == col_index, 1.0, 0.0)
    inside = mul_nt(pick, inside)
    row_index = lax.broadcasted_iota(jnp.int32, (TICKS // BT, TICKS), 0)
    col_index = lax.broadcasted_iota(jnp.int32, (TICKS // BT, TICKS), 1) // BT
    inside = mul(inside, jnp.where(row_index == col_index, 1.0, 0.0))

    @pl.when(greet_after)
    def _():
        pl.semaphore_wait(entered.at[0], 1)
        send_edges(0)

    @pl.when(greet_before)
    def _():
        pl.semaphore_wait(entered.at[1], 1)
        send_edges(1)

    for step in range(1, CHAN):
        source = lax.rem(me + step, CHAN)
        pltpu.make_async_remote_copy(
            src_ref=tx1.at[source],
            dst_ref=rx1.at[source],
            send_sem=send1.at[source],
            recv_sem=recv1.at[source],
            device_id={"chan": source},
            device_id_type=MESH,
        ).wait_recv()
    for pair in range(CHAN // 2):
        lanes = slice(pair * 2 * SHARE, (pair + 1) * 2 * SHARE)
        values = []
        for s in (2 * pair, 2 * pair + 1):
            value = from_short(rx1[s])
            values.append(value[:, :SHARE] * (jnp.exp2(value[:, SHARE : SHARE + 1] / STEPS) / LEVELS))
        high, low = split(jnp.concatenate(values, axis=1))
        for h in range(RADIX):
            mask = jnp.concatenate([masks[h, :, lanes], masks[h, :, lanes]], axis=0)
            big[h * ROWS : (h + 1) * ROWS, lanes] = high * mask
            big[256 + h * ROWS : 256 + (h + 1) * ROWS, lanes] = low * mask
    placed = mul_nt(big[...], onehot[...])

    def second_copy(dest):
        return pltpu.make_async_remote_copy(
            src_ref=tx2.at[dest],
            dst_ref=rx2.at[me],
            send_sem=send2.at[dest],
            recv_sem=recv2.at[me],
            device_id={"chan": dest},
            device_id_type=MESH,
        )

    def send_on(dests):
        for dest in dests:

            @pl.when(me != dest)
            def _():
                second_copy(dest).start()

            @pl.when(me == dest)
            def _():
                rx2[dest] = tx2[dest]

    def plane(lanes, fwd, kern_part, twiddle, table, width):
        high = placed[0:256, lanes].astype(bf16)
        low = placed[256:512, lanes].astype(bf16)
        product = mul(jnp.concatenate([high, low, high], axis=1), fwd[...])
        return inverse_product(table, channel_product(product, kern_part, twiddle, width))

    part_u = plane(slice(0, 128), fwd_u, kern_u, tw_u, inv_u, 128)
    part_v = plane(slice(128, 256), fwd_u, kern_v, tw_u, inv_v, 128)
    middle = jnp.concatenate([part_u[80:96], part_u[96:104] + part_v[0:8], part_v[8:24]], axis=0)
    for dest, part in enumerate([part_u[0:40], part_u[40:80], middle, part_v[24:64], part_v[64:104]]):
        tx2[dest] = message(part)
    send_on(range(0, 5))

    def edge_arrivals(way):
        for source in range(CHAN):
            pltpu.make_async_remote_copy(
                src_ref=txh.at[way, source],
                dst_ref=rxh.at[way, source],
                send_sem=sendh.at[way, source],
                recv_sem=recvh.at[way, source],
                device_id={"apa": before if way == 0 else after, "chan": source},
                device_id_type=MESH,
            ).wait_recv()

    @pl.when(has_before)
    def _():
        edge_arrivals(0)

    @pl.when(has_after)
    def _():
        edge_arrivals(1)

    sums = []
    for way in range(2):
        total = jnp.zeros((ROWS, HALO), f32)
        for source in range(CHAN):
            value = from_short(rxh[way, source])
            total = total + value[:ROWS] * (jnp.exp2(value[ROWS : ROWS + 1] / STEPS) / LEVELS)
        sums.append(total)
    from_before, from_after = sums
    lower = lower[:ROWS]
    upper = upper[:ROWS]
    blank = jnp.zeros_like(from_before)
    rim_low = jnp.where(lower == before, from_before, jnp.where(lower == after, from_after, blank))
    rim_up = jnp.where(upper == after, from_after, jnp.where(upper == before, from_before, blank))
    rims = jnp.concatenate([rim_low, rim_up], axis=1)
    lane = lax.bitwise_and(lax.broadcasted_iota(jnp.int32, (ROWS, 2 * HALO), 1), RADIX - 1)
    spread = [jnp.where(lane == h, part.astype(f32), 0.0) for part in split(rims) for h in range(RADIX)]
    rim_part = mul_nt(jnp.concatenate(spread, axis=0).astype(bf16), rim[...])
    full = placed[:, 256:512] + rim_part
    high = full[0:256].astype(bf16)
    low = full[256:512].astype(bf16)
    product = mul(jnp.concatenate([high, low, high], axis=1), fwd_w[...])
    part_w = inverse_product(inv_w, channel_product(product, kern_w, tw_w, 256))
    for dest in range(3):
        tx2[5 + dest] = message(part_w[dest * OUTS : (dest + 1) * OUTS])
    send_on(range(5, 8))

    for step in range(1, CHAN):
        source = lax.rem(me + step, CHAN)
        pltpu.make_async_remote_copy(
            src_ref=tx2.at[source],
            dst_ref=rx2.at[source],
            send_sem=send2.at[source],
            recv_sem=recv2.at[source],
            device_id={"chan": source},
            device_id_type=MESH,
        ).wait_recv()

    block = lax.broadcasted_iota(jnp.int32, (OUTS, 128), 1) // ROWS
    columns = []
    pieces = []
    for s in range(CHAN):
        value = from_short(rx2[s])
        pieces.append(value[:OUTS] * (jnp.exp2(value[OUTS : OUTS + 1] / STEPS) / LEVELS))
    for side in range(2):
        for c in range(RADIX):
            acc = None
            for q in range(4):
                piece = pieces[4 * side + q][:, c // 4 * 128 : (c // 4 + 1) * 128]
                turn = (q - c % 4) % 4 * ROWS
                if turn:
                    piece = pltpu.roll(piece, turn, axis=1)
                acc = piece if acc is None else jnp.where(block == q, piece, acc)
            columns.append(acc)
    gathered = jnp.concatenate(
        [jnp.concatenate(columns[:RADIX], axis=0), jnp.concatenate(columns[RADIX:], axis=0)], axis=1
    )

    def signal(gain):
        high, low = split(gathered * gain)
        return mul(high, back[0]) + mul(low, back[0]) + mul(high, back[1])

    wide_signal = signal(gains[0:1])
    tight_signal = signal(gains[1:2])
    for c in range(RADIX):
        rows = slice(c * OUTS, (c + 1) * OUTS)
        chosen = jnp.where(inside > 0.5, wide_signal[rows], tight_signal[rows])
        for side in range(2):
            result[side, pl.ds(c, OUTS, stride=RADIX), :] = chosen[:, side * 128 : (side + 1) * 128]
    stores = [
        pltpu.make_async_copy(result.at[side], out.at[0, :, pl.ds(side * 128, 128)], out_sem.at[side])
        for side in range(2)
    ]
    for store in stores:
        store.start()
    for store in stores:
        store.wait()

    for step in range(1, CHAN):
        first_copy(step).wait_send()
        second_copy(lax.rem(me + step, CHAN)).wait_send()
    @pl.when(has_after)
    def _():
        for dest in range(CHAN):
            edge_copy(0, dest).wait_send()

    @pl.when(has_before)
    def _():
        for dest in range(CHAN):
            edge_copy(1, dest).wait_send()


def body(frames, links, near, kern, wide, tight, roi):
    apas = lax.axis_size("apa")
    arrays = [
        frames,
        jnp.asarray(forward_ticks()),
        links,
        kern,
        wide.reshape(1, FREQS),
        tight.reshape(1, FREQS),
        jnp.swapaxes(roi, 1, 2),
        jnp.asarray(forward_dense(NU, 128)),
        jnp.asarray(forward_dense(NW, 256)),
        jnp.asarray(inverse_dense(NU, 128, PU, 0, NU, 0, 104)),
        jnp.asarray(inverse_dense(NU, 128, PV, 0, NU, 4, 104)),
        jnp.asarray(inverse_dense(NW, 256, PE, HALO // RADIX, PW // RADIX, 0, 120)),
        jnp.asarray(twiddles(NU, 128, PU)),
        jnp.asarray(twiddles(NW, 256, PE)),
        jnp.asarray(rim_places()),
        jnp.asarray(inverse_ticks()),
        jnp.asarray(spread_filters()),
        near,
    ]
    scratch = [pltpu.VMEM(a.shape, a.dtype) for a in arrays]
    scratch += [
        pltpu.VMEM((CHAN, ROWS, PAD), jnp.int16),
        pltpu.VMEM((CHAN, ROWS, PAD), jnp.int16),
        pltpu.VMEM((CHAN, OUTS + 8, 256), jnp.int16),
        pltpu.VMEM((CHAN, OUTS + 8, 256), jnp.int16),
        pltpu.VMEM((2, CHAN, ROWS + 8, HALO), jnp.int16),
        pltpu.VMEM((2, CHAN, ROWS + 8, HALO), jnp.int16),
        pltpu.VMEM((512, CHANNELS), bf16),
        pltpu.VMEM((RADIX, 16, CHANNELS), bf16),
        pltpu.VMEM((512, CHANNELS), bf16),
        pltpu.VMEM((RADIX, 2, KB, 128), f32),
        pltpu.VMEM((RADIX, 2, KB, 128), f32),
        pltpu.VMEM((RADIX, 2, KB, 256), f32),
        pltpu.VMEM((2, SHARE, 128), f32),
        pltpu.SemaphoreType.DMA((INPUTS,)),
        pltpu.SemaphoreType.DMA((CHAN,)),
        pltpu.SemaphoreType.DMA((CHAN,)),
        pltpu.SemaphoreType.DMA((CHAN,)),
        pltpu.SemaphoreType.DMA((CHAN,)),
        pltpu.SemaphoreType.DMA((2, CHAN)),
        pltpu.SemaphoreType.DMA((2, CHAN)),
        pltpu.SemaphoreType.REGULAR((2,)),
        pltpu.SemaphoreType.DMA((2,)),
    ]

    def kernel(*refs):
        body_kernel(apas, *refs)

    halves_out = pl.pallas_call(
        kernel,
        out_shape=jax.ShapeDtypeStruct(frames.shape, f32),
        in_specs=[pl.BlockSpec(memory_space=pltpu.HBM)] * len(arrays),
        out_specs=pl.BlockSpec(memory_space=pl.ANY),
        scratch_shapes=scratch,
        compiler_params=pltpu.CompilerParams(
            collective_id=0, has_side_effects=True, vmem_limit_bytes=40 * 1024 * 1024
        ),
    )(*[pltpu.with_memory_space_constraint(a, pltpu.HBM) for a in arrays])
    return halves_out


def solution(mesh):
    placed = (
        P("apa", "chan", None),
        P("apa", None),
        P("apa", None),
        P(None, "chan", None),
        P(),
        P(),
        P("apa", "chan", None),
    )
    return jax.shard_map(body, mesh=mesh, in_specs=placed, out_specs=P("apa", "chan", None), check_vma=False)
```

```python
import math

import jax
import jax.numpy as jnp
import numpy as np
from jax import lax
from jax.experimental import pallas as pl
from jax.experimental.pallas import tpu as pltpu
from jax.sharding import PartitionSpec as P

PU = 800
PV = 800
PW = 960
HALO = 128
BC = 16
BT = 64
CHANNELS = 2560
TICKS = 256
FREQS = 128

CHAN = 8
SHARE = CHANNELS // CHAN
PAD = 384
KB = FREQS // CHAN
ROWS = 2 * KB
RADIX = 8
NU = PU // RADIX
PE = PW + 2 * HALO
NW = PE // RADIX
OUTS = SHARE // RADIX
HEAD = 256
TAIL = CHANNELS // RADIX - HEAD

MESH = pl.DeviceIdType.MESH
NT = (((1,), (1,)), ((), ()))
f32 = jnp.float32
bf16 = jnp.bfloat16


def halves(table):
    high = table.astype(bf16)
    low = (table - high.astype(np.float64)).astype(bf16)
    return high, low


def tick_rows():
    row = np.arange(2 * FREQS)
    k = row // ROWS * KB + row % KB
    return k, row % ROWS // KB


def forward_ticks():
    k, z = tick_rows()
    angle = 2.0 * math.pi / TICKS * (k[:, None] * np.arange(TICKS)[None, :] % TICKS)
    return np.where(z[:, None] == 0, np.cos(angle), -np.sin(angle)).astype(bf16)


def inverse_ticks():
    k, z = tick_rows()
    angle = 2.0 * math.pi / TICKS * (k[:, None] * np.arange(TICKS)[None, :] % TICKS)
    weight = np.where(k == 0, 1.0, 2.0)[:, None] / TICKS
    return (np.where(z[:, None] == 0, np.cos(angle), -np.sin(angle)) * weight).astype(np.float32)


def spread_filters():
    k, _ = tick_rows()
    return (np.arange(FREQS)[:, None] == k[None, :]).astype(np.float32)


def dense(length, width, scale=1.0):
    index = np.arange(length)
    angle = 2.0 * math.pi / length * (index[:, None] * index[None, :] % length)
    table = np.zeros((width, 2 * width))
    table[:length, :length] = np.cos(angle) * scale
    table[:length, width : width + length] = np.sin(angle) * scale
    return table


def forward_dense(length, width, places):
    rows = dense(length, width)[np.maximum(places, 0)] * (places[:, None] >= 0)
    high, low = halves(rows)
    return np.concatenate([high, high, low], axis=0)


def lanes_of(lanes, *runs):
    places = np.full(lanes, -1)
    for lane, first, count in runs:
        places[lane : lane + count] = first + np.arange(count)
    return places


def inverse_dense(length, width, period, first, count, lead, rows):
    table = np.zeros((rows, 2 * width))
    table[lead : lead + count] = dense(length, width, 1.0 / period)[first : first + count]
    return np.stack(halves(table))


def twiddles(length, width, period):
    angle = 2.0 * math.pi / period * (np.arange(RADIX)[:, None] * np.arange(length)[None, :])
    table = np.zeros((2, RADIX, 1, width), np.float32)
    table[0, :, 0, :length] = np.cos(angle)
    table[1, :, 0, :length] = np.sin(angle)
    return table


def rim_table():
    lane = np.arange(2 * HALO)
    places = np.where(lane < HALO, lane // RADIX, (PW + HALO) // RADIX + (lane - HALO) // RADIX)
    return forward_dense(NW, 256, places)


def levels_of(largest):
    return jnp.ceil(jnp.log2(jnp.maximum(largest, 1e-30)) * STEPS)


def to_short(value):
    return value.astype(jnp.int32).astype(jnp.int16)


def from_short(value):
    return value.astype(jnp.int32).astype(f32)


def split(value):
    high = value.astype(bf16)
    return high, (value - high.astype(f32)).astype(bf16)


def mul(left, right):
    return jnp.dot(left, right, preferred_element_type=f32)


def mul_nt(left, right):
    return lax.dot_general(left, right, NT, preferred_element_type=f32)


def four(values, sign):
    (ar, ai), (br, bi), (cr, ci), (dr, di) = values
    s0r, s0i, s1r, s1i = ar + cr, ai + ci, ar - cr, ai - ci
    s2r, s2i, s3r, s3i = br + dr, bi + di, br - dr, bi - di
    if sign > 0:
        tr, ti = -s3i, s3r
    else:
        tr, ti = s3i, -s3r
    return [(s0r + s2r, s0i + s2i), (s1r + tr, s1i + ti), (s0r - s2r, s0i - s2i), (s1r - tr, s1i - ti)]


def eight(values, sign):
    even = four(values[0::2], sign)
    odd = four(values[1::2], sign)
    root = math.sqrt(0.5)
    r, i = odd[1]
    odd[1] = ((r - sign * i) * root, (i + sign * r) * root)
    r, i = odd[2]
    odd[2] = (-i, r) if sign > 0 else (i, -r)
    r, i = odd[3]
    odd[3] = ((-r - sign * i) * root, (sign * r - i) * root)
    first = [(a + c, b + d) for (a, b), (c, d) in zip(even, odd)]
    second = [(a - c, b - d) for (a, b), (c, d) in zip(even, odd)]
    return first + second


def channel_product(product, kern, twiddle, width):
    cosine, sine = product
    values = []
    for c in range(RADIX):
        re = slice(c * ROWS, c * ROWS + KB)
        im = slice(c * ROWS + KB, (c + 1) * ROWS)
        yr = cosine[re] + sine[im]
        yi = cosine[im] - sine[re]
        if c > 0:
            tc, ts = twiddle[0, c], twiddle[1, c]
            yr, yi = yr * tc + yi * ts, yi * tc - yr * ts
        values.append((yr, yi))
    values = eight(values, -1)
    values = [
        (r * kern[m, 0] - i * kern[m, 1], r * kern[m, 1] + i * kern[m, 0]) for m, (r, i) in enumerate(values)
    ]
    values = eight(values, 1)
    rows = []
    for c, (r, i) in enumerate(values):
        if c > 0:
            tc, ts = twiddle[0, c], twiddle[1, c]
            r, i = r * tc - i * ts, i * tc + r * ts
        rows.append(jnp.concatenate([r, -i], axis=1))
        rows.append(jnp.concatenate([i, r], axis=1))
    return jnp.concatenate(rows, axis=0)


def inverse_product(table, value):
    high, low = split(value)
    return mul_nt(table[0], high) + mul_nt(table[1], high) + mul_nt(table[0], low)


def message(part):
    level = levels_of(jnp.max(jnp.abs(part), axis=0, keepdims=True))
    scaled = jnp.round(part * (LEVELS * jnp.exp2(-level / STEPS)))
    return to_short(jnp.concatenate([scaled, jnp.broadcast_to(level, (8, part.shape[1]))], axis=0))


def kernel_window(kern, part, start, length, width):
    base = start // 128 * 128
    span = -(-(start - base + length) // 128) * 128
    span = max(span, width)
    piece = kern[part, :, base : base + span]
    if start > base:
        piece = pltpu.roll(piece, span - (start - base), axis=1)
    return piece[:, :width]


INPUTS = 19
LEVELS = 32000.0
STEPS = 8.0


def body_kernel(apas, *refs):
    hbm = refs[:INPUTS]
    out = refs[INPUTS]
    local = refs[INPUTS + 1 : 2 * INPUTS + 1]
    (tx1, rx1, tx2, rx2, txh, rxh, onehot, masks, big, inverse, kern_u, kern_v, kern_w, result) = refs[
        2 * INPUTS + 1 : 2 * INPUTS + 15
    ]
    in_sem, send1, recv1, send2, recv2, sendh, recvh, entered, out_sem = refs[2 * INPUTS + 15 :]
    (frames, ticks, links, near, kern, wide, tight, roi, fwd_u, fwd_w, inv_u, inv_v, inv_w, tw_u, tw_w, rim, back, expand, fwd_v) = local

    me = lax.axis_index("chan")
    apa = lax.axis_index("apa")
    after = apa + 1
    before = apa - 1
    has_after = apa < apas - 1
    has_before = apa > 0
    even = lax.rem(apa, 2) == 0
    wait_after = has_after & (even | (after == apas // 2))
    wait_before = has_before & even & (apa != apas // 2)
    greet_after = has_after & jnp.logical_not(wait_after)
    greet_before = has_before & jnp.logical_not(wait_before)

    loads = [pltpu.make_async_copy(hbm[i], local[i], in_sem.at[i]) for i in range(INPUTS)]
    for load in loads[:4]:
        load.start()
    barrier = pltpu.get_barrier_semaphore()
    for step in range(1, CHAN):
        pl.semaphore_signal(barrier, inc=1, device_id={"chan": lax.rem(me + step, CHAN)}, device_id_type=MESH)
    for load in loads[4:]:
        load.start()

    loads[2].wait()
    loads[3].wait()
    mine = jnp.zeros((1, SHARE), jnp.int32)
    for s in range(CHAN):
        mine = jnp.where(me == s, links[:, s * SHARE : (s + 1) * SHARE], mine)
    mine = jnp.concatenate([mine, jnp.full((1, PAD - SHARE), -8, jnp.int32)], axis=1)
    row = lax.broadcasted_iota(jnp.int32, (2 * HALO, PAD), 0)
    spot = row + jnp.where(row >= HALO, CHANNELS - 2 * HALO, PU + PV)
    local_edge = jnp.where(spot == mine, 1.0, 0.0).astype(bf16)

    loads[0].wait()
    loads[1].wait()
    padded = jnp.concatenate([frames[0], jnp.zeros((PAD - SHARE, TICKS), bf16)], axis=0)
    bands = mul_nt(ticks[...], mul(local_edge, padded).astype(bf16))
    first_band = bands[:, :HALO]
    last_band = bands[:, HALO:]
    lower = jnp.broadcast_to(near[:, 0:1], first_band.shape)
    upper = jnp.broadcast_to(near[:, 1:2], first_band.shape)
    none = jnp.zeros_like(first_band)
    to_after = jnp.where(upper == after, last_band, jnp.where(lower == after, first_band, none))
    to_before = jnp.where(lower == before, first_band, jnp.where(upper == before, last_band, none))
    for way, band in enumerate([to_after, to_before]):
        for dest in range(CHAN):
            txh[way, dest] = message(band[dest * ROWS : (dest + 1) * ROWS])

    spectra = mul_nt(ticks[...], padded)
    level = levels_of(jnp.max(jnp.abs(spectra), axis=1, keepdims=True))
    scaled = jnp.round(spectra * (LEVELS * jnp.exp2(-level / STEPS)))
    lane = lax.broadcasted_iota(jnp.int32, scaled.shape, 1)
    tx1[...] = to_short(jnp.where(lane < SHARE, scaled, level)).reshape(CHAN, ROWS, PAD)

    pl.semaphore_wait(barrier, CHAN - 1 + wait_after.astype(jnp.int32) + wait_before.astype(jnp.int32))

    @pl.when(greet_after)
    def _():
        pl.semaphore_signal(barrier, inc=1, device_id={"apa": after}, device_id_type=MESH)

    @pl.when(greet_before)
    def _():
        pl.semaphore_signal(barrier, inc=1, device_id={"apa": before}, device_id_type=MESH)

    @pl.when(wait_after)
    def _():
        pl.semaphore_signal(entered.at[1], inc=1, device_id={"apa": after}, device_id_type=MESH)

    @pl.when(wait_before)
    def _():
        pl.semaphore_signal(entered.at[0], inc=1, device_id={"apa": before}, device_id_type=MESH)

    def edge_copy(way, dest):
        return pltpu.make_async_remote_copy(
            src_ref=txh.at[way, dest],
            dst_ref=rxh.at[way, me],
            send_sem=sendh.at[way, dest],
            recv_sem=recvh.at[way, me],
            device_id={"apa": after if way == 0 else before, "chan": dest},
            device_id_type=MESH,
        )

    def send_edges(way):
        for step in range(CHAN):
            edge_copy(way, lax.rem(me + step, CHAN)).start()

    @pl.when(wait_after & (after == apas // 2))
    def _():
        send_edges(0)

    def first_copy(step):
        dest = lax.rem(me + step, CHAN)
        return pltpu.make_async_remote_copy(
            src_ref=tx1.at[dest],
            dst_ref=rx1.at[me],
            send_sem=send1.at[dest],
            recv_sem=recv1.at[me],
            device_id={"chan": dest},
            device_id_type=MESH,
        )

    for step in range(1, CHAN):
        first_copy(step).start()
    rx1[me] = tx1[me]

    @pl.when(wait_after & (after != apas // 2))
    def _():
        send_edges(0)

    @pl.when(wait_before)
    def _():
        send_edges(1)

    @pl.when(apa == 0)
    def _():
        rxh[0] = jnp.zeros((CHAN, ROWS + 8, HALO), jnp.int16)

    @pl.when(apa == apas - 1)
    def _():
        rxh[1] = jnp.zeros((CHAN, ROWS + 8, HALO), jnp.int16)

    for part in range(5):
        lanes = slice(part * 512, (part + 1) * 512)
        wire = links[:, lanes]
        group = lax.shift_right_arithmetic(wire, 3)
        rest = lax.bitwise_and(wire, 7)
        other = lax.shift_right_arithmetic(rest, 1) * TAIL + group - HEAD
        other = jnp.where(group >= HEAD, other, -1)
        row = lax.broadcasted_iota(jnp.int32, (256, 512), 0)
        onehot[0:256, lanes] = jnp.where(row == group, 1.0, 0.0).astype(bf16)
        onehot[256:512, lanes] = jnp.where(row == other, 1.0, 0.0).astype(bf16)
        for h in range(RADIX):
            masks[h, :, lanes] = jnp.broadcast_to(jnp.where(rest == h, 1.0, 0.0), (16, 512)).astype(bf16)
        parity = lax.bitwise_and(wire, 1)
        for h in range(2):
            masks[RADIX + h, :, lanes] = jnp.broadcast_to(jnp.where(parity == h, 1.0, 0.0), (16, 512)).astype(bf16)

    loads[4].wait()
    for m in range(RADIX):
        for part in range(2):
            kern_u[m, part] = kernel_window(kern, part, NU * m, NU, 128)
            kern_v[m, part] = kernel_window(kern, part, PU + NU * m, NU, 128)
            kern_w[m, part] = kernel_window(kern, part, PU + PV + NW * m, NW, 256)

    for load in loads[5:]:
        load.wait()
    gains = jnp.concatenate([wide[...], tight[...], jnp.zeros((6, FREQS), f32)], axis=0)
    gains = jnp.dot(gains, expand[0:FREQS], precision=lax.Precision.HIGHEST, preferred_element_type=f32)
    gains = jnp.transpose(gains)
    for column in range(2):
        high, low = split(back[...] * gains[:, column : column + 1])
        lanes = slice(column * TICKS, (column + 1) * TICKS)
        inverse[0:256, lanes] = high
        inverse[256:512, lanes] = high
        inverse[512:768, lanes] = low
    inside = roi[0].astype(f32)
    row_index = lax.broadcasted_iota(jnp.int32, (OUTS, SHARE // BC), 0) // (BC // RADIX)
    col_index = lax.broadcasted_iota(jnp.int32, (OUTS, SHARE // BC), 1)
    pick = jnp.where(row_index == col_index, 1.0, 0.0)
    inside = mul_nt(pick, inside)
    row_index = lax.broadcasted_iota(jnp.int32, (TICKS // BT, TICKS), 0)
    col_index = lax.broadcasted_iota(jnp.int32, (TICKS // BT, TICKS), 1) // BT
    inside = mul(inside, jnp.where(row_index == col_index, 1.0, 0.0))

    @pl.when(greet_after)
    def _():
        pl.semaphore_wait(entered.at[0], 1)
        send_edges(0)

    @pl.when(greet_before & jnp.logical_not(even))
    def _():
        pl.semaphore_wait(entered.at[1], 1)
        send_edges(1)

    for step in range(1, CHAN):
        source = lax.rem(me + step, CHAN)
        pltpu.make_async_remote_copy(
            src_ref=tx1.at[source],
            dst_ref=rx1.at[source],
            send_sem=send1.at[source],
            recv_sem=recv1.at[source],
            device_id={"chan": source},
            device_id_type=MESH,
        ).wait_recv()
    @pl.when(greet_before & even)
    def _():
        pl.semaphore_wait(entered.at[1], 1)
        send_edges(1)

    for pair in range(CHAN // 2):
        lanes = slice(pair * 2 * SHARE, (pair + 1) * 2 * SHARE)
        values = []
        for s in (2 * pair, 2 * pair + 1):
            value = from_short(rx1[s])
            values.append(value[:, :SHARE] * (jnp.exp2(value[:, SHARE : SHARE + 1] / STEPS) / LEVELS))
        high, low = split(jnp.concatenate(values, axis=1))
        for h in range(RADIX + 2):
            mask = jnp.concatenate([masks[h, :, lanes], masks[h, :, lanes]], axis=0)
            first = h * ROWS if h < RADIX else 512 + (h - RADIX) * ROWS
            second = first + (256 if h < RADIX else 2 * ROWS)
            big[first : first + ROWS, lanes] = high * mask
            big[second : second + ROWS, lanes] = low * mask
    placed = [mul_nt(big[0:256], onehot[0:256]), mul_nt(big[256:512], onehot[0:256])]

    def second_copy(dest):
        return pltpu.make_async_remote_copy(
            src_ref=tx2.at[dest],
            dst_ref=rx2.at[me],
            send_sem=send2.at[dest],
            recv_sem=recv2.at[me],
            device_id={"chan": dest},
            device_id_type=MESH,
        )

    def send_on(dests):
        for dest in dests:

            @pl.when(me != dest)
            def _():
                second_copy(dest).start()

            @pl.when(me == dest)
            def _():
                rx2[dest] = tx2[dest]

    def first_stage(lanes, fwd, width):
        high = placed[0][:, lanes].astype(bf16)
        low = placed[1][:, lanes].astype(bf16)
        value = jnp.concatenate([high, low, high], axis=1)
        both = mul(value, fwd[...])
        return both[:, :width], both[:, width:]

    stage_u = first_stage(slice(0, 128), fwd_u, 128)
    stage_v = first_stage(slice(0, 256), fwd_v, 128)
    tail = mul_nt(big[512:640], onehot[256:512])
    part_u = inverse_product(inv_u, channel_product(stage_u, kern_u, tw_u, 128))
    part_v = inverse_product(inv_v, channel_product(stage_v, kern_v, tw_u, 128))
    middle = jnp.concatenate([part_u[80:96], part_u[96:104] + part_v[0:8], part_v[8:24]], axis=0)
    for dest, part in enumerate([part_u[0:40], part_u[40:80], middle, part_v[24:64], part_v[64:104]]):
        tx2[dest] = message(part)
    send_on(range(0, 5))

    ends = []
    for part in range(2):
        for c in range(RADIX):
            pair = c // 2
            first = part * 2 * ROWS + c % 2 * ROWS
            piece = tail[first : first + ROWS, pair // 2 * 128 : (pair // 2 + 1) * 128]
            if pair % 2:
                piece = pltpu.roll(piece, TAIL, axis=1)
            ends.append(piece)
    high = jnp.concatenate([placed[0][:, 128:256], jnp.concatenate(ends[:RADIX], axis=0)], axis=1).astype(bf16)
    low = jnp.concatenate([placed[1][:, 128:256], jnp.concatenate(ends[RADIX:], axis=0)], axis=1).astype(bf16)
    native = mul(jnp.concatenate([high, low, high], axis=1), fwd_w[...])

    def edge_arrivals(way):
        for source in range(CHAN):
            pltpu.make_async_remote_copy(
                src_ref=txh.at[way, source],
                dst_ref=rxh.at[way, source],
                send_sem=sendh.at[way, source],
                recv_sem=recvh.at[way, source],
                device_id={"apa": before if way == 0 else after, "chan": source},
                device_id_type=MESH,
            ).wait_recv()

    @pl.when(has_before)
    def _():
        edge_arrivals(0)

    @pl.when(has_after)
    def _():
        edge_arrivals(1)

    sums = []
    for way in range(2):
        total = jnp.zeros((ROWS, HALO), f32)
        for source in range(CHAN):
            value = from_short(rxh[way, source])
            total = total + value[:ROWS] * (jnp.exp2(value[ROWS : ROWS + 1] / STEPS) / LEVELS)
        sums.append(total)
    from_before, from_after = sums
    lower = lower[:ROWS]
    upper = upper[:ROWS]
    blank = jnp.zeros_like(from_before)
    rim_low = jnp.where(lower == before, from_before, jnp.where(lower == after, from_after, blank))
    rim_up = jnp.where(upper == after, from_after, jnp.where(upper == before, from_before, blank))
    rims = jnp.concatenate([rim_low, rim_up], axis=1)
    lane = lax.bitwise_and(lax.broadcasted_iota(jnp.int32, (ROWS, 2 * HALO), 1), RADIX - 1)
    spread = [
        jnp.concatenate([jnp.where(lane == h, part.astype(f32), 0.0) for h in range(RADIX)], axis=0).astype(bf16)
        for part in split(rims)
    ]
    added = mul(jnp.concatenate([spread[0], spread[1], spread[0]], axis=1), rim[...])
    product = native[:, :256] + added[:, :256], native[:, 256:] + added[:, 256:]
    part_w = inverse_product(inv_w, channel_product(product, kern_w, tw_w, 256))
    for dest in range(3):
        tx2[5 + dest] = message(part_w[dest * OUTS : (dest + 1) * OUTS])
    send_on(range(5, 8))

    for step in range(1, CHAN):
        source = lax.rem(me + step, CHAN)
        pltpu.make_async_remote_copy(
            src_ref=tx2.at[source],
            dst_ref=rx2.at[source],
            send_sem=send2.at[source],
            recv_sem=recv2.at[source],
            device_id={"chan": source},
            device_id_type=MESH,
        ).wait_recv()

    block = lax.broadcasted_iota(jnp.int32, (OUTS, 128), 1) // ROWS
    columns = []
    pieces = []
    for s in range(CHAN):
        value = from_short(rx2[s])
        pieces.append(value[:OUTS] * (jnp.exp2(value[OUTS : OUTS + 1] / STEPS) / LEVELS))
    for side in range(2):
        for c in range(RADIX):
            acc = None
            for q in range(4):
                piece = pieces[4 * side + q][:, c // 4 * 128 : (c // 4 + 1) * 128]
                turn = (q - c % 4) % 4 * ROWS
                if turn:
                    piece = pltpu.roll(piece, turn, axis=1)
                acc = piece if acc is None else jnp.where(block == q, piece, acc)
            columns.append(acc)
    gathered = jnp.concatenate(
        [jnp.concatenate(columns[:RADIX], axis=0), jnp.concatenate(columns[RADIX:], axis=0)], axis=1
    )

    high, low = split(gathered)
    signals = mul(jnp.concatenate([high, low, high], axis=1), inverse[...])
    for c in range(RADIX):
        rows = slice(c * OUTS, (c + 1) * OUTS)
        chosen = jnp.where(inside > 0.5, signals[rows, :TICKS], signals[rows, TICKS:])
        for side in range(2):
            result[side, pl.ds(c, OUTS, stride=RADIX), :] = chosen[:, side * 128 : (side + 1) * 128]
    stores = [
        pltpu.make_async_copy(result.at[side], out.at[0, :, pl.ds(side * 128, 128)], out_sem.at[side])
        for side in range(2)
    ]
    for store in stores:
        store.start()
    for store in stores:
        store.wait()

    for step in range(1, CHAN):
        first_copy(step).wait_send()
        second_copy(lax.rem(me + step, CHAN)).wait_send()
    @pl.when(has_after)
    def _():
        for dest in range(CHAN):
            edge_copy(0, dest).wait_send()

    @pl.when(has_before)
    def _():
        for dest in range(CHAN):
            edge_copy(1, dest).wait_send()


def body(frames, links, near, kern, wide, tight, roi):
    apas = lax.axis_size("apa")
    rim = HALO // RADIX
    head = HEAD - 2 * NU
    collection = ((128 - head, rim, head), (128, rim + head, TAIL))
    arrays = [
        frames,
        jnp.asarray(forward_ticks()),
        links,
        near,
        kern,
        wide.reshape(1, FREQS),
        tight.reshape(1, FREQS),
        jnp.swapaxes(roi, 1, 2),
        jnp.asarray(forward_dense(NU, 128, lanes_of(128, (0, 0, NU)))),
        jnp.asarray(forward_dense(NW, 256, lanes_of(256, *collection))),
        jnp.asarray(inverse_dense(NU, 128, PU, 0, NU, 0, 104)),
        jnp.asarray(inverse_dense(NU, 128, PV, 0, NU, 4, 104)),
        jnp.asarray(inverse_dense(NW, 256, PE, HALO // RADIX, PW // RADIX, 0, 120)),
        jnp.asarray(twiddles(NU, 128, PU)),
        jnp.asarray(twiddles(NW, 256, PE)),
        jnp.asarray(rim_table()),
        jnp.asarray(inverse_ticks()),
        jnp.asarray(spread_filters()),
        jnp.asarray(forward_dense(NU, 128, lanes_of(256, (NU, 0, NU)))),
    ]
    scratch = [pltpu.VMEM(a.shape, a.dtype) for a in arrays]
    scratch += [
        pltpu.VMEM((CHAN, ROWS, PAD), jnp.int16),
        pltpu.VMEM((CHAN, ROWS, PAD), jnp.int16),
        pltpu.VMEM((CHAN, OUTS + 8, 256), jnp.int16),
        pltpu.VMEM((CHAN, OUTS + 8, 256), jnp.int16),
        pltpu.VMEM((2, CHAN, ROWS + 8, HALO), jnp.int16),
        pltpu.VMEM((2, CHAN, ROWS + 8, HALO), jnp.int16),
        pltpu.VMEM((512, CHANNELS), bf16),
        pltpu.VMEM((RADIX + 2, 16, CHANNELS), bf16),
        pltpu.VMEM((640, CHANNELS), bf16),
        pltpu.VMEM((768, 2 * TICKS), bf16),
        pltpu.VMEM((RADIX, 2, KB, 128), f32),
        pltpu.VMEM((RADIX, 2, KB, 128), f32),
        pltpu.VMEM((RADIX, 2, KB, 256), f32),
        pltpu.VMEM((2, SHARE, 128), f32),
        pltpu.SemaphoreType.DMA((INPUTS,)),
        pltpu.SemaphoreType.DMA((CHAN,)),
        pltpu.SemaphoreType.DMA((CHAN,)),
        pltpu.SemaphoreType.DMA((CHAN,)),
        pltpu.SemaphoreType.DMA((CHAN,)),
        pltpu.SemaphoreType.DMA((2, CHAN)),
        pltpu.SemaphoreType.DMA((2, CHAN)),
        pltpu.SemaphoreType.REGULAR((2,)),
        pltpu.SemaphoreType.DMA((2,)),
    ]

    def kernel(*refs):
        body_kernel(apas, *refs)

    halves_out = pl.pallas_call(
        kernel,
        out_shape=jax.ShapeDtypeStruct(frames.shape, f32),
        in_specs=[pl.BlockSpec(memory_space=pltpu.HBM)] * len(arrays),
        out_specs=pl.BlockSpec(memory_space=pl.ANY),
        scratch_shapes=scratch,
        compiler_params=pltpu.CompilerParams(
            collective_id=0, has_side_effects=True, vmem_limit_bytes=40 * 1024 * 1024
        ),
    )(*[pltpu.with_memory_space_constraint(a, pltpu.HBM) for a in arrays])
    return halves_out


def solution(mesh):
    placed = (
        P("apa", "chan", None),
        P("apa", None),
        P("apa", None),
        P(None, "chan", None),
        P(),
        P(),
        P("apa", "chan", None),
    )
    return jax.shard_map(body, mesh=mesh, in_specs=placed, out_specs=P("apa", "chan", None), check_vma=False)
```

```python
import math

import jax
import jax.numpy as jnp
import numpy as np
from jax import lax
from jax.experimental import pallas as pl
from jax.experimental.pallas import tpu as pltpu
from jax.sharding import PartitionSpec as P

PU = 800
PV = 800
PW = 960
HALO = 128
BC = 16
BT = 64
CHANNELS = 2560
TICKS = 256
FREQS = 128

CHAN = 8
SHARE = CHANNELS // CHAN
PAD = 384
KB = FREQS // CHAN
ROWS = 2 * KB
RADIX = 8
NU = PU // RADIX
PE = PW + 2 * HALO
NW = PE // RADIX
OUTS = SHARE // RADIX
SIDE = 4
FAR_FIRST = ((1, 2), (1, 3), (1, 1), (0, 2), (0, 3), (0, 1), (1, 0))
HEAD = 256
TAIL = CHANNELS // RADIX - HEAD

MESH = pl.DeviceIdType.MESH
NT = (((1,), (1,)), ((), ()))
f32 = jnp.float32
bf16 = jnp.bfloat16


def halves(table):
    high = table.astype(bf16)
    low = (table - high.astype(np.float64)).astype(bf16)
    return high, low


def tick_rows():
    row = np.arange(2 * FREQS)
    k = row // ROWS * KB + row % KB
    return k, row % ROWS // KB


def forward_ticks():
    k, z = tick_rows()
    angle = 2.0 * math.pi / TICKS * (k[:, None] * np.arange(TICKS)[None, :] % TICKS)
    return np.where(z[:, None] == 0, np.cos(angle), -np.sin(angle)).astype(bf16)


def inverse_ticks():
    k, z = tick_rows()
    angle = 2.0 * math.pi / TICKS * (k[:, None] * np.arange(TICKS)[None, :] % TICKS)
    weight = np.where(k == 0, 1.0, 2.0)[:, None] / TICKS
    return (np.where(z[:, None] == 0, np.cos(angle), -np.sin(angle)) * weight).astype(np.float32)


def spread_filters():
    k, _ = tick_rows()
    return (np.arange(FREQS)[:, None] == k[None, :]).astype(np.float32)


def dense(length, width, scale=1.0):
    index = np.arange(length)
    angle = 2.0 * math.pi / length * (index[:, None] * index[None, :] % length)
    table = np.zeros((width, 2 * width))
    table[:length, :length] = np.cos(angle) * scale
    table[:length, width : width + length] = np.sin(angle) * scale
    return table


def forward_dense(length, width, places):
    rows = dense(length, width)[np.maximum(places, 0)] * (places[:, None] >= 0)
    high, low = halves(rows)
    return np.concatenate([high, high, low], axis=0)


def lanes_of(lanes, *runs):
    places = np.full(lanes, -1)
    for lane, first, count in runs:
        places[lane : lane + count] = first + np.arange(count)
    return places


def inverse_dense(length, width, period, first, count, lead, rows):
    table = np.zeros((rows, 2 * width))
    table[lead : lead + count] = dense(length, width, 1.0 / period)[first : first + count]
    return np.stack(halves(table))


def twiddles(length, width, period):
    angle = 2.0 * math.pi / period * (np.arange(RADIX)[:, None] * np.arange(length)[None, :])
    table = np.zeros((2, RADIX, 1, width), np.float32)
    table[0, :, 0, :length] = np.cos(angle)
    table[1, :, 0, :length] = np.sin(angle)
    return table


def rim_table():
    lane = np.arange(2 * HALO)
    places = np.where(lane < HALO, lane // RADIX, (PW + HALO) // RADIX + (lane - HALO) // RADIX)
    return forward_dense(NW, 256, places)


def levels_of(largest):
    return jnp.ceil(jnp.log2(jnp.maximum(largest, 1e-30)) * STEPS)


def to_short(value):
    return value.astype(jnp.int32).astype(jnp.int16)


def from_short(value):
    return value.astype(jnp.int32).astype(f32)


def split(value):
    high = value.astype(bf16)
    return high, (value - high.astype(f32)).astype(bf16)


def mul(left, right):
    return jnp.dot(left, right, preferred_element_type=f32)


def mul_nt(left, right):
    return lax.dot_general(left, right, NT, preferred_element_type=f32)


def four(values, sign):
    (ar, ai), (br, bi), (cr, ci), (dr, di) = values
    s0r, s0i, s1r, s1i = ar + cr, ai + ci, ar - cr, ai - ci
    s2r, s2i, s3r, s3i = br + dr, bi + di, br - dr, bi - di
    if sign > 0:
        tr, ti = -s3i, s3r
    else:
        tr, ti = s3i, -s3r
    return [(s0r + s2r, s0i + s2i), (s1r + tr, s1i + ti), (s0r - s2r, s0i - s2i), (s1r - tr, s1i - ti)]


def eight(values, sign):
    even = four(values[0::2], sign)
    odd = four(values[1::2], sign)
    root = math.sqrt(0.5)
    r, i = odd[1]
    odd[1] = ((r - sign * i) * root, (i + sign * r) * root)
    r, i = odd[2]
    odd[2] = (-i, r) if sign > 0 else (i, -r)
    r, i = odd[3]
    odd[3] = ((-r - sign * i) * root, (sign * r - i) * root)
    first = [(a + c, b + d) for (a, b), (c, d) in zip(even, odd)]
    second = [(a - c, b - d) for (a, b), (c, d) in zip(even, odd)]
    return first + second


def channel_product(product, kern, twiddle, width):
    cosine, sine = product
    values = []
    for c in range(RADIX):
        re = slice(c * ROWS, c * ROWS + KB)
        im = slice(c * ROWS + KB, (c + 1) * ROWS)
        yr = cosine[re] + sine[im]
        yi = cosine[im] - sine[re]
        if c > 0:
            tc, ts = twiddle[0, c], twiddle[1, c]
            yr, yi = yr * tc + yi * ts, yi * tc - yr * ts
        values.append((yr, yi))
    values = eight(values, -1)
    values = [
        (r * kern[m, 0] - i * kern[m, 1], r * kern[m, 1] + i * kern[m, 0]) for m, (r, i) in enumerate(values)
    ]
    values = eight(values, 1)
    rows = []
    for c, (r, i) in enumerate(values):
        if c > 0:
            tc, ts = twiddle[0, c], twiddle[1, c]
            r, i = r * tc - i * ts, i * tc + r * ts
        rows.append(jnp.concatenate([r, -i], axis=1))
        rows.append(jnp.concatenate([i, r], axis=1))
    return jnp.concatenate(rows, axis=0)


def inverse_product(table, value):
    high, low = split(value)
    return mul_nt(table[0], high) + mul_nt(table[1], high) + mul_nt(table[0], low)


def message(part):
    level = levels_of(jnp.max(jnp.abs(part), axis=0, keepdims=True))
    scaled = jnp.round(part * (LEVELS * jnp.exp2(-level / STEPS)))
    return to_short(jnp.concatenate([scaled, jnp.broadcast_to(level, (8, part.shape[1]))], axis=0))


def kernel_window(kern, part, start, length, width):
    base = start // 128 * 128
    span = -(-(start - base + length) // 128) * 128
    span = max(span, width)
    piece = kern[part, :, base : base + span]
    if start > base:
        piece = pltpu.roll(piece, span - (start - base), axis=1)
    return piece[:, :width]


INPUTS = 19
LEVELS = 32000.0
STEPS = 8.0


def body_kernel(apas, *refs):
    hbm = refs[:INPUTS]
    out = refs[INPUTS]
    local = refs[INPUTS + 1 : 2 * INPUTS + 1]
    (tx1, rx1, tx2, rx2, txh, rxh, onehot, masks, big, inverse, kern_u, kern_v, kern_w, result) = refs[
        2 * INPUTS + 1 : 2 * INPUTS + 15
    ]
    in_sem, send1, recv1, send2, recv2, sendh, recvh, entered, out_sem = refs[2 * INPUTS + 15 :]
    (frames, ticks, links, near, kern, wide, tight, roi, fwd_u, fwd_w, inv_u, inv_v, inv_w, tw_u, tw_w, rim, back, expand, fwd_v) = local

    me = lax.axis_index("chan")
    apa = lax.axis_index("apa")
    after = apa + 1
    before = apa - 1
    has_after = apa < apas - 1
    has_before = apa > 0
    even = lax.rem(apa, 2) == 0
    wait_after = has_after & (even | (after == apas // 2))
    wait_before = has_before & even & (apa != apas // 2)
    greet_after = has_after & jnp.logical_not(wait_after)
    greet_before = has_before & jnp.logical_not(wait_before)

    def partner(step):
        across, along = FAR_FIRST[step - 1]
        return lax.rem(me // SIDE + across, CHAN // SIDE) * SIDE + lax.rem(me % SIDE + along, SIDE)

    loads = [pltpu.make_async_copy(hbm[i], local[i], in_sem.at[i]) for i in range(INPUTS)]
    for load in loads[:4]:
        load.start()
    barrier = pltpu.get_barrier_semaphore()
    for step in range(1, CHAN):
        pl.semaphore_signal(barrier, inc=1, device_id={"chan": lax.rem(me + step, CHAN)}, device_id_type=MESH)
    for load in loads[4:]:
        load.start()

    loads[2].wait()
    loads[3].wait()
    mine = jnp.zeros((1, SHARE), jnp.int32)
    for s in range(CHAN):
        mine = jnp.where(me == s, links[:, s * SHARE : (s + 1) * SHARE], mine)
    mine = jnp.concatenate([mine, jnp.full((1, PAD - SHARE), -8, jnp.int32)], axis=1)
    row = lax.broadcasted_iota(jnp.int32, (2 * HALO, PAD), 0)
    spot = row + jnp.where(row >= HALO, CHANNELS - 2 * HALO, PU + PV)
    local_edge = jnp.where(spot == mine, 1.0, 0.0).astype(bf16)

    loads[0].wait()
    loads[1].wait()
    padded = jnp.concatenate([frames[0], jnp.zeros((PAD - SHARE, TICKS), bf16)], axis=0)
    bands = mul_nt(ticks[...], mul(local_edge, padded).astype(bf16))
    first_band = bands[:, :HALO]
    last_band = bands[:, HALO:]
    lower = jnp.broadcast_to(near[:, 0:1], first_band.shape)
    upper = jnp.broadcast_to(near[:, 1:2], first_band.shape)
    none = jnp.zeros_like(first_band)
    to_after = jnp.where(upper == after, last_band, jnp.where(lower == after, first_band, none))
    to_before = jnp.where(lower == before, first_band, jnp.where(upper == before, last_band, none))
    for way, band in enumerate([to_after, to_before]):
        for dest in range(CHAN):
            txh[way, dest] = message(band[dest * ROWS : (dest + 1) * ROWS])

    spectra = mul_nt(ticks[...], padded)
    level = levels_of(jnp.max(jnp.abs(spectra), axis=1, keepdims=True))
    scaled = jnp.round(spectra * (LEVELS * jnp.exp2(-level / STEPS)))
    lane = lax.broadcasted_iota(jnp.int32, scaled.shape, 1)
    tx1[...] = to_short(jnp.where(lane < SHARE, scaled, level)).reshape(CHAN, ROWS, PAD)

    pl.semaphore_wait(barrier, CHAN - 1 + wait_after.astype(jnp.int32) + wait_before.astype(jnp.int32))

    @pl.when(greet_after)
    def _():
        pl.semaphore_signal(barrier, inc=1, device_id={"apa": after}, device_id_type=MESH)

    @pl.when(greet_before)
    def _():
        pl.semaphore_signal(barrier, inc=1, device_id={"apa": before}, device_id_type=MESH)

    @pl.when(wait_after)
    def _():
        pl.semaphore_signal(entered.at[1], inc=1, device_id={"apa": after}, device_id_type=MESH)

    @pl.when(wait_before)
    def _():
        pl.semaphore_signal(entered.at[0], inc=1, device_id={"apa": before}, device_id_type=MESH)

    def edge_copy(way, dest):
        return pltpu.make_async_remote_copy(
            src_ref=txh.at[way, dest],
            dst_ref=rxh.at[way, me],
            send_sem=sendh.at[way, dest],
            recv_sem=recvh.at[way, me],
            device_id={"apa": after if way == 0 else before, "chan": dest},
            device_id_type=MESH,
        )

    def send_edges(way):
        for step in range(1, CHAN):
            edge_copy(way, partner(step)).start()
        edge_copy(way, me).start()

    @pl.when(wait_after & (after == apas // 2))
    def _():
        send_edges(0)

    def first_copy(step):
        dest = partner(step)
        return pltpu.make_async_remote_copy(
            src_ref=tx1.at[dest],
            dst_ref=rx1.at[me],
            send_sem=send1.at[dest],
            recv_sem=recv1.at[me],
            device_id={"chan": dest},
            device_id_type=MESH,
        )

    for step in range(1, CHAN):
        first_copy(step).start()
    rx1[me] = tx1[me]

    @pl.when(wait_after & (after != apas // 2))
    def _():
        send_edges(0)

    @pl.when(wait_before)
    def _():
        send_edges(1)

    @pl.when(apa == 0)
    def _():
        rxh[0] = jnp.zeros((CHAN, ROWS + 8, HALO), jnp.int16)

    @pl.when(apa == apas - 1)
    def _():
        rxh[1] = jnp.zeros((CHAN, ROWS + 8, HALO), jnp.int16)

    for part in range(5):
        lanes = slice(part * 512, (part + 1) * 512)
        wire = links[:, lanes]
        group = lax.shift_right_arithmetic(wire, 3)
        rest = lax.bitwise_and(wire, 7)
        other = lax.shift_right_arithmetic(rest, 1) * TAIL + group - HEAD
        other = jnp.where(group >= HEAD, other, -1)
        row = lax.broadcasted_iota(jnp.int32, (256, 512), 0)
        onehot[0:256, lanes] = jnp.where(row == group, 1.0, 0.0).astype(bf16)
        onehot[256:512, lanes] = jnp.where(row == other, 1.0, 0.0).astype(bf16)
        for h in range(RADIX):
            masks[h, :, lanes] = jnp.broadcast_to(jnp.where(rest == h, 1.0, 0.0), (16, 512)).astype(bf16)
        parity = lax.bitwise_and(wire, 1)
        for h in range(2):
            masks[RADIX + h, :, lanes] = jnp.broadcast_to(jnp.where(parity == h, 1.0, 0.0), (16, 512)).astype(bf16)

    loads[4].wait()
    for m in range(RADIX):
        for part in range(2):
            kern_u[m, part] = kernel_window(kern, part, NU * m, NU, 128)
            kern_v[m, part] = kernel_window(kern, part, PU + NU * m, NU, 128)
            kern_w[m, part] = kernel_window(kern, part, PU + PV + NW * m, NW, 256)

    for load in loads[5:]:
        load.wait()
    gains = jnp.concatenate([wide[...], tight[...], jnp.zeros((6, FREQS), f32)], axis=0)
    gains = jnp.dot(gains, expand[0:FREQS], precision=lax.Precision.HIGHEST, preferred_element_type=f32)
    gains = jnp.transpose(gains)
    for column in range(2):
        high, low = split(back[...] * gains[:, column : column + 1])
        lanes = slice(column * TICKS, (column + 1) * TICKS)
        inverse[0:256, lanes] = high
        inverse[256:512, lanes] = high
        inverse[512:768, lanes] = low
    inside = roi[0].astype(f32)
    row_index = lax.broadcasted_iota(jnp.int32, (OUTS, SHARE // BC), 0) // (BC // RADIX)
    col_index = lax.broadcasted_iota(jnp.int32, (OUTS, SHARE // BC), 1)
    pick = jnp.where(row_index == col_index, 1.0, 0.0)
    inside = mul_nt(pick, inside)
    row_index = lax.broadcasted_iota(jnp.int32, (TICKS // BT, TICKS), 0)
    col_index = lax.broadcasted_iota(jnp.int32, (TICKS // BT, TICKS), 1) // BT
    inside = mul(inside, jnp.where(row_index == col_index, 1.0, 0.0))

    @pl.when(greet_after)
    def _():
        pl.semaphore_wait(entered.at[0], 1)
        send_edges(0)

    @pl.when(greet_before & jnp.logical_not(even))
    def _():
        pl.semaphore_wait(entered.at[1], 1)
        send_edges(1)

    for step in range(1, CHAN):
        source = lax.rem(me + step, CHAN)
        pltpu.make_async_remote_copy(
            src_ref=tx1.at[source],
            dst_ref=rx1.at[source],
            send_sem=send1.at[source],
            recv_sem=recv1.at[source],
            device_id={"chan": source},
            device_id_type=MESH,
        ).wait_recv()
    @pl.when(greet_before & even)
    def _():
        pl.semaphore_wait(entered.at[1], 1)
        send_edges(1)

    for pair in range(CHAN // 2):
        lanes = slice(pair * 2 * SHARE, (pair + 1) * 2 * SHARE)
        values = []
        for s in (2 * pair, 2 * pair + 1):
            value = from_short(rx1[s])
            values.append(value[:, :SHARE] * (jnp.exp2(value[:, SHARE : SHARE + 1] / STEPS) / LEVELS))
        high, low = split(jnp.concatenate(values, axis=1))
        for h in range(RADIX + 2):
            mask = jnp.concatenate([masks[h, :, lanes], masks[h, :, lanes]], axis=0)
            first = h * ROWS if h < RADIX else 512 + (h - RADIX) * ROWS
            second = first + (256 if h < RADIX else 2 * ROWS)
            big[first : first + ROWS, lanes] = high * mask
            big[second : second + ROWS, lanes] = low * mask
    placed = [mul_nt(big[0:256], onehot[0:256]), mul_nt(big[256:512], onehot[0:256])]

    def second_copy(dest):
        return pltpu.make_async_remote_copy(
            src_ref=tx2.at[dest],
            dst_ref=rx2.at[me],
            send_sem=send2.at[dest],
            recv_sem=recv2.at[me],
            device_id={"chan": dest},
            device_id_type=MESH,
        )

    def send_on(chosen):
        for step in range(1, CHAN):
            dest = partner(step)

            @pl.when(chosen(dest))
            def _():
                second_copy(dest).start()

        @pl.when(chosen(me))
        def _():
            rx2[me] = tx2[me]

    def first_stage(lanes, fwd, width):
        high = placed[0][:, lanes].astype(bf16)
        low = placed[1][:, lanes].astype(bf16)
        value = jnp.concatenate([high, low, high], axis=1)
        both = mul(value, fwd[...])
        return both[:, :width], both[:, width:]

    stage_u = first_stage(slice(0, 128), fwd_u, 128)
    stage_v = first_stage(slice(0, 256), fwd_v, 128)
    tail = mul_nt(big[512:640], onehot[256:512])
    part_u = inverse_product(inv_u, channel_product(stage_u, kern_u, tw_u, 128))
    part_v = inverse_product(inv_v, channel_product(stage_v, kern_v, tw_u, 128))
    middle = jnp.concatenate([part_u[80:96], part_u[96:104] + part_v[0:8], part_v[8:24]], axis=0)
    for dest, part in enumerate([part_u[0:40], part_u[40:80], middle, part_v[24:64], part_v[64:104]]):
        tx2[dest] = message(part)
    send_on(lambda dest: dest < 5)

    ends = []
    for part in range(2):
        for c in range(RADIX):
            pair = c // 2
            first = part * 2 * ROWS + c % 2 * ROWS
            piece = tail[first : first + ROWS, pair // 2 * 128 : (pair // 2 + 1) * 128]
            if pair % 2:
                piece = pltpu.roll(piece, TAIL, axis=1)
            ends.append(piece)
    high = jnp.concatenate([placed[0][:, 128:256], jnp.concatenate(ends[:RADIX], axis=0)], axis=1).astype(bf16)
    low = jnp.concatenate([placed[1][:, 128:256], jnp.concatenate(ends[RADIX:], axis=0)], axis=1).astype(bf16)
    native = mul(jnp.concatenate([high, low, high], axis=1), fwd_w[...])

    def edge_arrivals(way):
        for source in range(CHAN):
            pltpu.make_async_remote_copy(
                src_ref=txh.at[way, source],
                dst_ref=rxh.at[way, source],
                send_sem=sendh.at[way, source],
                recv_sem=recvh.at[way, source],
                device_id={"apa": before if way == 0 else after, "chan": source},
                device_id_type=MESH,
            ).wait_recv()

    @pl.when(has_before)
    def _():
        edge_arrivals(0)

    @pl.when(has_after)
    def _():
        edge_arrivals(1)

    sums = []
    for way in range(2):
        total = jnp.zeros((ROWS, HALO), f32)
        for source in range(CHAN):
            value = from_short(rxh[way, source])
            total = total + value[:ROWS] * (jnp.exp2(value[ROWS : ROWS + 1] / STEPS) / LEVELS)
        sums.append(total)
    from_before, from_after = sums
    lower = lower[:ROWS]
    upper = upper[:ROWS]
    blank = jnp.zeros_like(from_before)
    rim_low = jnp.where(lower == before, from_before, jnp.where(lower == after, from_after, blank))
    rim_up = jnp.where(upper == after, from_after, jnp.where(upper == before, from_before, blank))
    rims = jnp.concatenate([rim_low, rim_up], axis=1)
    lane = lax.bitwise_and(lax.broadcasted_iota(jnp.int32, (ROWS, 2 * HALO), 1), RADIX - 1)
    spread = [
        jnp.concatenate([jnp.where(lane == h, part.astype(f32), 0.0) for h in range(RADIX)], axis=0).astype(bf16)
        for part in split(rims)
    ]
    added = mul(jnp.concatenate([spread[0], spread[1], spread[0]], axis=1), rim[...])
    product = native[:, :256] + added[:, :256], native[:, 256:] + added[:, 256:]
    part_w = inverse_product(inv_w, channel_product(product, kern_w, tw_w, 256))
    for dest in range(3):
        tx2[5 + dest] = message(part_w[dest * OUTS : (dest + 1) * OUTS])
    send_on(lambda dest: dest >= 5)

    for step in range(1, CHAN):
        source = lax.rem(me + step, CHAN)
        pltpu.make_async_remote_copy(
            src_ref=tx2.at[source],
            dst_ref=rx2.at[source],
            send_sem=send2.at[source],
            recv_sem=recv2.at[source],
            device_id={"chan": source},
            device_id_type=MESH,
        ).wait_recv()

    block = lax.broadcasted_iota(jnp.int32, (OUTS, 128), 1) // ROWS
    columns = []
    pieces = []
    for s in range(CHAN):
        value = from_short(rx2[s])
        pieces.append(value[:OUTS] * (jnp.exp2(value[OUTS : OUTS + 1] / STEPS) / LEVELS))
    for side in range(2):
        for c in range(RADIX):
            acc = None
            for q in range(4):
                piece = pieces[4 * side + q][:, c // 4 * 128 : (c // 4 + 1) * 128]
                turn = (q - c % 4) % 4 * ROWS
                if turn:
                    piece = pltpu.roll(piece, turn, axis=1)
                acc = piece if acc is None else jnp.where(block == q, piece, acc)
            columns.append(acc)
    gathered = jnp.concatenate(
        [jnp.concatenate(columns[:RADIX], axis=0), jnp.concatenate(columns[RADIX:], axis=0)], axis=1
    )

    high, low = split(gathered)
    signals = mul(jnp.concatenate([high, low, high], axis=1), inverse[...])
    for c in range(RADIX):
        rows = slice(c * OUTS, (c + 1) * OUTS)
        chosen = jnp.where(inside > 0.5, signals[rows, :TICKS], signals[rows, TICKS:])
        for side in range(2):
            result[side, pl.ds(c, OUTS, stride=RADIX), :] = chosen[:, side * 128 : (side + 1) * 128]
    stores = [
        pltpu.make_async_copy(result.at[side], out.at[0, :, pl.ds(side * 128, 128)], out_sem.at[side])
        for side in range(2)
    ]
    for store in stores:
        store.start()
    for store in stores:
        store.wait()

    for step in range(1, CHAN):
        first_copy(step).wait_send()
        second_copy(lax.rem(me + step, CHAN)).wait_send()
    @pl.when(has_after)
    def _():
        for dest in range(CHAN):
            edge_copy(0, dest).wait_send()

    @pl.when(has_before)
    def _():
        for dest in range(CHAN):
            edge_copy(1, dest).wait_send()


def body(frames, links, near, kern, wide, tight, roi):
    apas = lax.axis_size("apa")
    rim = HALO // RADIX
    head = HEAD - 2 * NU
    collection = ((128 - head, rim, head), (128, rim + head, TAIL))
    arrays = [
        frames,
        jnp.asarray(forward_ticks()),
        links,
        near,
        kern,
        wide.reshape(1, FREQS),
        tight.reshape(1, FREQS),
        jnp.swapaxes(roi, 1, 2),
        jnp.asarray(forward_dense(NU, 128, lanes_of(128, (0, 0, NU)))),
        jnp.asarray(forward_dense(NW, 256, lanes_of(256, *collection))),
        jnp.asarray(inverse_dense(NU, 128, PU, 0, NU, 0, 104)),
        jnp.asarray(inverse_dense(NU, 128, PV, 0, NU, 4, 104)),
        jnp.asarray(inverse_dense(NW, 256, PE, HALO // RADIX, PW // RADIX, 0, 120)),
        jnp.asarray(twiddles(NU, 128, PU)),
        jnp.asarray(twiddles(NW, 256, PE)),
        jnp.asarray(rim_table()),
        jnp.asarray(inverse_ticks()),
        jnp.asarray(spread_filters()),
        jnp.asarray(forward_dense(NU, 128, lanes_of(256, (NU, 0, NU)))),
    ]
    scratch = [pltpu.VMEM(a.shape, a.dtype) for a in arrays]
    scratch += [
        pltpu.VMEM((CHAN, ROWS, PAD), jnp.int16),
        pltpu.VMEM((CHAN, ROWS, PAD), jnp.int16),
        pltpu.VMEM((CHAN, OUTS + 8, 256), jnp.int16),
        pltpu.VMEM((CHAN, OUTS + 8, 256), jnp.int16),
        pltpu.VMEM((2, CHAN, ROWS + 8, HALO), jnp.int16),
        pltpu.VMEM((2, CHAN, ROWS + 8, HALO), jnp.int16),
        pltpu.VMEM((512, CHANNELS), bf16),
        pltpu.VMEM((RADIX + 2, 16, CHANNELS), bf16),
        pltpu.VMEM((640, CHANNELS), bf16),
        pltpu.VMEM((768, 2 * TICKS), bf16),
        pltpu.VMEM((RADIX, 2, KB, 128), f32),
        pltpu.VMEM((RADIX, 2, KB, 128), f32),
        pltpu.VMEM((RADIX, 2, KB, 256), f32),
        pltpu.VMEM((2, SHARE, 128), f32),
        pltpu.SemaphoreType.DMA((INPUTS,)),
        pltpu.SemaphoreType.DMA((CHAN,)),
        pltpu.SemaphoreType.DMA((CHAN,)),
        pltpu.SemaphoreType.DMA((CHAN,)),
        pltpu.SemaphoreType.DMA((CHAN,)),
        pltpu.SemaphoreType.DMA((2, CHAN)),
        pltpu.SemaphoreType.DMA((2, CHAN)),
        pltpu.SemaphoreType.REGULAR((2,)),
        pltpu.SemaphoreType.DMA((2,)),
    ]

    def kernel(*refs):
        body_kernel(apas, *refs)

    halves_out = pl.pallas_call(
        kernel,
        out_shape=jax.ShapeDtypeStruct(frames.shape, f32),
        in_specs=[pl.BlockSpec(memory_space=pltpu.HBM)] * len(arrays),
        out_specs=pl.BlockSpec(memory_space=pl.ANY),
        scratch_shapes=scratch,
        compiler_params=pltpu.CompilerParams(
            collective_id=0, has_side_effects=True, vmem_limit_bytes=40 * 1024 * 1024
        ),
    )(*[pltpu.with_memory_space_constraint(a, pltpu.HBM) for a in arrays])
    return halves_out


def solution(mesh):
    placed = (
        P("apa", "chan", None),
        P("apa", None),
        P("apa", None),
        P(None, "chan", None),
        P(),
        P(),
        P("apa", "chan", None),
    )
    return jax.shard_map(body, mesh=mesh, in_specs=placed, out_specs=P("apa", "chan", None), check_vma=False)
```

```python
import math

import jax
import jax.numpy as jnp
import numpy as np
from jax import lax
from jax.experimental import pallas as pl
from jax.experimental.pallas import tpu as pltpu
from jax.sharding import PartitionSpec as P

PU = 800
PV = 800
PW = 960
HALO = 128
BC = 16
BT = 64
CHANNELS = 2560
TICKS = 256
FREQS = 128

CHAN = 8
SHARE = CHANNELS // CHAN
PAD = 384
KB = FREQS // CHAN
ROWS = 2 * KB
RADIX = 8
NU = PU // RADIX
PE = PW + 2 * HALO
NW = PE // RADIX
OUTS = SHARE // RADIX
SIDE = 4
FAR_FIRST = ((1, 2), (1, 3), (1, 1), (0, 2), (0, 3), (0, 1), (1, 0))
HEAD = 256
TAIL = CHANNELS // RADIX - HEAD

MESH = pl.DeviceIdType.MESH
NT = (((1,), (1,)), ((), ()))
f32 = jnp.float32
bf16 = jnp.bfloat16


def halves(table):
    high = table.astype(bf16)
    low = (table - high.astype(np.float64)).astype(bf16)
    return high, low


def tick_rows():
    row = np.arange(2 * FREQS)
    k = row // ROWS * KB + row % KB
    return k, row % ROWS // KB


def forward_ticks():
    k, z = tick_rows()
    angle = 2.0 * math.pi / TICKS * (k[:, None] * np.arange(TICKS)[None, :] % TICKS)
    return np.where(z[:, None] == 0, np.cos(angle), -np.sin(angle)).astype(bf16)


def inverse_ticks():
    k, z = tick_rows()
    angle = 2.0 * math.pi / TICKS * (k[:, None] * np.arange(TICKS)[None, :] % TICKS)
    weight = np.where(k == 0, 1.0, 2.0)[:, None] / TICKS
    return (np.where(z[:, None] == 0, np.cos(angle), -np.sin(angle)) * weight).astype(np.float32)


def spread_filters():
    k, _ = tick_rows()
    return (np.arange(FREQS)[:, None] == k[None, :]).astype(np.float32)


def dense(length, width, scale=1.0):
    index = np.arange(length)
    angle = 2.0 * math.pi / length * (index[:, None] * index[None, :] % length)
    table = np.zeros((width, 2 * width))
    table[:length, :length] = np.cos(angle) * scale
    table[:length, width : width + length] = np.sin(angle) * scale
    return table


def forward_dense(length, width, places):
    rows = dense(length, width)[np.maximum(places, 0)] * (places[:, None] >= 0)
    high, low = halves(rows)
    return np.concatenate([high, high, low], axis=0)


def lanes_of(lanes, *runs):
    places = np.full(lanes, -1)
    for lane, first, count in runs:
        places[lane : lane + count] = first + np.arange(count)
    return places


def inverse_dense(length, width, period, first, count, lead, rows):
    table = np.zeros((rows, 2 * width))
    table[lead : lead + count] = dense(length, width, 1.0 / period)[first : first + count]
    return np.stack(halves(table))


def twiddles(length, width, period):
    angle = 2.0 * math.pi / period * (np.arange(RADIX)[:, None] * np.arange(length)[None, :])
    table = np.zeros((2, RADIX, 1, width), np.float32)
    table[0, :, 0, :length] = np.cos(angle)
    table[1, :, 0, :length] = np.sin(angle)
    return table


def rim_table():
    lane = np.arange(2 * HALO)
    places = np.where(lane < HALO, lane // RADIX, (PW + HALO) // RADIX + (lane - HALO) // RADIX)
    return forward_dense(NW, 256, places)


def levels_of(largest):
    return jnp.ceil(jnp.log2(jnp.maximum(largest, 1e-30)) * STEPS)


def to_short(value):
    return value.astype(jnp.int32).astype(jnp.int16)


def from_short(value):
    return value.astype(jnp.int32).astype(f32)


def split(value):
    high = value.astype(bf16)
    return high, (value - high.astype(f32)).astype(bf16)


def mul(left, right):
    return jnp.dot(left, right, preferred_element_type=f32)


def mul_nt(left, right):
    return lax.dot_general(left, right, NT, preferred_element_type=f32)


def four(values, sign):
    (ar, ai), (br, bi), (cr, ci), (dr, di) = values
    s0r, s0i, s1r, s1i = ar + cr, ai + ci, ar - cr, ai - ci
    s2r, s2i, s3r, s3i = br + dr, bi + di, br - dr, bi - di
    if sign > 0:
        tr, ti = -s3i, s3r
    else:
        tr, ti = s3i, -s3r
    return [(s0r + s2r, s0i + s2i), (s1r + tr, s1i + ti), (s0r - s2r, s0i - s2i), (s1r - tr, s1i - ti)]


def eight(values, sign):
    even = four(values[0::2], sign)
    odd = four(values[1::2], sign)
    root = math.sqrt(0.5)
    r, i = odd[1]
    odd[1] = ((r - sign * i) * root, (i + sign * r) * root)
    r, i = odd[2]
    odd[2] = (-i, r) if sign > 0 else (i, -r)
    r, i = odd[3]
    odd[3] = ((-r - sign * i) * root, (sign * r - i) * root)
    first = [(a + c, b + d) for (a, b), (c, d) in zip(even, odd)]
    second = [(a - c, b - d) for (a, b), (c, d) in zip(even, odd)]
    return first + second


def channel_product(product, kern, twiddle, width):
    cosine, sine = product
    values = []
    for c in range(RADIX):
        re = slice(c * ROWS, c * ROWS + KB)
        im = slice(c * ROWS + KB, (c + 1) * ROWS)
        yr = cosine[re] + sine[im]
        yi = cosine[im] - sine[re]
        if c > 0:
            tc, ts = twiddle[0, c], twiddle[1, c]
            yr, yi = yr * tc + yi * ts, yi * tc - yr * ts
        values.append((yr, yi))
    values = eight(values, -1)
    values = [
        (r * kern[m, 0] - i * kern[m, 1], r * kern[m, 1] + i * kern[m, 0]) for m, (r, i) in enumerate(values)
    ]
    values = eight(values, 1)
    rows = []
    for c, (r, i) in enumerate(values):
        if c > 0:
            tc, ts = twiddle[0, c], twiddle[1, c]
            r, i = r * tc - i * ts, i * tc + r * ts
        rows.append(jnp.concatenate([r, -i], axis=1))
        rows.append(jnp.concatenate([i, r], axis=1))
    return jnp.concatenate(rows, axis=0)


def inverse_product(table, value):
    high, low = split(value)
    if table.shape[1] == 104:
        return mul_nt(table[0], high) + mul_nt(table[1], high) + mul_nt(table[0], low)
    parts = []
    for rows in (slice(0, 64), slice(64, table.shape[1])):
        first, second = table[0, rows], table[1, rows]
        parts.append(mul_nt(first, high) + mul_nt(second, high) + mul_nt(first, low))
    return jnp.concatenate(parts, axis=0)


def message(part):
    level = levels_of(jnp.max(jnp.abs(part), axis=0, keepdims=True))
    scaled = jnp.round(part * (LEVELS * jnp.exp2(-level / STEPS)))
    return to_short(jnp.concatenate([scaled, jnp.broadcast_to(level, (8, part.shape[1]))], axis=0))


def kernel_window(kern, part, start, length, width):
    base = start // 128 * 128
    span = -(-(start - base + length) // 128) * 128
    span = max(span, width)
    piece = kern[part, :, base : base + span]
    if start > base:
        piece = pltpu.roll(piece, span - (start - base), axis=1)
    return piece[:, :width]


INPUTS = 19
LEVELS = 32000.0
STEPS = 8.0


def body_kernel(apas, *refs):
    hbm = refs[:INPUTS]
    out = refs[INPUTS]
    local = refs[INPUTS + 1 : 2 * INPUTS + 1]
    (tx1, rx1, tx2, rx2, txh, rxh, onehot, masks, big, inverse, kern_u, kern_v, kern_w, result) = refs[
        2 * INPUTS + 1 : 2 * INPUTS + 15
    ]
    in_sem, send1, recv1, send2, recv2, sendh, recvh, entered, out_sem = refs[2 * INPUTS + 15 :]
    (frames, ticks, links, near, kern, wide, tight, roi, fwd_u, fwd_w, inv_u, inv_v, inv_w, tw_u, tw_w, rim, back, expand, fwd_v) = local

    me = lax.axis_index("chan")
    apa = lax.axis_index("apa")
    after = apa + 1
    before = apa - 1
    has_after = apa < apas - 1
    has_before = apa > 0
    even = lax.rem(apa, 2) == 0
    wait_after = has_after & (even | (after == apas // 2))
    wait_before = has_before & even & (apa != apas // 2)
    greet_after = has_after & jnp.logical_not(wait_after)
    greet_before = has_before & jnp.logical_not(wait_before)

    def partner(step):
        across, along = FAR_FIRST[step - 1]
        return lax.rem(me // SIDE + across, CHAN // SIDE) * SIDE + lax.rem(me % SIDE + along, SIDE)

    loads = [pltpu.make_async_copy(hbm[i], local[i], in_sem.at[i]) for i in range(INPUTS)]
    for load in loads[:4]:
        load.start()
    barrier = pltpu.get_barrier_semaphore()
    for step in range(1, CHAN):
        pl.semaphore_signal(barrier, inc=1, device_id={"chan": lax.rem(me + step, CHAN)}, device_id_type=MESH)

    loads[2].wait()
    loads[3].wait()
    mine = jnp.zeros((1, SHARE), jnp.int32)
    for s in range(CHAN):
        mine = jnp.where(me == s, links[:, s * SHARE : (s + 1) * SHARE], mine)
    mine = jnp.concatenate([mine, jnp.full((1, PAD - SHARE), -8, jnp.int32)], axis=1)
    row = lax.broadcasted_iota(jnp.int32, (2 * HALO, PAD), 0)
    spot = row + jnp.where(row >= HALO, CHANNELS - 2 * HALO, PU + PV)
    local_edge = jnp.where(spot == mine, 1.0, 0.0).astype(bf16)

    loads[0].wait()
    loads[1].wait()
    padded = jnp.concatenate([frames[0], jnp.zeros((PAD - SHARE, TICKS), bf16)], axis=0)
    bands = mul_nt(ticks[...], mul(local_edge, padded).astype(bf16))
    first_band = bands[:, :HALO]
    last_band = bands[:, HALO:]
    lower = jnp.broadcast_to(near[:, 0:1], first_band.shape)
    upper = jnp.broadcast_to(near[:, 1:2], first_band.shape)
    none = jnp.zeros_like(first_band)
    to_after = jnp.where(upper == after, last_band, jnp.where(lower == after, first_band, none))
    to_before = jnp.where(lower == before, first_band, jnp.where(upper == before, last_band, none))
    for way, band in enumerate([to_after, to_before]):
        for dest in range(CHAN):
            txh[way, dest] = message(band[dest * ROWS : (dest + 1) * ROWS])

    spectra = mul_nt(ticks[...], padded)
    level = levels_of(jnp.max(jnp.abs(spectra), axis=1, keepdims=True))
    scaled = jnp.round(spectra * (LEVELS * jnp.exp2(-level / STEPS)))
    lane = lax.broadcasted_iota(jnp.int32, scaled.shape, 1)
    tx1[...] = to_short(jnp.where(lane < SHARE, scaled, level)).reshape(CHAN, ROWS, PAD)

    pl.semaphore_wait(barrier, CHAN - 1 + wait_after.astype(jnp.int32) + wait_before.astype(jnp.int32))

    @pl.when(greet_after)
    def _():
        pl.semaphore_signal(barrier, inc=1, device_id={"apa": after}, device_id_type=MESH)

    @pl.when(greet_before)
    def _():
        pl.semaphore_signal(barrier, inc=1, device_id={"apa": before}, device_id_type=MESH)

    @pl.when(wait_after)
    def _():
        pl.semaphore_signal(entered.at[1], inc=1, device_id={"apa": after}, device_id_type=MESH)

    @pl.when(wait_before)
    def _():
        pl.semaphore_signal(entered.at[0], inc=1, device_id={"apa": before}, device_id_type=MESH)

    def edge_copy(way, dest):
        return pltpu.make_async_remote_copy(
            src_ref=txh.at[way, dest],
            dst_ref=rxh.at[way, me],
            send_sem=sendh.at[way, dest],
            recv_sem=recvh.at[way, me],
            device_id={"apa": after if way == 0 else before, "chan": dest},
            device_id_type=MESH,
        )

    def send_edges(way):
        for step in range(1, CHAN):
            edge_copy(way, partner(step)).start()
        edge_copy(way, me).start()

    @pl.when(wait_after & (after == apas // 2))
    def _():
        send_edges(0)

    def first_copy(step):
        dest = partner(step)
        return pltpu.make_async_remote_copy(
            src_ref=tx1.at[dest],
            dst_ref=rx1.at[me],
            send_sem=send1.at[dest],
            recv_sem=recv1.at[me],
            device_id={"chan": dest},
            device_id_type=MESH,
        )

    for step in range(1, CHAN):
        first_copy(step).start()
    for load in loads[4:]:
        load.start()
    rx1[me] = tx1[me]

    @pl.when(wait_after & (after != apas // 2))
    def _():
        send_edges(0)

    @pl.when(wait_before)
    def _():
        send_edges(1)

    @pl.when(apa == 0)
    def _():
        rxh[0] = jnp.zeros((CHAN, ROWS + 8, HALO), jnp.int16)

    @pl.when(apa == apas - 1)
    def _():
        rxh[1] = jnp.zeros((CHAN, ROWS + 8, HALO), jnp.int16)

    for part in range(5):
        lanes = slice(part * 512, (part + 1) * 512)
        wire = links[:, lanes]
        group = lax.shift_right_arithmetic(wire, 3)
        rest = lax.bitwise_and(wire, 7)
        other = lax.shift_right_arithmetic(rest, 1) * TAIL + group - HEAD
        other = jnp.where(group >= HEAD, other, -1)
        row = lax.broadcasted_iota(jnp.int32, (256, 512), 0)
        onehot[0:256, lanes] = jnp.where(row == group, 1.0, 0.0).astype(bf16)
        onehot[256:512, lanes] = jnp.where(row == other, 1.0, 0.0).astype(bf16)
        for h in range(RADIX):
            masks[h, :, lanes] = jnp.broadcast_to(jnp.where(rest == h, 1.0, 0.0), (16, 512)).astype(bf16)
        parity = lax.bitwise_and(wire, 1)
        for h in range(2):
            masks[RADIX + h, :, lanes] = jnp.broadcast_to(jnp.where(parity == h, 1.0, 0.0), (16, 512)).astype(bf16)

    loads[4].wait()
    for m in range(RADIX):
        for part in range(2):
            kern_u[m, part] = kernel_window(kern, part, NU * m, NU, 128)
            kern_v[m, part] = kernel_window(kern, part, PU + NU * m, NU, 128)
            kern_w[m, part] = kernel_window(kern, part, PU + PV + NW * m, NW, 256)

    for load in loads[5:]:
        load.wait()
    gains = jnp.concatenate([wide[...], tight[...], jnp.zeros((6, FREQS), f32)], axis=0)
    gains = jnp.dot(gains, expand[0:FREQS], precision=lax.Precision.HIGHEST, preferred_element_type=f32)
    gains = jnp.transpose(gains)
    for column in range(2):
        high, low = split(back[...] * gains[:, column : column + 1])
        lanes = slice(column * TICKS, (column + 1) * TICKS)
        inverse[0:256, lanes] = high
        inverse[256:512, lanes] = high
        inverse[512:768, lanes] = low
    inside = roi[0].astype(f32)
    row_index = lax.broadcasted_iota(jnp.int32, (OUTS, SHARE // BC), 0) // (BC // RADIX)
    col_index = lax.broadcasted_iota(jnp.int32, (OUTS, SHARE // BC), 1)
    pick = jnp.where(row_index == col_index, 1.0, 0.0)
    inside = mul_nt(pick, inside)
    row_index = lax.broadcasted_iota(jnp.int32, (TICKS // BT, TICKS), 0)
    col_index = lax.broadcasted_iota(jnp.int32, (TICKS // BT, TICKS), 1) // BT
    inside = mul(inside, jnp.where(row_index == col_index, 1.0, 0.0))

    @pl.when(greet_after)
    def _():
        pl.semaphore_wait(entered.at[0], 1)
        send_edges(0)

    @pl.when(greet_before & jnp.logical_not(even))
    def _():
        pl.semaphore_wait(entered.at[1], 1)
        send_edges(1)

    for step in range(1, CHAN):
        source = lax.rem(me + step, CHAN)
        pltpu.make_async_remote_copy(
            src_ref=tx1.at[source],
            dst_ref=rx1.at[source],
            send_sem=send1.at[source],
            recv_sem=recv1.at[source],
            device_id={"chan": source},
            device_id_type=MESH,
        ).wait_recv()
    @pl.when(greet_before & even)
    def _():
        pl.semaphore_wait(entered.at[1], 1)
        send_edges(1)

    for pair in range(CHAN // 2):
        lanes = slice(pair * 2 * SHARE, (pair + 1) * 2 * SHARE)
        values = []
        for s in (2 * pair, 2 * pair + 1):
            value = from_short(rx1[s])
            values.append(value[:, :SHARE] * (jnp.exp2(value[:, SHARE : SHARE + 1] / STEPS) / LEVELS))
        high, low = split(jnp.concatenate(values, axis=1))
        for h in range(RADIX + 2):
            mask = jnp.concatenate([masks[h, :, lanes], masks[h, :, lanes]], axis=0)
            first = h * ROWS if h < RADIX else 512 + (h - RADIX) * ROWS
            second = first + (256 if h < RADIX else 2 * ROWS)
            big[first : first + ROWS, lanes] = high * mask
            big[second : second + ROWS, lanes] = low * mask
    placed = [mul_nt(big[0:256], onehot[0:256]), mul_nt(big[256:512], onehot[0:256])]

    def second_copy(dest):
        return pltpu.make_async_remote_copy(
            src_ref=tx2.at[dest],
            dst_ref=rx2.at[me],
            send_sem=send2.at[dest],
            recv_sem=recv2.at[me],
            device_id={"chan": dest},
            device_id_type=MESH,
        )

    def send_on(chosen):
        for step in range(1, CHAN):
            dest = partner(step)

            @pl.when(chosen(dest))
            def _():
                second_copy(dest).start()

        @pl.when(chosen(me))
        def _():
            rx2[me] = tx2[me]

    def first_stage(lanes, fwd, width):
        high = placed[0][:, lanes].astype(bf16)
        low = placed[1][:, lanes].astype(bf16)
        value = jnp.concatenate([high, low, high], axis=1)
        both = mul(value, fwd[...])
        return both[:, :width], both[:, width:]

    stage_u = first_stage(slice(0, 128), fwd_u, 128)
    stage_v = first_stage(slice(0, 256), fwd_v, 128)
    tail = mul_nt(big[512:640], onehot[256:512])
    part_u = inverse_product(inv_u, channel_product(stage_u, kern_u, tw_u, 128))
    part_v = inverse_product(inv_v, channel_product(stage_v, kern_v, tw_u, 128))
    middle = jnp.concatenate([part_u[80:96], part_u[96:104] + part_v[0:8], part_v[8:24]], axis=0)
    for dest, part in enumerate([part_u[0:40], part_u[40:80], middle, part_v[24:64], part_v[64:104]]):
        tx2[dest] = message(part)
    send_on(lambda dest: dest < 5)

    ends = []
    for part in range(2):
        for c in range(RADIX):
            pair = c // 2
            first = part * 2 * ROWS + c % 2 * ROWS
            piece = tail[first : first + ROWS, pair // 2 * 128 : (pair // 2 + 1) * 128]
            if pair % 2:
                piece = pltpu.roll(piece, TAIL, axis=1)
            ends.append(piece)
    high = jnp.concatenate([placed[0][:, 128:256], jnp.concatenate(ends[:RADIX], axis=0)], axis=1).astype(bf16)
    low = jnp.concatenate([placed[1][:, 128:256], jnp.concatenate(ends[RADIX:], axis=0)], axis=1).astype(bf16)
    operand = jnp.concatenate([high, low, high], axis=1)
    native = jnp.concatenate([mul(operand[:128], fwd_w[...]), mul(operand[128:], fwd_w[...])], axis=0)

    def edge_arrivals(way):
        for source in range(CHAN):
            pltpu.make_async_remote_copy(
                src_ref=txh.at[way, source],
                dst_ref=rxh.at[way, source],
                send_sem=sendh.at[way, source],
                recv_sem=recvh.at[way, source],
                device_id={"apa": before if way == 0 else after, "chan": source},
                device_id_type=MESH,
            ).wait_recv()

    @pl.when(has_before)
    def _():
        edge_arrivals(0)

    @pl.when(has_after)
    def _():
        edge_arrivals(1)

    sums = []
    for way in range(2):
        total = jnp.zeros((ROWS, HALO), f32)
        for source in range(CHAN):
            value = from_short(rxh[way, source])
            total = total + value[:ROWS] * (jnp.exp2(value[ROWS : ROWS + 1] / STEPS) / LEVELS)
        sums.append(total)
    from_before, from_after = sums
    lower = lower[:ROWS]
    upper = upper[:ROWS]
    blank = jnp.zeros_like(from_before)
    rim_low = jnp.where(lower == before, from_before, jnp.where(lower == after, from_after, blank))
    rim_up = jnp.where(upper == after, from_after, jnp.where(upper == before, from_before, blank))
    rims = jnp.concatenate([rim_low, rim_up], axis=1)
    lane = lax.bitwise_and(lax.broadcasted_iota(jnp.int32, (ROWS, 2 * HALO), 1), RADIX - 1)
    spread = [
        jnp.concatenate([jnp.where(lane == h, part.astype(f32), 0.0) for h in range(RADIX)], axis=0).astype(bf16)
        for part in split(rims)
    ]
    operand = jnp.concatenate([spread[0], spread[1], spread[0]], axis=1)
    added = jnp.concatenate([mul(operand[:128], rim[...]), mul(operand[128:], rim[...])], axis=0)
    product = native[:, :256] + added[:, :256], native[:, 256:] + added[:, 256:]
    part_w = inverse_product(inv_w, channel_product(product, kern_w, tw_w, 256))
    for dest in range(3):
        tx2[5 + dest] = message(part_w[dest * OUTS : (dest + 1) * OUTS])
    send_on(lambda dest: dest >= 5)

    for step in range(1, CHAN):
        source = lax.rem(me + step, CHAN)
        pltpu.make_async_remote_copy(
            src_ref=tx2.at[source],
            dst_ref=rx2.at[source],
            send_sem=send2.at[source],
            recv_sem=recv2.at[source],
            device_id={"chan": source},
            device_id_type=MESH,
        ).wait_recv()

    block = lax.broadcasted_iota(jnp.int32, (OUTS, 128), 1) // ROWS
    columns = []
    pieces = []
    for s in range(CHAN):
        value = from_short(rx2[s])
        pieces.append(value[:OUTS] * (jnp.exp2(value[OUTS : OUTS + 1] / STEPS) / LEVELS))
    for side in range(2):
        for c in range(RADIX):
            acc = None
            for q in range(4):
                piece = pieces[4 * side + q][:, c // 4 * 128 : (c // 4 + 1) * 128]
                turn = (q - c % 4) % 4 * ROWS
                if turn:
                    piece = pltpu.roll(piece, turn, axis=1)
                acc = piece if acc is None else jnp.where(block == q, piece, acc)
            columns.append(acc)
    gathered = jnp.concatenate(
        [jnp.concatenate(columns[:RADIX], axis=0), jnp.concatenate(columns[RADIX:], axis=0)], axis=1
    )

    high, low = split(gathered)
    signals = mul(jnp.concatenate([high, low, high], axis=1), inverse[...])
    for c in range(RADIX):
        rows = slice(c * OUTS, (c + 1) * OUTS)
        chosen = jnp.where(inside > 0.5, signals[rows, :TICKS], signals[rows, TICKS:])
        for side in range(2):
            result[side, pl.ds(c, OUTS, stride=RADIX), :] = chosen[:, side * 128 : (side + 1) * 128]
    stores = [
        pltpu.make_async_copy(result.at[side], out.at[0, :, pl.ds(side * 128, 128)], out_sem.at[side])
        for side in range(2)
    ]
    for store in stores:
        store.start()
    for store in stores:
        store.wait()

    for step in range(1, CHAN):
        first_copy(step).wait_send()
        second_copy(lax.rem(me + step, CHAN)).wait_send()
    @pl.when(has_after)
    def _():
        for dest in range(CHAN):
            edge_copy(0, dest).wait_send()

    @pl.when(has_before)
    def _():
        for dest in range(CHAN):
            edge_copy(1, dest).wait_send()


def body(frames, links, near, kern, wide, tight, roi):
    apas = lax.axis_size("apa")
    rim = HALO // RADIX
    head = HEAD - 2 * NU
    collection = ((128 - head, rim, head), (128, rim + head, TAIL))
    arrays = [
        frames,
        jnp.asarray(forward_ticks()),
        links,
        near,
        kern,
        wide.reshape(1, FREQS),
        tight.reshape(1, FREQS),
        jnp.swapaxes(roi, 1, 2),
        jnp.asarray(forward_dense(NU, 128, lanes_of(128, (0, 0, NU)))),
        jnp.asarray(forward_dense(NW, 256, lanes_of(256, *collection))),
        jnp.asarray(inverse_dense(NU, 128, PU, 0, NU, 0, 104)),
        jnp.asarray(inverse_dense(NU, 128, PV, 0, NU, 4, 104)),
        jnp.asarray(inverse_dense(NW, 256, PE, HALO // RADIX, PW // RADIX, 0, 120)),
        jnp.asarray(twiddles(NU, 128, PU)),
        jnp.asarray(twiddles(NW, 256, PE)),
        jnp.asarray(rim_table()),
        jnp.asarray(inverse_ticks()),
        jnp.asarray(spread_filters()),
        jnp.asarray(forward_dense(NU, 128, lanes_of(256, (NU, 0, NU)))),
    ]
    scratch = [pltpu.VMEM(a.shape, a.dtype) for a in arrays]
    scratch += [
        pltpu.VMEM((CHAN, ROWS, PAD), jnp.int16),
        pltpu.VMEM((CHAN, ROWS, PAD), jnp.int16),
        pltpu.VMEM((CHAN, OUTS + 8, 256), jnp.int16),
        pltpu.VMEM((CHAN, OUTS + 8, 256), jnp.int16),
        pltpu.VMEM((2, CHAN, ROWS + 8, HALO), jnp.int16),
        pltpu.VMEM((2, CHAN, ROWS + 8, HALO), jnp.int16),
        pltpu.VMEM((512, CHANNELS), bf16),
        pltpu.VMEM((RADIX + 2, 16, CHANNELS), bf16),
        pltpu.VMEM((640, CHANNELS), bf16),
        pltpu.VMEM((768, 2 * TICKS), bf16),
        pltpu.VMEM((RADIX, 2, KB, 128), f32),
        pltpu.VMEM((RADIX, 2, KB, 128), f32),
        pltpu.VMEM((RADIX, 2, KB, 256), f32),
        pltpu.VMEM((2, SHARE, 128), f32),
        pltpu.SemaphoreType.DMA((INPUTS,)),
        pltpu.SemaphoreType.DMA((CHAN,)),
        pltpu.SemaphoreType.DMA((CHAN,)),
        pltpu.SemaphoreType.DMA((CHAN,)),
        pltpu.SemaphoreType.DMA((CHAN,)),
        pltpu.SemaphoreType.DMA((2, CHAN)),
        pltpu.SemaphoreType.DMA((2, CHAN)),
        pltpu.SemaphoreType.REGULAR((2,)),
        pltpu.SemaphoreType.DMA((2,)),
    ]

    def kernel(*refs):
        body_kernel(apas, *refs)

    halves_out = pl.pallas_call(
        kernel,
        out_shape=jax.ShapeDtypeStruct(frames.shape, f32),
        in_specs=[pl.BlockSpec(memory_space=pltpu.HBM)] * len(arrays),
        out_specs=pl.BlockSpec(memory_space=pl.ANY),
        scratch_shapes=scratch,
        compiler_params=pltpu.CompilerParams(
            collective_id=0, has_side_effects=True, vmem_limit_bytes=40 * 1024 * 1024
        ),
    )(*[pltpu.with_memory_space_constraint(a, pltpu.HBM) for a in arrays])
    return halves_out


def solution(mesh):
    placed = (
        P("apa", "chan", None),
        P("apa", None),
        P("apa", None),
        P(None, "chan", None),
        P(),
        P(),
        P("apa", "chan", None),
    )
    return jax.shard_map(body, mesh=mesh, in_specs=placed, out_specs=P("apa", "chan", None), check_vma=False)
```

```python
import math

import jax
import jax.numpy as jnp
import numpy as np
from jax import lax
from jax.experimental import pallas as pl
from jax.experimental.pallas import tpu as pltpu
from jax.sharding import PartitionSpec as P

PU = 800
PV = 800
PW = 960
HALO = 128
BC = 16
BT = 64
CHANNELS = 2560
TICKS = 256
FREQS = 128

CHAN = 8
SHARE = CHANNELS // CHAN
PAD = 384
KB = FREQS // CHAN
ROWS = 2 * KB
RADIX = 8
NU = PU // RADIX
PE = PW + 2 * HALO
NW = PE // RADIX
OUTS = SHARE // RADIX
SIDE = 4
FAR_FIRST = ((1, 2), (1, 3), (1, 1), (0, 2), (0, 3), (0, 1), (1, 0))
HEAD = 256
TAIL = CHANNELS // RADIX - HEAD

MESH = pl.DeviceIdType.MESH
NT = (((1,), (1,)), ((), ()))
f32 = jnp.float32
bf16 = jnp.bfloat16


def halves(table):
    high = table.astype(bf16)
    low = (table - high.astype(np.float64)).astype(bf16)
    return high, low


def tick_rows():
    row = np.arange(2 * FREQS)
    k = row // ROWS * KB + row % KB
    return k, row % ROWS // KB


def forward_ticks():
    k, z = tick_rows()
    angle = 2.0 * math.pi / TICKS * (k[:, None] * np.arange(TICKS)[None, :] % TICKS)
    return np.where(z[:, None] == 0, np.cos(angle), -np.sin(angle)).astype(bf16)


def inverse_ticks():
    k, z = tick_rows()
    angle = 2.0 * math.pi / TICKS * (k[:, None] * np.arange(TICKS)[None, :] % TICKS)
    weight = np.where(k == 0, 1.0, 2.0)[:, None] / TICKS
    return (np.where(z[:, None] == 0, np.cos(angle), -np.sin(angle)) * weight).astype(np.float32)


def spread_filters():
    k, _ = tick_rows()
    return (np.arange(FREQS)[:, None] == k[None, :]).astype(np.float32)


def dense(length, width, scale=1.0):
    index = np.arange(length)
    angle = 2.0 * math.pi / length * (index[:, None] * index[None, :] % length)
    table = np.zeros((width, 2 * width))
    table[:length, :length] = np.cos(angle) * scale
    table[:length, width : width + length] = np.sin(angle) * scale
    return table


def forward_dense(length, width, places):
    rows = dense(length, width)[np.maximum(places, 0)] * (places[:, None] >= 0)
    high, low = halves(rows)
    return np.concatenate([high, high, low], axis=0)


def lanes_of(lanes, *runs):
    places = np.full(lanes, -1)
    for lane, first, count in runs:
        places[lane : lane + count] = first + np.arange(count)
    return places


def inverse_dense(length, width, period, first, count, lead, rows):
    table = np.zeros((rows, 2 * width))
    table[lead : lead + count] = dense(length, width, 1.0 / period)[first : first + count]
    return np.stack(halves(table))


def twiddles(length, width, period):
    angle = 2.0 * math.pi / period * (np.arange(RADIX)[:, None] * np.arange(length)[None, :])
    table = np.zeros((2, RADIX, 1, width), np.float32)
    table[0, :, 0, :length] = np.cos(angle)
    table[1, :, 0, :length] = np.sin(angle)
    return table


def rim_table():
    lane = np.arange(2 * HALO)
    places = np.where(lane < HALO, lane // RADIX, (PW + HALO) // RADIX + (lane - HALO) // RADIX)
    return forward_dense(NW, 256, places)


def levels_of(largest):
    return jnp.ceil(jnp.log2(jnp.maximum(largest, 1e-30)) * STEPS)


def to_short(value):
    return value.astype(jnp.int32).astype(jnp.int16)


def from_short(value):
    return value.astype(jnp.int32).astype(f32)


def split(value):
    high = value.astype(bf16)
    return high, (value - high.astype(f32)).astype(bf16)


def mul(left, right):
    return jnp.dot(left, right, preferred_element_type=f32)


def mul_nt(left, right):
    return lax.dot_general(left, right, NT, preferred_element_type=f32)


def four(values, sign):
    (ar, ai), (br, bi), (cr, ci), (dr, di) = values
    s0r, s0i, s1r, s1i = ar + cr, ai + ci, ar - cr, ai - ci
    s2r, s2i, s3r, s3i = br + dr, bi + di, br - dr, bi - di
    if sign > 0:
        tr, ti = -s3i, s3r
    else:
        tr, ti = s3i, -s3r
    return [(s0r + s2r, s0i + s2i), (s1r + tr, s1i + ti), (s0r - s2r, s0i - s2i), (s1r - tr, s1i - ti)]


def eight(values, sign):
    even = four(values[0::2], sign)
    odd = four(values[1::2], sign)
    root = math.sqrt(0.5)
    r, i = odd[1]
    odd[1] = ((r - sign * i) * root, (i + sign * r) * root)
    r, i = odd[2]
    odd[2] = (-i, r) if sign > 0 else (i, -r)
    r, i = odd[3]
    odd[3] = ((-r - sign * i) * root, (sign * r - i) * root)
    first = [(a + c, b + d) for (a, b), (c, d) in zip(even, odd)]
    second = [(a - c, b - d) for (a, b), (c, d) in zip(even, odd)]
    return first + second


def channel_product(product, kern, twiddle, width):
    cosine, sine = product
    values = []
    for c in range(RADIX):
        re = slice(c * ROWS, c * ROWS + KB)
        im = slice(c * ROWS + KB, (c + 1) * ROWS)
        yr = cosine[re] + sine[im]
        yi = cosine[im] - sine[re]
        if c > 0:
            tc, ts = twiddle[0, c], twiddle[1, c]
            yr, yi = yr * tc + yi * ts, yi * tc - yr * ts
        values.append((yr, yi))
    values = eight(values, -1)
    values = [
        (r * kern[m, 0] - i * kern[m, 1], r * kern[m, 1] + i * kern[m, 0]) for m, (r, i) in enumerate(values)
    ]
    values = eight(values, 1)
    rows = []
    for c, (r, i) in enumerate(values):
        if c > 0:
            tc, ts = twiddle[0, c], twiddle[1, c]
            r, i = r * tc - i * ts, i * tc + r * ts
        rows.append(jnp.concatenate([r, -i], axis=1))
        rows.append(jnp.concatenate([i, r], axis=1))
    return jnp.concatenate(rows, axis=0)


def inverse_product(table, value):
    high, low = split(value)
    if table.shape[1] == 104:
        return mul_nt(table[0], high) + mul_nt(table[1], high) + mul_nt(table[0], low)
    parts = []
    for rows in (slice(0, 64), slice(64, table.shape[1])):
        first, second = table[0, rows], table[1, rows]
        parts.append(mul_nt(first, high) + mul_nt(second, high) + mul_nt(first, low))
    return jnp.concatenate(parts, axis=0)


def message(part):
    level = levels_of(jnp.max(jnp.abs(part), axis=0, keepdims=True))
    scaled = jnp.round(part * (LEVELS * jnp.exp2(-level / STEPS)))
    return to_short(jnp.concatenate([scaled, jnp.broadcast_to(level, (8, part.shape[1]))], axis=0))


def kernel_window(kern, part, start, length, width):
    base = start // 128 * 128
    span = -(-(start - base + length) // 128) * 128
    span = max(span, width)
    piece = kern[part, :, base : base + span]
    if start > base:
        piece = pltpu.roll(piece, span - (start - base), axis=1)
    return piece[:, :width]


INPUTS = 19
LEVELS = 32000.0
STEPS = 8.0


def body_kernel(apas, *refs):
    hbm = refs[:INPUTS]
    out = refs[INPUTS]
    local = refs[INPUTS + 1 : 2 * INPUTS + 1]
    (tx1, rx1, tx2, rx2, txh, rxh, onehot, masks, big, inverse, kern_u, kern_v, kern_w, result) = refs[
        2 * INPUTS + 1 : 2 * INPUTS + 15
    ]
    in_sem, send1, recv1, send2, recv2, sendh, recvh, entered, out_sem = refs[2 * INPUTS + 15 :]
    (frames, ticks, links, near, kern, wide, tight, roi, fwd_u, fwd_w, inv_u, inv_v, inv_w, tw_u, tw_w, rim, back, expand, fwd_v) = local

    me = lax.axis_index("chan")
    apa = lax.axis_index("apa")
    after = apa + 1
    before = apa - 1
    has_after = apa < apas - 1
    has_before = apa > 0
    even = lax.rem(apa, 2) == 0
    wait_after = has_after & (even | (after == apas // 2))
    wait_before = has_before & even & (apa != apas // 2)
    greet_after = has_after & jnp.logical_not(wait_after)
    greet_before = has_before & jnp.logical_not(wait_before)

    def partner(step):
        across, along = FAR_FIRST[step - 1]
        return lax.rem(me // SIDE + across, CHAN // SIDE) * SIDE + lax.rem(me % SIDE + along, SIDE)

    loads = [pltpu.make_async_copy(hbm[i], local[i], in_sem.at[i]) for i in range(INPUTS)]
    for load in loads[:4]:
        load.start()
    barrier = pltpu.get_barrier_semaphore()
    for step in range(1, CHAN):
        pl.semaphore_signal(barrier, inc=1, device_id={"chan": lax.rem(me + step, CHAN)}, device_id_type=MESH)

    loads[2].wait()
    loads[3].wait()
    mine = jnp.zeros((1, SHARE), jnp.int32)
    for s in range(CHAN):
        mine = jnp.where(me == s, links[:, s * SHARE : (s + 1) * SHARE], mine)
    mine = jnp.concatenate([mine, jnp.full((1, PAD - SHARE), -8, jnp.int32)], axis=1)
    row = lax.broadcasted_iota(jnp.int32, (2 * HALO, PAD), 0)
    spot = row + jnp.where(row >= HALO, CHANNELS - 2 * HALO, PU + PV)
    local_edge = jnp.where(spot == mine, 1.0, 0.0).astype(bf16)

    loads[0].wait()
    loads[1].wait()
    padded = jnp.concatenate([frames[0], jnp.zeros((PAD - SHARE, TICKS), bf16)], axis=0)
    bands = mul_nt(ticks[...], mul(local_edge, padded).astype(bf16))
    first_band = bands[:, :HALO]
    last_band = bands[:, HALO:]
    lower = jnp.broadcast_to(near[:, 0:1], first_band.shape)
    upper = jnp.broadcast_to(near[:, 1:2], first_band.shape)
    none = jnp.zeros_like(first_band)
    to_after = jnp.where(upper == after, last_band, jnp.where(lower == after, first_band, none))
    to_before = jnp.where(lower == before, first_band, jnp.where(upper == before, last_band, none))
    for way, band in enumerate([to_after, to_before]):
        for dest in range(CHAN):
            txh[way, dest] = message(band[dest * ROWS : (dest + 1) * ROWS])

    spectra = mul_nt(ticks[...], padded)
    level = levels_of(jnp.max(jnp.abs(spectra), axis=1, keepdims=True))
    scaled = jnp.round(spectra * (LEVELS * jnp.exp2(-level / STEPS)))
    lane = lax.broadcasted_iota(jnp.int32, scaled.shape, 1)
    tx1[...] = to_short(jnp.where(lane < SHARE, scaled, level)).reshape(CHAN, ROWS, PAD)

    pl.semaphore_wait(barrier, CHAN - 1 + wait_after.astype(jnp.int32) + wait_before.astype(jnp.int32))

    @pl.when(greet_after)
    def _():
        pl.semaphore_signal(barrier, inc=1, device_id={"apa": after}, device_id_type=MESH)

    @pl.when(greet_before)
    def _():
        pl.semaphore_signal(barrier, inc=1, device_id={"apa": before}, device_id_type=MESH)

    @pl.when(wait_after)
    def _():
        pl.semaphore_signal(entered.at[1], inc=1, device_id={"apa": after}, device_id_type=MESH)

    @pl.when(wait_before)
    def _():
        pl.semaphore_signal(entered.at[0], inc=1, device_id={"apa": before}, device_id_type=MESH)

    def edge_copy(way, dest):
        return pltpu.make_async_remote_copy(
            src_ref=txh.at[way, dest],
            dst_ref=rxh.at[way, me],
            send_sem=sendh.at[way, dest],
            recv_sem=recvh.at[way, me],
            device_id={"apa": after if way == 0 else before, "chan": dest},
            device_id_type=MESH,
        )

    def send_edges(way):
        for step in range(1, CHAN):
            edge_copy(way, partner(step)).start()
        edge_copy(way, me).start()

    @pl.when(wait_after & (after == apas // 2))
    def _():
        send_edges(0)

    def first_copy(step):
        dest = partner(step)
        return pltpu.make_async_remote_copy(
            src_ref=tx1.at[dest],
            dst_ref=rx1.at[me],
            send_sem=send1.at[dest],
            recv_sem=recv1.at[me],
            device_id={"chan": dest},
            device_id_type=MESH,
        )

    for step in range(1, CHAN):
        first_copy(step).start()
    for load in loads[4:]:
        load.start()
    rx1[me] = tx1[me]

    @pl.when(wait_after & (after != apas // 2))
    def _():
        send_edges(0)

    @pl.when(wait_before)
    def _():
        send_edges(1)

    @pl.when(apa == 0)
    def _():
        rxh[0] = jnp.zeros((CHAN, ROWS + 8, HALO), jnp.int16)

    @pl.when(apa == apas - 1)
    def _():
        rxh[1] = jnp.zeros((CHAN, ROWS + 8, HALO), jnp.int16)

    for part in range(5):
        lanes = slice(part * 512, (part + 1) * 512)
        wire = links[:, lanes]
        group = lax.shift_right_arithmetic(wire, 3)
        rest = lax.bitwise_and(wire, 7)
        other = lax.shift_right_arithmetic(rest, 1) * TAIL + group - HEAD
        other = jnp.where(group >= HEAD, other, -1)
        row = lax.broadcasted_iota(jnp.int32, (256, 512), 0)
        onehot[0:256, lanes] = jnp.where(row == group, 1.0, 0.0).astype(bf16)
        onehot[256:512, lanes] = jnp.where(row == other, 1.0, 0.0).astype(bf16)
        for h in range(RADIX):
            masks[h, :, lanes] = jnp.broadcast_to(jnp.where(rest == h, 1.0, 0.0), (16, 512)).astype(bf16)
        parity = lax.bitwise_and(wire, 1)
        for h in range(2):
            masks[RADIX + h, :, lanes] = jnp.broadcast_to(jnp.where(parity == h, 1.0, 0.0), (16, 512)).astype(bf16)

    loads[4].wait()
    for m in range(RADIX):
        for part in range(2):
            kern_u[m, part] = kernel_window(kern, part, NU * m, NU, 128)
            kern_v[m, part] = kernel_window(kern, part, PU + NU * m, NU, 128)
            kern_w[m, part] = kernel_window(kern, part, PU + PV + NW * m, NW, 256)

    for load in loads[5:]:
        load.wait()
    gains = jnp.concatenate([wide[...], tight[...], jnp.zeros((6, FREQS), f32)], axis=0)
    gains = jnp.dot(gains, expand[0:FREQS], precision=lax.Precision.HIGHEST, preferred_element_type=f32)
    gains = jnp.transpose(gains)
    for column in range(2):
        high, low = split(back[...] * gains[:, column : column + 1])
        lanes = slice(column * TICKS, (column + 1) * TICKS)
        inverse[0:256, lanes] = high
        inverse[256:512, lanes] = high
        inverse[512:768, lanes] = low
    inside = roi[0].astype(f32)
    row_index = lax.broadcasted_iota(jnp.int32, (OUTS, SHARE // BC), 0) // (BC // RADIX)
    col_index = lax.broadcasted_iota(jnp.int32, (OUTS, SHARE // BC), 1)
    pick = jnp.where(row_index == col_index, 1.0, 0.0)
    inside = mul_nt(pick, inside)
    row_index = lax.broadcasted_iota(jnp.int32, (TICKS // BT, TICKS), 0)
    col_index = lax.broadcasted_iota(jnp.int32, (TICKS // BT, TICKS), 1) // BT
    inside = mul(inside, jnp.where(row_index == col_index, 1.0, 0.0))

    @pl.when(greet_after)
    def _():
        pl.semaphore_wait(entered.at[0], 1)
        send_edges(0)

    @pl.when(greet_before & jnp.logical_not(even))
    def _():
        pl.semaphore_wait(entered.at[1], 1)
        send_edges(1)

    for step in range(1, CHAN):
        source = lax.rem(me + step, CHAN)
        pltpu.make_async_remote_copy(
            src_ref=tx1.at[source],
            dst_ref=rx1.at[source],
            send_sem=send1.at[source],
            recv_sem=recv1.at[source],
            device_id={"chan": source},
            device_id_type=MESH,
        ).wait_recv()
    @pl.when(greet_before & even)
    def _():
        pl.semaphore_wait(entered.at[1], 1)
        send_edges(1)

    for pair in range(CHAN // 2):
        lanes = slice(pair * 2 * SHARE, (pair + 1) * 2 * SHARE)
        values = []
        for s in (2 * pair, 2 * pair + 1):
            value = from_short(rx1[s])
            values.append(value[:, :SHARE] * (jnp.exp2(value[:, SHARE : SHARE + 1] / STEPS) / LEVELS))
        high, low = split(jnp.concatenate(values, axis=1))
        for h in range(RADIX + 2):
            mask = jnp.concatenate([masks[h, :, lanes], masks[h, :, lanes]], axis=0)
            first = h * ROWS if h < RADIX else 512 + (h - RADIX) * ROWS
            second = first + (256 if h < RADIX else 2 * ROWS)
            big[first : first + ROWS, lanes] = high * mask
            big[second : second + ROWS, lanes] = low * mask
    placed = [mul_nt(big[0:256], onehot[0:256]), mul_nt(big[256:512], onehot[0:256])]

    def second_copy(dest):
        return pltpu.make_async_remote_copy(
            src_ref=tx2.at[dest],
            dst_ref=rx2.at[me],
            send_sem=send2.at[dest],
            recv_sem=recv2.at[me],
            device_id={"chan": dest},
            device_id_type=MESH,
        )

    def send_on(chosen):
        for step in range(1, CHAN):
            dest = partner(step)

            @pl.when(chosen(dest))
            def _():
                second_copy(dest).start()

        @pl.when(chosen(me))
        def _():
            rx2[me] = tx2[me]

    def first_stage(lanes, fwd, width):
        high = placed[0][:, lanes].astype(bf16)
        low = placed[1][:, lanes].astype(bf16)
        value = jnp.concatenate([high, low, high], axis=1)
        both = mul(value, fwd[...])
        return both[:, :width], both[:, width:]

    stage_u = first_stage(slice(0, 128), fwd_u, 128)
    stage_v = first_stage(slice(0, 256), fwd_v, 128)
    tail = mul_nt(big[512:640], onehot[256:512])
    part_u = inverse_product(inv_u, channel_product(stage_u, kern_u, tw_u, 128))
    part_v = inverse_product(inv_v, channel_product(stage_v, kern_v, tw_u, 128))
    middle = jnp.concatenate([part_u[80:96], part_u[96:104] + part_v[0:8], part_v[8:24]], axis=0)
    for dest, part in enumerate([part_u[0:40], part_u[40:80], middle, part_v[24:64], part_v[64:104]]):
        tx2[dest] = message(part)
    send_on(lambda dest: dest < 5)

    ends = []
    for part in range(2):
        for c in range(RADIX):
            pair = c // 2
            first = part * 2 * ROWS + c % 2 * ROWS
            piece = tail[first : first + ROWS, pair // 2 * 128 : (pair // 2 + 1) * 128]
            if pair % 2:
                piece = pltpu.roll(piece, TAIL, axis=1)
            ends.append(piece)
    high = jnp.concatenate([placed[0][:, 128:256], jnp.concatenate(ends[:RADIX], axis=0)], axis=1).astype(bf16)
    low = jnp.concatenate([placed[1][:, 128:256], jnp.concatenate(ends[RADIX:], axis=0)], axis=1).astype(bf16)
    operand = jnp.concatenate([high, low, high], axis=1)
    native = jnp.concatenate([mul(operand[:128], fwd_w[...]), mul(operand[128:], fwd_w[...])], axis=0)

    def edge_arrivals(way):
        for source in range(CHAN):
            pltpu.make_async_remote_copy(
                src_ref=txh.at[way, source],
                dst_ref=rxh.at[way, source],
                send_sem=sendh.at[way, source],
                recv_sem=recvh.at[way, source],
                device_id={"apa": before if way == 0 else after, "chan": source},
                device_id_type=MESH,
            ).wait_recv()

    @pl.when(has_before)
    def _():
        edge_arrivals(0)

    @pl.when(has_after)
    def _():
        edge_arrivals(1)

    sums = []
    for way in range(2):
        total = jnp.zeros((ROWS, HALO), f32)
        for source in range(CHAN):
            value = from_short(rxh[way, source])
            total = total + value[:ROWS] * (jnp.exp2(value[ROWS : ROWS + 1] / STEPS) / LEVELS)
        sums.append(total)
    from_before, from_after = sums
    lower = lower[:ROWS]
    upper = upper[:ROWS]
    blank = jnp.zeros_like(from_before)
    rim_low = jnp.where(lower == before, from_before, jnp.where(lower == after, from_after, blank))
    rim_up = jnp.where(upper == after, from_after, jnp.where(upper == before, from_before, blank))
    rims = jnp.concatenate([rim_low, rim_up], axis=1)
    lane = lax.bitwise_and(lax.broadcasted_iota(jnp.int32, (ROWS, 2 * HALO), 1), RADIX - 1)
    spread = [
        jnp.concatenate([jnp.where(lane == h, part.astype(f32), 0.0) for h in range(RADIX)], axis=0).astype(bf16)
        for part in split(rims)
    ]
    operand = jnp.concatenate([spread[0], spread[1], spread[0]], axis=1)
    added = jnp.concatenate([mul(operand[:128], rim[...]), mul(operand[128:], rim[...])], axis=0)
    product = native[:, :256] + added[:, :256], native[:, 256:] + added[:, 256:]
    part_w = inverse_product(inv_w, channel_product(product, kern_w, tw_w, 256))
    for dest in range(3):
        tx2[5 + dest] = message(part_w[dest * OUTS : (dest + 1) * OUTS])
    send_on(lambda dest: dest >= 5)

    for step in range(1, CHAN):
        source = lax.rem(me + step, CHAN)
        pltpu.make_async_remote_copy(
            src_ref=tx2.at[source],
            dst_ref=rx2.at[source],
            send_sem=send2.at[source],
            recv_sem=recv2.at[source],
            device_id={"chan": source},
            device_id_type=MESH,
        ).wait_recv()

    block = lax.broadcasted_iota(jnp.int32, (OUTS, 128), 1) // ROWS
    columns = []
    pieces = []
    for s in range(CHAN):
        value = from_short(rx2[s])
        pieces.append(value[:OUTS] * (jnp.exp2(value[OUTS : OUTS + 1] / STEPS) / LEVELS))
    for side in range(2):
        for c in range(RADIX):
            acc = None
            for q in range(4):
                piece = pieces[4 * side + q][:, c // 4 * 128 : (c // 4 + 1) * 128]
                turn = (q - c % 4) % 4 * ROWS
                if turn:
                    piece = pltpu.roll(piece, turn, axis=1)
                acc = piece if acc is None else jnp.where(block == q, piece, acc)
            columns.append(acc)
    gathered = jnp.concatenate(
        [jnp.concatenate(columns[:RADIX], axis=0), jnp.concatenate(columns[RADIX:], axis=0)], axis=1
    )

    high, low = split(gathered)
    signals = mul(jnp.concatenate([high, low, high], axis=1), inverse[...])
    for c in range(RADIX):
        rows = slice(c * OUTS, (c + 1) * OUTS)
        chosen = jnp.where(inside > 0.5, signals[rows, :TICKS], signals[rows, TICKS:])
        for side in range(2):
            result[side, pl.ds(c, OUTS, stride=RADIX), :] = chosen[:, side * 128 : (side + 1) * 128]
    stores = [
        pltpu.make_async_copy(result.at[side], out.at[0, :, pl.ds(side * 128, 128)], out_sem.at[side])
        for side in range(2)
    ]
    for store in stores:
        store.start()

    for step in range(1, CHAN):
        first_copy(step).wait_send()
        second_copy(lax.rem(me + step, CHAN)).wait_send()
    @pl.when(has_after)
    def _():
        for dest in range(CHAN):
            edge_copy(0, dest).wait_send()

    @pl.when(has_before)
    def _():
        for dest in range(CHAN):
            edge_copy(1, dest).wait_send()

    for store in stores:
        store.wait()


def body(frames, links, near, kern, wide, tight, roi):
    apas = lax.axis_size("apa")
    rim = HALO // RADIX
    head = HEAD - 2 * NU
    collection = ((128 - head, rim, head), (128, rim + head, TAIL))
    arrays = [
        frames,
        jnp.asarray(forward_ticks()),
        links,
        near,
        kern,
        wide.reshape(1, FREQS),
        tight.reshape(1, FREQS),
        jnp.swapaxes(roi, 1, 2),
        jnp.asarray(forward_dense(NU, 128, lanes_of(128, (0, 0, NU)))),
        jnp.asarray(forward_dense(NW, 256, lanes_of(256, *collection))),
        jnp.asarray(inverse_dense(NU, 128, PU, 0, NU, 0, 104)),
        jnp.asarray(inverse_dense(NU, 128, PV, 0, NU, 4, 104)),
        jnp.asarray(inverse_dense(NW, 256, PE, HALO // RADIX, PW // RADIX, 0, 120)),
        jnp.asarray(twiddles(NU, 128, PU)),
        jnp.asarray(twiddles(NW, 256, PE)),
        jnp.asarray(rim_table()),
        jnp.asarray(inverse_ticks()),
        jnp.asarray(spread_filters()),
        jnp.asarray(forward_dense(NU, 128, lanes_of(256, (NU, 0, NU)))),
    ]
    scratch = [pltpu.VMEM(a.shape, a.dtype) for a in arrays]
    scratch += [
        pltpu.VMEM((CHAN, ROWS, PAD), jnp.int16),
        pltpu.VMEM((CHAN, ROWS, PAD), jnp.int16),
        pltpu.VMEM((CHAN, OUTS + 8, 256), jnp.int16),
        pltpu.VMEM((CHAN, OUTS + 8, 256), jnp.int16),
        pltpu.VMEM((2, CHAN, ROWS + 8, HALO), jnp.int16),
        pltpu.VMEM((2, CHAN, ROWS + 8, HALO), jnp.int16),
        pltpu.VMEM((512, CHANNELS), bf16),
        pltpu.VMEM((RADIX + 2, 16, CHANNELS), bf16),
        pltpu.VMEM((640, CHANNELS), bf16),
        pltpu.VMEM((768, 2 * TICKS), bf16),
        pltpu.VMEM((RADIX, 2, KB, 128), f32),
        pltpu.VMEM((RADIX, 2, KB, 128), f32),
        pltpu.VMEM((RADIX, 2, KB, 256), f32),
        pltpu.VMEM((2, SHARE, 128), f32),
        pltpu.SemaphoreType.DMA((INPUTS,)),
        pltpu.SemaphoreType.DMA((CHAN,)),
        pltpu.SemaphoreType.DMA((CHAN,)),
        pltpu.SemaphoreType.DMA((CHAN,)),
        pltpu.SemaphoreType.DMA((CHAN,)),
        pltpu.SemaphoreType.DMA((2, CHAN)),
        pltpu.SemaphoreType.DMA((2, CHAN)),
        pltpu.SemaphoreType.REGULAR((2,)),
        pltpu.SemaphoreType.DMA((2,)),
    ]

    def kernel(*refs):
        body_kernel(apas, *refs)

    halves_out = pl.pallas_call(
        kernel,
        out_shape=jax.ShapeDtypeStruct(frames.shape, f32),
        in_specs=[pl.BlockSpec(memory_space=pltpu.HBM)] * len(arrays),
        out_specs=pl.BlockSpec(memory_space=pl.ANY),
        scratch_shapes=scratch,
        compiler_params=pltpu.CompilerParams(
            collective_id=0, has_side_effects=True, vmem_limit_bytes=40 * 1024 * 1024
        ),
    )(*[pltpu.with_memory_space_constraint(a, pltpu.HBM) for a in arrays])
    return halves_out


def solution(mesh):
    placed = (
        P("apa", "chan", None),
        P("apa", None),
        P("apa", None),
        P(None, "chan", None),
        P(),
        P(),
        P("apa", "chan", None),
    )
    return jax.shard_map(body, mesh=mesh, in_specs=placed, out_specs=P("apa", "chan", None), check_vma=False)
```
